32 devices in a mesh: dp: 16 (over z, y, core), fsdp: 2 (over x).
Axes of the slice: x: 2, y: 2, z: 4, core: 2. Of those that a mesh axis runs over, the one named last changes fastest.
Arguments:
- block_input: bfloat16 [32768, 768], P(('dp', 'fsdp')), may hold values from -6 to 6
- seq_long: int32 [16], P('dp'), may hold values 0 or 1
- ln1_gain: bfloat16 [768], P(('dp', 'fsdp')), may hold values from 0.099609375 to 1.8984375
- ln1_bias: bfloat16 [768], P(('dp', 'fsdp')), may hold values from -1.796875 to 1.796875
- w_qkv: bfloat16 [768, 2304], P(('dp', 'fsdp')), may hold values from -0.21875 to 0.21875
- b_qkv: bfloat16 [2304], P(('dp', 'fsdp')), may hold values from -1.796875 to 1.796875
- w_out: bfloat16 [768, 768], P(('dp', 'fsdp')), may hold values from -6 to 6
- b_out: bfloat16 [768], P(('dp', 'fsdp')), may hold values from -1.796875 to 1.796875
- ln2_gain: bfloat16 [768], P(('dp', 'fsdp')), may hold values from 0.099609375 to 1.8984375
- ln2_bias: bfloat16 [768], P(('dp', 'fsdp')), may hold values from -1.796875 to 1.796875
- w_fc: bfloat16 [768, 3072], P(('dp', 'fsdp')), may hold values from -0.21875 to 0.21875
- b_fc: bfloat16 [3072], P(('dp', 'fsdp')), may hold values from -1.796875 to 1.796875
- w_proj: bfloat16 [3072, 768], P(('dp', 'fsdp')), may hold values from -0.109375 to 0.109375
- b_proj: bfloat16 [768], P(('dp', 'fsdp')), may hold values from -1.796875 to 1.796875
- out_grad: bfloat16 [32768, 768], P(('dp', 'fsdp')), may hold values from -6 to 6
Outputs:
- block_output: bfloat16 [32768, 768], P(('dp', 'fsdp'))
- input_grad: float32 [32768, 768], P(('dp', 'fsdp'))
- grad_ln1_gain: float32 [768], P(('dp', 'fsdp'))
- grad_ln1_bias: float32 [768], P(('dp', 'fsdp'))
- grad_w_qkv: float32 [768, 2304], P(('dp', 'fsdp'))
- grad_b_qkv: float32 [2304], P(('dp', 'fsdp'))
- grad_w_out: float32 [768, 768], P(('dp', 'fsdp'))
- grad_b_out: float32 [768], P(('dp', 'fsdp'))
- grad_ln2_gain: float32 [768], P(('dp', 'fsdp'))
- grad_ln2_bias: float32 [768], P(('dp', 'fsdp'))
- grad_w_fc: float32 [768, 3072], P(('dp', 'fsdp'))
- grad_b_fc: float32 [3072], P(('dp', 'fsdp'))
- grad_w_proj: float32 [3072, 768], P(('dp', 'fsdp'))
- grad_b_proj: float32 [768], P(('dp', 'fsdp'))
The draws below stay inside these ranges and needn't reach their ends.
Inputs may be any that keep to these rules, and one draw needn't show every extreme that they name: `seq_long`: 0 or 1 for each group of 2048 tokens.
All inputs are finite; a program needn't handle non-finite values.
Results may differ from the reference program's by a relative error of at most 0.0098.
Values may be sent and summed in bfloat16 or wider, within the bound.
No kernel may reach another device: no remote copies, remote signals or barrier semaphores. Data moves between devices by JAX's collectives and lax.ppermute only.
A program may use at most 256 MiB of HBM per device.

```python
import math
import jax
import jax.numpy as jnp
from jax import lax

D = 768
HEADS = 12
HD = 64
FF = 3072
SEQ = 1024
GROUP = 2048
TOKENS = 32768
N_DP = 16


def with_ends(array, stream_key, smallest, high):
    shape = array.shape
    spot = [jax.random.randint(jax.random.fold_in(stream_key, axis), (), 0, shape[axis]) for axis in range(len(shape))]
    array = array.at[tuple(spot)].set(smallest)
    longest = shape.index(max(shape))
    spot[longest] = (spot[longest] + 1) % shape[longest]
    return array.at[tuple(spot)].set(high)


def levels(own_key, dims, shards, least, top_value):
    loudness, own = 1.0, jax.random.fold_in(own_key, 6)
    for dim, parts in shards:
        draws = jnp.exp(jax.random.uniform(jax.random.fold_in(own, dim), (parts,), jnp.float32, least / len(shards), top_value / len(shards)))
        loudness = loudness * jnp.repeat(draws, dims[dim] // parts).reshape([-1 if axis == dim else 1 for axis in range(len(dims))])
    return loudness


def gaussian(own_key, shape, deviation, bound, cuts=(), kind=jnp.bfloat16):
    drawn = jax.random.normal(own_key, shape, jnp.float32) * deviation
    if len(cuts) > 0:
        drawn = levels(own_key, shape, cuts, -0.22, 0.18) * drawn
    return jnp.clip(drawn, min=-bound, max=bound).astype(kind)


def setup_inputs(seed: int = 0) -> dict:
    key_of = jax.random.split(jax.random.key(seed), 16)
    return {
        "block_input": gaussian(key_of[0], (TOKENS, D), 1.0, 6.0, ((0, 32),)),
        "seq_long": with_ends((jax.random.randint(key_of[1], (N_DP,), 0, 2) < 1).astype(jnp.int32), jax.random.fold_in(key_of[1], 1), 0, 1),
        "ln1_gain": jnp.clip(1.0 + 0.18 * jax.random.normal(key_of[2], (D,), jnp.float32), 0.099609375, 1.8984375).astype(jnp.bfloat16),
        "ln1_bias": gaussian(key_of[3], (D,), 0.3, 1.796875, ((0, 32),)),
        "w_qkv": gaussian(key_of[4], (D, 3 * D), D ** -0.5, 0.21875, ((0, 32),)),
        "b_qkv": gaussian(key_of[5], (3 * D,), 0.3, 1.796875, ((0, 32),)),
        "w_out": gaussian(key_of[6], (D, D), (max(1, 2 * D // SEQ)) ** -0.5, 6.0, ((0, 32),)),
        "b_out": gaussian(key_of[7], (D,), 0.3, 1.796875, ((0, 32),)),
        "ln2_gain": jnp.clip(1.0 + 0.18 * jax.random.normal(key_of[8], (D,), jnp.float32), 0.099609375, 1.8984375).astype(jnp.bfloat16),
        "ln2_bias": gaussian(key_of[9], (D,), 0.3, 1.796875, ((0, 32),)),
        "w_fc": gaussian(key_of[10], (D, FF), D ** -0.5, 0.21875, ((0, 32),)),
        "b_fc": gaussian(key_of[11], (FF,), 0.3, 1.796875, ((0, 32),)),
        "w_proj": gaussian(key_of[12], (FF, D), FF ** -0.5, 0.109375, ((0, 32),)),
        "b_proj": gaussian(key_of[13], (D,), 0.3, 1.796875, ((0, 32),)),
        "out_grad": gaussian(key_of[14], (TOKENS, D), 1.0, 6.0, ((0, 32),)),
    }


@jax.custom_vjp
def low(v):
    return lax.optimization_barrier(v.astype(jnp.bfloat16)).astype(jnp.float32)

@jax.custom_vjp
def low_back(v):
    return v

def low_keep(v):
    return (low(v), None)

def low_pass(kept, grad):
    return (grad,)

def back_keep(v):
    return (v, None)

def back_low(kept, grad):
    return (low(grad),)
low.defvjp(low_keep, low_pass)
low_back.defvjp(back_keep, back_low)
EPS = 1e-05
FAR = -1e+30
HIGH = lax.Precision.HIGHEST

def layer_norm(rows_in, gain_vec, bias_vec):
    row_mean = lax.optimization_barrier(jnp.mean(rows_in, axis=-1, keepdims=True))
    centred = rows_in - row_mean
    variance = lax.optimization_barrier(jnp.mean(centred * centred, axis=-1, keepdims=True))
    return centred * lax.rsqrt(variance + EPS) * gain_vec + bias_vec

def product(left, right):
    return jnp.dot(left, right, precision=HIGH, preferred_element_type=jnp.float32)

def group_forward(group_input, long_flag, param_set):
    ln1_gain, ln1_bias, w_qkv, b_qkv, w_out, b_out, ln2_gain, ln2_bias, w_fc, b_fc, w_proj, b_proj = param_set
    row_count = group_input.shape[0]
    seq_length = jnp.where(long_flag == 1, 2 * SEQ, SEQ).astype(jnp.int32)
    normed_one = low(layer_norm(group_input, ln1_gain, ln1_bias))
    projected = low(low_back(product(normed_one, w_qkv) + b_qkv))
    queries = projected[:, :D].reshape(row_count, HEADS, HD)
    key_rows = projected[:, D:2 * D].reshape(row_count, HEADS, HD)
    value_rows = projected[:, 2 * D:].reshape(row_count, HEADS, HD)
    positions = jnp.arange(row_count, dtype=jnp.int32)
    query_block = math.gcd(row_count, 512)

    def attend_block(start_row):
        query_part = lax.dynamic_slice_in_dim(queries, start_row, query_block, 0)
        query_pos = start_row + jnp.arange(query_block, dtype=jnp.int32)
        scores = low_back(jnp.einsum('qhd,khd->hqk', query_part, key_rows, precision=HIGH) * HD ** (-0.5))
        allowed = (query_pos[:, None] // seq_length == positions[None, :] // seq_length) & (positions[None, :] <= query_pos[:, None])
        magnitude = jnp.sqrt(scores * scores + 1.0)
        masked = jnp.where(allowed[None], magnitude, FAR)
        row_top = lax.optimization_barrier(jnp.max(masked, axis=-1, keepdims=True))
        row_total = lax.optimization_barrier(jnp.sum(jnp.where(allowed[None], jnp.exp(masked - row_top), 0.0), axis=-1, keepdims=True))
        log_total = row_top + jnp.log(row_total)
        weights = low(jnp.where(allowed[None], jnp.tanh(scores) * jnp.exp(masked - log_total), 0.0))
        return jnp.einsum('hqk,khd->qhd', weights, value_rows, precision=HIGH)
    starts = jnp.arange(row_count // query_block, dtype=jnp.int32) * query_block
    attn_heads = lax.map(jax.checkpoint(attend_block), starts).reshape(row_count, D)
    mixed = low(low_back(attn_heads))
    attention = low_back(product(mixed, w_out) + b_out)
    middle = group_input + attention
    normed_two = low(layer_norm(middle, ln2_gain, ln2_bias))
    hidden_pre = low_back(product(normed_two, w_fc) + b_fc)
    hidden_act = low(jax.nn.gelu(hidden_pre))
    branch = low_back(product(hidden_act, w_proj) + b_proj)
    return middle + branch

def reference(block_input, seq_long, ln1_gain, ln1_bias, w_qkv, b_qkv, w_out, b_out, ln2_gain, ln2_bias, w_fc, b_fc, w_proj, b_proj, out_grad):
    param_set = tuple((weight_item.astype(jnp.float32) for weight_item in (ln1_gain, ln1_bias, w_qkv, b_qkv, w_out, b_out, ln2_gain, ln2_bias, w_fc, b_fc, w_proj, b_proj)))
    group_inputs = block_input.astype(jnp.float32).reshape(N_DP, GROUP, D)
    group_grads = out_grad.astype(jnp.float32).reshape(N_DP, GROUP, D)
    zero_set = tuple((jnp.zeros_like(weight_item) for weight_item in param_set))

    def scan_step(totals, group_item):
        group_input, long_flag, group_grad = group_item

        def apply_group(input_rows, weights_in):
            return group_forward(input_rows, long_flag, weights_in)
        group_out, pullback = jax.vjp(apply_group, group_input, param_set)
        input_part, param_part = pullback(group_grad)
        totals = tuple((total_now + part_now for total_now, part_now in zip(totals, param_part)))
        return (totals, (group_out, input_part))
    totals, (outputs, input_parts) = lax.scan(scan_step, zero_set, (group_inputs, seq_long, group_grads))
    return (outputs.reshape(TOKENS, D).astype(jnp.bfloat16), input_parts.reshape(TOKENS, D), totals[0], totals[1], totals[2], totals[3], totals[4], totals[5], totals[6], totals[7], totals[8], totals[9], totals[10], totals[11])
```

```python
import functools
import math

import jax
import jax.numpy as jnp
from jax import lax
from jax.experimental import pallas as pl
from jax.experimental.pallas import tpu as pltpu
from jax.sharding import PartitionSpec as P

f32 = jnp.float32
bf = jnp.bfloat16


D = 768
HEADS = 12
HD = 64
SEQ = 1024


EPS = 1e-05
FAR = -1e30


def layer_norm(rows_in, gain_vec, bias_vec):
    row_mean = jnp.mean(rows_in, axis=-1, keepdims=True)
    centred = rows_in - row_mean
    variance = jnp.mean(centred * centred, axis=-1, keepdims=True)
    return centred * lax.rsqrt(variance + EPS) * gain_vec + bias_vec


def product(left, right):
    return jnp.dot(left, right, preferred_element_type=jnp.float32)


def product_tn(left, right):
    return lax.dot_general(
        left, right, (((0,), (0,)), ((), ())), preferred_element_type=jnp.float32
    )


def product_nt(left, right):
    return lax.dot_general(
        left, right, (((1,), (1,)), ((), ())), preferred_element_type=jnp.float32
    )


def gather_first(kv_rows):
    return lax.all_gather(kv_rows, "fsdp", axis=0, tiled=True)


def gather_second(kv_rows):
    return lax.all_gather(kv_rows, "fsdp", axis=0, tiled=True)


def block_layout(kv_all):
    group_rows = kv_all.shape[0]
    key_block = math.gcd(group_rows, 512)
    block_count = group_rows // key_block
    kv_blocks = kv_all.reshape(block_count, key_block, 2, HEADS, HD)
    return (key_block, kv_blocks, jnp.arange(block_count, dtype=jnp.int32))


def block_allowed(query_pos, key_start, key_block, seq_length):
    key_pos = key_start + jnp.arange(key_block, dtype=jnp.int32)
    return (query_pos[:, None] // seq_length == key_pos[None, :] // seq_length) & (
        key_pos[None, :] <= query_pos[:, None]
    )


def block_useful(key_start, key_block, query_pos, first_valid):
    return (key_start <= query_pos[-1]) & (key_start + key_block - 1 >= first_valid)


def score_parts(queries, key_part):
    scores = jnp.einsum(
        "qhd,khd->hqk", queries, key_part, preferred_element_type=jnp.float32
    ) * HD ** (-0.5)
    return (scores, jnp.sqrt(scores * scores + 1.0))


def attend(queries, kv_all, query_pos, seq_length, first_valid):
    key_block, kv_blocks, block_ids = block_layout(kv_all)
    row_total = queries.shape[0]

    def stats_step(state_now, block_item):
        block_id, kv_part = block_item
        key_start = block_id * key_block

        def stats_compute(state_in):
            row_top, row_sum = state_in
            allowed = block_allowed(query_pos, key_start, key_block, seq_length)[None]
            scores, magnitude = score_parts(queries, kv_part[:, 0])
            masked = jnp.where(allowed, magnitude, FAR)
            new_top = jnp.maximum(row_top, jnp.max(masked, axis=-1))
            fresh = jnp.sum(jnp.where(allowed, jnp.exp(masked - new_top[:, :, None]), 0.0), axis=-1)
            return (new_top, row_sum * jnp.exp(row_top - new_top) + fresh)

        useful = block_useful(key_start, key_block, query_pos, first_valid)
        return (lax.cond(useful, stats_compute, lambda kept_state: kept_state, state_now), None)

    start_state = (
        jnp.full((HEADS, row_total), FAR, jnp.float32),
        jnp.zeros((HEADS, row_total), jnp.float32),
    )
    (row_top, row_sum), unused = lax.scan(stats_step, start_state, (block_ids, kv_blocks))
    log_total = row_top + jnp.log(row_sum)

    def value_step(accum_now, block_item):
        block_id, kv_part = block_item
        key_start = block_id * key_block

        def value_compute(accum_in):
            allowed = block_allowed(query_pos, key_start, key_block, seq_length)[None]
            scores, magnitude = score_parts(queries, kv_part[:, 0])
            weights = jnp.where(
                allowed, jnp.tanh(scores) * jnp.exp(magnitude - log_total[:, :, None]), 0.0
            ).astype(jnp.bfloat16)
            return accum_in + jnp.einsum(
                "hqk,khd->qhd", weights, kv_part[:, 1], preferred_element_type=jnp.float32
            )

        useful = block_useful(key_start, key_block, query_pos, first_valid)
        return (lax.cond(useful, value_compute, lambda kept_accum: kept_accum, accum_now), None)

    start_accum = jnp.zeros((row_total, HEADS, HD), jnp.float32)
    attn_heads, unused = lax.scan(value_step, start_accum, (block_ids, kv_blocks))
    return (attn_heads, log_total)


def attend_back(
    queries, kv_all, query_pos, seq_length, first_valid, log_total, attn_heads, grad_heads
):
    key_block, kv_blocks, block_ids = block_layout(kv_all)
    row_total = queries.shape[0]
    inner = jnp.transpose(jnp.sum(grad_heads.astype(jnp.float32) * attn_heads, axis=-1))

    def grad_step(dq_now, block_item):
        block_id, kv_part = block_item
        key_start = block_id * key_block

        def grad_compute(dq_in):
            allowed = block_allowed(query_pos, key_start, key_block, seq_length)[None]
            scores, magnitude = score_parts(queries, kv_part[:, 0])
            expo = jnp.where(allowed, jnp.exp(magnitude - log_total[:, :, None]), 0.0)
            tangent = jnp.tanh(scores)
            weights = (tangent * expo).astype(jnp.bfloat16)
            grad_v = jnp.einsum(
                "hqk,qhd->khd", weights, grad_heads, preferred_element_type=jnp.float32
            )
            grad_weight = jnp.einsum(
                "qhd,khd->hqk", grad_heads, kv_part[:, 1], preferred_element_type=jnp.float32
            )
            slope = scores / magnitude
            grad_scores = (
                expo
                * (
                    grad_weight * (1.0 - tangent * tangent + tangent * slope)
                    - slope * inner[:, :, None]
                )
            ).astype(jnp.bfloat16)
            dq_out = dq_in + jnp.einsum(
                "hqk,khd->qhd", grad_scores, kv_part[:, 0], preferred_element_type=jnp.float32
            ) * HD ** (-0.5)
            grad_k = jnp.einsum(
                "hqk,qhd->khd", grad_scores, queries, preferred_element_type=jnp.float32
            ) * HD ** (-0.5)
            return (
                dq_out,
                jnp.concatenate(
                    [grad_k.reshape(key_block, D), grad_v.reshape(key_block, D)], axis=1
                ),
            )

        def skip_block(dq_in):
            return (dq_in, jnp.zeros((key_block, 2 * D), jnp.float32))

        useful = block_useful(key_start, key_block, query_pos, first_valid)
        return lax.cond(useful, grad_compute, skip_block, dq_now)

    start_dq = jnp.zeros((row_total, HEADS, HD), jnp.float32)
    grad_q, kv_grads = lax.scan(grad_step, start_dq, (block_ids, kv_blocks))
    return (grad_q, kv_grads.reshape(kv_all.shape[0], 2 * D))


def forward(block_input, weight_set, long_flag, fsdp_index, gather_keys):
    (
        ln1_gain,
        ln1_bias,
        w_qkv,
        b_qkv,
        w_out,
        b_out,
        ln2_gain,
        ln2_bias,
        w_fc,
        b_fc,
        w_proj,
        b_proj,
    ) = weight_set
    row_total = block_input.shape[0]
    wide_input = block_input.astype(jnp.float32)
    normed_one = layer_norm(
        wide_input, ln1_gain.astype(jnp.float32), ln1_bias.astype(jnp.float32)
    ).astype(jnp.bfloat16)
    projected = (product(normed_one, w_qkv) + b_qkv.astype(jnp.float32)).astype(jnp.bfloat16)
    queries = projected[:, :D].reshape(row_total, HEADS, HD)
    kv_all = gather_keys(projected[:, D:])
    seq_length = jnp.where(long_flag == 1, 2 * SEQ, SEQ).astype(jnp.int32)
    query_pos = fsdp_index * row_total + jnp.arange(row_total, dtype=jnp.int32)
    first_valid = query_pos[0] // seq_length * seq_length
    attn_heads, log_total = attend(queries, kv_all, query_pos, seq_length, first_valid)
    mixed = attn_heads.reshape(row_total, D).astype(jnp.bfloat16)
    middle = wide_input + product(mixed, w_out) + b_out.astype(jnp.float32)
    normed_two = layer_norm(
        middle, ln2_gain.astype(jnp.float32), ln2_bias.astype(jnp.float32)
    ).astype(jnp.bfloat16)
    hidden_pre = product(normed_two, w_fc) + b_fc.astype(jnp.float32)
    hidden_act = jax.nn.gelu(hidden_pre).astype(jnp.bfloat16)
    block_out = middle + product(hidden_act, w_proj) + b_proj.astype(jnp.float32)
    return (
        block_out,
        normed_one,
        queries,
        kv_all,
        query_pos,
        seq_length,
        first_valid,
        attn_heads,
        log_total,
        mixed,
        middle,
        normed_two,
        hidden_pre,
        hidden_act,
    )


def backward(saved, weight_set, block_input, out_grad):
    (
        block_out,
        normed_one,
        queries,
        kv_all,
        query_pos,
        seq_length,
        first_valid,
        attn_heads,
        log_total,
        mixed,
        middle,
        normed_two,
        hidden_pre,
        hidden_act,
    ) = saved
    (
        ln1_gain,
        ln1_bias,
        w_qkv,
        b_qkv,
        w_out,
        b_out,
        ln2_gain,
        ln2_bias,
        w_fc,
        b_fc,
        w_proj,
        b_proj,
    ) = weight_set
    row_total = block_input.shape[0]
    grad_out = out_grad.astype(jnp.float32)
    grad_w_proj = product_tn(hidden_act, out_grad)
    grad_b_proj = jnp.sum(grad_out, axis=0)
    grad_act = product_nt(out_grad, w_proj)
    unused, gelu_pull = jax.vjp(jax.nn.gelu, hidden_pre)
    grad_pre = gelu_pull(grad_act)[0].astype(jnp.bfloat16)
    grad_w_fc = product_tn(normed_two, grad_pre)
    grad_b_fc = jnp.sum(grad_pre.astype(jnp.float32), axis=0)
    unused, norm_pull_two = jax.vjp(
        layer_norm, middle, ln2_gain.astype(jnp.float32), ln2_bias.astype(jnp.float32)
    )
    grad_mid_norm, grad_ln2_gain, grad_ln2_bias = norm_pull_two(product_nt(grad_pre, w_fc))
    grad_middle = grad_out + grad_mid_norm
    grad_mid_low = grad_middle.astype(jnp.bfloat16)
    grad_w_out = product_tn(mixed, grad_mid_low)
    grad_b_out = jnp.sum(grad_mid_low.astype(jnp.float32), axis=0)
    grad_heads = product_nt(grad_mid_low, w_out).astype(jnp.bfloat16).reshape(row_total, HEADS, HD)
    grad_q, kv_grads = attend_back(
        queries, kv_all, query_pos, seq_length, first_valid, log_total, attn_heads, grad_heads
    )
    kv_mine = lax.psum_scatter(
        kv_grads.astype(jnp.bfloat16), "fsdp", scatter_dimension=0, tiled=True
    ).astype(jnp.float32)
    grad_proj = jnp.concatenate([grad_q.reshape(row_total, D), kv_mine], axis=1).astype(
        jnp.bfloat16
    )
    grad_w_qkv = product_tn(normed_one, grad_proj)
    grad_b_qkv = jnp.sum(grad_proj.astype(jnp.float32), axis=0)
    unused, norm_pull_one = jax.vjp(
        layer_norm,
        block_input.astype(jnp.float32),
        ln1_gain.astype(jnp.float32),
        ln1_bias.astype(jnp.float32),
    )
    grad_in_norm, grad_ln1_gain, grad_ln1_bias = norm_pull_one(product_nt(grad_proj, w_qkv))
    input_grad = grad_middle + grad_in_norm
    grad_set = (
        grad_ln1_gain,
        grad_ln1_bias,
        grad_w_qkv,
        grad_b_qkv,
        grad_w_out,
        grad_b_out,
        grad_ln2_gain,
        grad_ln2_bias,
        grad_w_fc,
        grad_b_fc,
        grad_w_proj,
        grad_b_proj,
    )
    return (input_grad, grad_set)


def on_device_generic(
    block_input,
    seq_long,
    ln1_gain,
    ln1_bias,
    w_qkv,
    b_qkv,
    w_out,
    b_out,
    ln2_gain,
    ln2_bias,
    w_fc,
    b_fc,
    w_proj,
    b_proj,
    out_grad,
):
    long_flag = seq_long[0]
    fsdp_index = lax.axis_index("fsdp")
    weight_set = (
        lax.all_gather(ln1_gain, ("dp", "fsdp"), axis=0, tiled=True),
        lax.all_gather(ln1_bias, ("dp", "fsdp"), axis=0, tiled=True),
        lax.all_gather(w_qkv, ("dp", "fsdp"), axis=0, tiled=True),
        lax.all_gather(b_qkv, ("dp", "fsdp"), axis=0, tiled=True),
        lax.all_gather(w_out, ("dp", "fsdp"), axis=0, tiled=True),
        lax.all_gather(b_out, ("dp", "fsdp"), axis=0, tiled=True),
        lax.all_gather(ln2_gain, ("dp", "fsdp"), axis=0, tiled=True),
        lax.all_gather(ln2_bias, ("dp", "fsdp"), axis=0, tiled=True),
        lax.all_gather(w_fc, ("dp", "fsdp"), axis=0, tiled=True),
        lax.all_gather(b_fc, ("dp", "fsdp"), axis=0, tiled=True),
        lax.all_gather(w_proj, ("dp", "fsdp"), axis=0, tiled=True),
        lax.all_gather(b_proj, ("dp", "fsdp"), axis=0, tiled=True),
    )
    saved = forward(block_input, weight_set, long_flag, fsdp_index, gather_first)
    block_output = saved[0].astype(jnp.bfloat16)
    weight_set = (
        lax.all_gather(ln1_gain, ("dp", "fsdp"), axis=0, tiled=True),
        lax.all_gather(ln1_bias, ("dp", "fsdp"), axis=0, tiled=True),
        lax.all_gather(w_qkv, ("dp", "fsdp"), axis=0, tiled=True),
        lax.all_gather(b_qkv, ("dp", "fsdp"), axis=0, tiled=True),
        lax.all_gather(w_out, ("dp", "fsdp"), axis=0, tiled=True),
        lax.all_gather(b_out, ("dp", "fsdp"), axis=0, tiled=True),
        lax.all_gather(ln2_gain, ("dp", "fsdp"), axis=0, tiled=True),
        lax.all_gather(ln2_bias, ("dp", "fsdp"), axis=0, tiled=True),
        lax.all_gather(w_fc, ("dp", "fsdp"), axis=0, tiled=True),
        lax.all_gather(b_fc, ("dp", "fsdp"), axis=0, tiled=True),
        lax.all_gather(w_proj, ("dp", "fsdp"), axis=0, tiled=True),
        lax.all_gather(b_proj, ("dp", "fsdp"), axis=0, tiled=True),
    )
    saved = forward(block_input, weight_set, long_flag, fsdp_index, gather_second)
    input_grad, grad_set = backward(saved, weight_set, block_input, out_grad)
    grad_shards = (
        lax.psum_scatter(grad_set[0], ("dp", "fsdp"), scatter_dimension=0, tiled=True),
        lax.psum_scatter(grad_set[1], ("dp", "fsdp"), scatter_dimension=0, tiled=True),
        lax.psum_scatter(grad_set[2], ("dp", "fsdp"), scatter_dimension=0, tiled=True),
        lax.psum_scatter(grad_set[3], ("dp", "fsdp"), scatter_dimension=0, tiled=True),
        lax.psum_scatter(grad_set[4], ("dp", "fsdp"), scatter_dimension=0, tiled=True),
        lax.psum_scatter(grad_set[5], ("dp", "fsdp"), scatter_dimension=0, tiled=True),
        lax.psum_scatter(grad_set[6], ("dp", "fsdp"), scatter_dimension=0, tiled=True),
        lax.psum_scatter(grad_set[7], ("dp", "fsdp"), scatter_dimension=0, tiled=True),
        lax.psum_scatter(grad_set[8], ("dp", "fsdp"), scatter_dimension=0, tiled=True),
        lax.psum_scatter(grad_set[9], ("dp", "fsdp"), scatter_dimension=0, tiled=True),
        lax.psum_scatter(grad_set[10], ("dp", "fsdp"), scatter_dimension=0, tiled=True),
        lax.psum_scatter(grad_set[11], ("dp", "fsdp"), scatter_dimension=0, tiled=True),
    )
    return (block_output, input_grad) + tuple(grad_shards)


def nt(a, b): return lax.dot_general(a,b,(((1,),(1,)),((),())),preferred_element_type=f32)
def nn(a,b): return jnp.dot(a,b,preferred_element_type=f32)

def head_lanes(rows):
    return lax.broadcasted_iota(jnp.int32,(rows,128),1) < HD

def split_heads(pair):
    left = head_lanes(pair.shape[0])
    zero = jnp.zeros_like(pair)
    return (jnp.where(left,pair,zero), jnp.where(left,zero,pair))

def fwd_kernel(block, flag_ref, q_ref, k_ref, v_ref, o_ref, lse_ref, vt_ref):
    i = pl.program_id(0)
    pairs = q_ref.shape[1]//128
    @pl.when(i==0)
    def _():
        for p in range(pairs):
            vt_ref[p*128:(p+1)*128,:] = v_ref[:,p*128:(p+1)*128].astype(f32).T.astype(bf)
    per_seq = jnp.where(flag_ref[0]==1, 2*SEQ, SEQ)//block
    first = i//per_seq*per_seq
    qm=[]
    for p in range(pairs):
        qm.extend(split_heads(q_ref[:,p*128:(p+1)*128]))
    nh=2*pairs
    diag = lax.broadcasted_iota(jnp.int32,(block,block),0) <= lax.broadcasted_iota(jnp.int32,(block,block),1)
    def step(j, state, masked):
        start = pl.multiple_of(j*block, block)
        out=[]
        for h in range(nh):
            p=h//2
            s = nt(k_ref[pl.ds(start,block),p*128:(p+1)*128], qm[h])
            x = s*s+1.0
            mag = x*lax.rsqrt(x)
            if masked: mag = jnp.where(diag,mag,-1e30)
            top = jnp.max(mag,axis=0,keepdims=True)
            if state is not None:
                old_top, old_sum, old_acc = state[h]
                top = jnp.maximum(top, old_top)
            e = jnp.exp(mag-top)
            fresh = jnp.sum(e,axis=0,keepdims=True)
            w = (jnp.tanh(s)*e).astype(bf)
            part = nn(vt_ref[h*HD:(h+1)*HD,pl.ds(start,block)], w)
            if state is not None:
                alpha = jnp.exp(old_top-top)
                fresh = fresh + alpha*old_sum
                part = part + alpha*old_acc
            out.append((top,fresh,part))
        return tuple(out)
    state = step(i,None,True)
    state = lax.fori_loop(first,i,lambda j,st: step(j,st,False),state)
    for h in range(nh):
        top,total,acc = state[h]
        lse_ref[h:h+1,:] = top+jnp.log(total)
    for p in range(pairs):
        o2 = jnp.concatenate([state[2*p][2]/state[2*p][1], state[2*p+1][2]/state[2*p+1][1]],axis=0)
        o_ref[:,p*128:(p+1)*128] = o2.T.astype(bf)

def attend_fwd(flag, qkv, block):
    rows=qkv.shape[0]; width=qkv.shape[1]//3
    full=lambda c: pl.BlockSpec((rows,width),lambda i,f:(0,c))
    return pl.pallas_call(functools.partial(fwd_kernel,block),
        grid_spec=pltpu.PrefetchScalarGridSpec(num_scalar_prefetch=1,grid=(rows//block,),
            in_specs=[pl.BlockSpec((block,width),lambda i,f:(i,0)),full(1),full(2)],
            out_specs=[pl.BlockSpec((block,width),lambda i,f:(i,0)),pl.BlockSpec((8,block),lambda i,f:(0,i))],
            scratch_shapes=[pltpu.VMEM((width,rows),bf)]),
        out_shape=[jax.ShapeDtypeStruct((rows,width),bf),jax.ShapeDtypeStruct((8,rows),f32)],
        name="attend_fwd")(flag,qkv,qkv,qkv)

def bwd_kernel(block, flag_ref, q_ref, k_ref, v_ref, o_ref, do_ref, lse_ref, g_ref, dqt_ref, inner_ref):
    j = pl.program_id(0); last = pl.num_programs(0)-1
    width=k_ref.shape[1]; pairs=width//128; nh=2*pairs; rows=q_ref.shape[0]
    @pl.when(j==0)
    def _():
        dqt_ref[...]=jnp.zeros_like(dqt_ref)
        acc=jnp.zeros((8,rows),f32)
        for p in range(pairs):
            prod=o_ref[:,p*128:(p+1)*128].astype(f32)*do_ref[:,p*128:(p+1)*128].astype(f32)
            hrow=lax.broadcasted_iota(jnp.int32,(8,128),0); lane=lax.broadcasted_iota(jnp.int32,(8,128),1)
            sel=(hrow==2*p+lane//HD).astype(f32)
            acc=acc+lax.dot_general(sel,prod,(((1,),(1,)),((),())),precision=lax.Precision.HIGHEST,preferred_element_type=f32)
        inner_ref[...]=acc
    per_seq = jnp.where(flag_ref[0]==1, 2*SEQ, SEQ)//block
    stop = (j//per_seq+1)*per_seq
    km=[];vm=[];kt=[]
    for p in range(pairs):
        kp=k_ref[:,p*128:(p+1)*128]
        km.extend(split_heads(kp)); vm.extend(split_heads(v_ref[:,p*128:(p+1)*128]))
        ktp=kp.astype(f32).T.astype(bf)
        kt.extend((ktp[:HD],ktp[HD:]))
    diag = lax.broadcasted_iota(jnp.int32,(block,block),0) <= lax.broadcasted_iota(jnp.int32,(block,block),1)
    def step(i, state, masked):
        start = pl.multiple_of(i*block, block)
        out=[]
        for p in range(pairs):
            cols=slice(p*128,(p+1)*128)
            qp=q_ref[pl.ds(start,block),cols]; dop=do_ref[pl.ds(start,block),cols]
            qh=split_heads(qp); doh=split_heads(dop)
            dk=dv=None
            for a in range(2):
                h=2*p+a
                s=nt(km[h],qp)
                x=s*s+1.0
                r=lax.rsqrt(x)
                e=jnp.exp(x*r-lse_ref[h:h+1,pl.ds(start,block)])
                if masked: e=jnp.where(diag,e,0.0)
                t=jnp.tanh(s)
                w=(t*e).astype(bf)
                gw=nt(vm[h],dop)
                slope=s*r
                ds=(e*(gw*(1.0-t*t+t*slope)-slope*inner_ref[h:h+1,pl.ds(start,block)])).astype(bf)
                pv=nn(w,doh[a]); pk=nn(ds,qh[a])
                dv = pv if dv is None else dv+pv
                dk = pk if dk is None else dk+pk
                dqt_ref[h*HD:(h+1)*HD,pl.ds(start,block)] += nn(kt[h],ds)
            if state is not None:
                dk=dk+state[p][0]; dv=dv+state[p][1]
            out.append((dk,dv))
        return tuple(out)
    state=step(j,None,True)
    state=lax.fori_loop(j+1,stop,lambda i,st: step(i,st,False),state)
    mine=pl.ds(pl.multiple_of(j*block,block),block)
    for p in range(pairs):
        g_ref[mine,width+p*128:width+(p+1)*128]=state[p][0].astype(bf)
        g_ref[mine,2*width+p*128:2*width+(p+1)*128]=state[p][1].astype(bf)
    @pl.when(j==last)
    def _():
        for p in range(pairs):
            g_ref[:,p*128:(p+1)*128]=(dqt_ref[p*128:(p+1)*128,:]*HD**-0.5).T.astype(bf)

def attend_bwd(flag, qkv, heads_out, grad_heads, lse, block):
    rows=qkv.shape[0]; width=qkv.shape[1]//3
    full=lambda c: pl.BlockSpec((rows,width),lambda j,f:(0,c))
    part=lambda c: pl.BlockSpec((block,width),lambda j,f:(j,c))
    return pl.pallas_call(functools.partial(bwd_kernel,block),
        grid_spec=pltpu.PrefetchScalarGridSpec(num_scalar_prefetch=1,grid=(rows//block,),
            in_specs=[full(0),part(1),part(2),full(0),full(0),pl.BlockSpec((8,rows),lambda j,f:(0,0))],
            out_specs=pl.BlockSpec((rows,3*width),lambda j,f:(0,0)),
            scratch_shapes=[pltpu.VMEM((width,rows),f32),pltpu.VMEM((8,rows),f32)]),
        out_shape=jax.ShapeDtypeStruct((rows,3*width),bf),
        name="attend_bwd")(flag,qkv,qkv,qkv,heads_out,grad_heads,lse)


AXES = ("dp", "fsdp")


def swap(value, bit, total):
    return lax.ppermute(value, AXES, [(i, i ^ bit) for i in range(total)])


def gather_dp(shard, dp_size, order):
    me = lax.axis_index("dp")
    bits = dp_size.bit_length() - 1
    held = shard.reshape((1,) * bits + shard.shape)
    for bit in order:
        other = swap(held, 2 << bit, 2 * dp_size)
        low = (me >> bit) & 1 == 0
        held = jnp.concatenate(
            [jnp.where(low, held, other), jnp.where(low, other, held)], axis=bits - 1 - bit
        )
    return held.reshape((dp_size * shard.shape[0],) + shard.shape[1:])


def scatter_dp(whole, dp_size, order):
    me = lax.axis_index("dp")
    bits = dp_size.bit_length() - 1
    rows = whole.shape[0] // dp_size
    held = whole.reshape((2,) * bits + (rows,) + whole.shape[1:])
    for bit in order:
        axis = bits - 1 - bit
        low = (me >> bit) & 1 == 0
        first = lax.slice_in_dim(held, 0, 1, axis=axis)
        second = lax.slice_in_dim(held, 1, 2, axis=axis)
        mine = jnp.where(low, first, second)
        sent = jnp.where(low, second, first).astype(bf)
        held = mine.astype(f32) + swap(sent, 2 << bit, 2 * dp_size).astype(f32)
    return held.reshape((rows,) + whole.shape[1:])


def sum_all(vector, total):
    bit = 1
    while bit < total:
        vector = vector + swap(vector, bit, total)
        bit *= 2
    return vector


def on_device_pair(
    dp_size,
    block_input,
    seq_long,
    ln1_gain,
    ln1_bias,
    w_qkv,
    b_qkv,
    w_out,
    b_out,
    ln2_gain,
    ln2_bias,
    w_fc,
    b_fc,
    w_proj,
    b_proj,
    out_grad,
):
    total = 2 * dp_size
    side = lax.axis_index("fsdp")
    flat = lax.axis_index("dp") * 2 + side
    on_left = side == 0
    row_total = block_input.shape[0]
    half = D // 2
    dp_bits = list(range(dp_size.bit_length() - 1))
    gather_order = dp_bits[1:2] + dp_bits[:1:-1] + dp_bits[:1]
    scatter_order = dp_bits[:1] + dp_bits[2:] + dp_bits[1:2]

    def ordered(mine, other, axis):
        return jnp.concatenate(
            [jnp.where(on_left, mine, other), jnp.where(on_left, other, mine)], axis=axis
        )

    def head_columns(rows_in, which):
        three = rows_in.reshape(rows_in.shape[0], 3, 2, half)
        return lax.dynamic_slice_in_dim(three, which, 1, axis=2).reshape(
            rows_in.shape[0], 3 * half
        )

    small = (ln1_gain, ln1_bias, b_qkv, b_out, ln2_gain, ln2_bias, b_fc, b_proj)
    placed = jnp.concatenate(
        [
            lax.dynamic_update_slice(
                jnp.zeros((item.shape[0] * total,), bf), item, (item.shape[0] * flat,)
            )
            for item in small
        ]
    )
    gathered = sum_all(placed, total).astype(f32)
    pieces = []
    start = 0
    for item in small:
        pieces.append(gathered[start : start + item.shape[0] * total])
        start += item.shape[0] * total
    ln1_gain, ln1_bias, b_qkv, b_out, ln2_gain, ln2_bias, b_fc, b_proj = pieces

    other_input = swap(block_input, 1, total)
    received = swap(head_columns(w_qkv, 1 - side), 1, total)
    w_mine = gather_dp(ordered(head_columns(w_qkv, side), received, 0), dp_size, gather_order)
    w_out = lax.all_gather(w_out, AXES, axis=0, tiled=True)
    w_fc = lax.all_gather(w_fc, AXES, axis=0, tiled=True)
    w_proj = lax.all_gather(w_proj, AXES, axis=0, tiled=True)

    wide_input = block_input.astype(f32)
    group_input = ordered(block_input, other_input, 0)
    normed_one = layer_norm(group_input.astype(f32), ln1_gain, ln1_bias).astype(bf)
    b_mine = head_columns(b_qkv.reshape(1, 3 * D), side)
    projected = (product(normed_one, w_mine) + b_mine).astype(bf)
    q_scale = jnp.where(jnp.arange(3 * half) < half, HD**-0.5, 1.0).astype(bf)
    projected = projected * q_scale
    heads_mine, log_total = attend_fwd(seq_long, projected, 512)

    def rows_of(whole, which):
        return lax.dynamic_slice_in_dim(whole, which * row_total, row_total, axis=0)

    heads_other = swap(rows_of(heads_mine, 1 - side), 1, total)
    mixed = ordered(rows_of(heads_mine, side), heads_other, 1)
    middle = wide_input + product(mixed, w_out) + b_out
    normed_two = layer_norm(middle, ln2_gain, ln2_bias).astype(bf)
    hidden_pre = product(normed_two, w_fc) + b_fc
    hidden_act = jax.nn.gelu(hidden_pre).astype(bf)
    block_output = (middle + product(hidden_act, w_proj) + b_proj).astype(bf)

    grad_out = out_grad.astype(f32)
    grad_w_proj = product_tn(hidden_act, out_grad).astype(bf)
    shard_w_proj = lax.psum_scatter(grad_w_proj, AXES, scatter_dimension=0, tiled=True)
    grad_b_proj = jnp.sum(grad_out, axis=0)
    grad_act = product_nt(out_grad, w_proj)
    unused, gelu_pull = jax.vjp(jax.nn.gelu, hidden_pre)
    grad_pre = gelu_pull(grad_act)[0].astype(bf)
    grad_w_fc = product_tn(normed_two, grad_pre).astype(bf)
    shard_w_fc = lax.psum_scatter(grad_w_fc, AXES, scatter_dimension=0, tiled=True)
    grad_b_fc = jnp.sum(grad_pre.astype(f32), axis=0)
    unused, norm_pull_two = jax.vjp(layer_norm, middle, ln2_gain, ln2_bias)
    grad_mid_norm, grad_ln2_gain, grad_ln2_bias = norm_pull_two(product_nt(grad_pre, w_fc))
    grad_middle = grad_out + grad_mid_norm
    grad_mid_low = grad_middle.astype(bf)
    grad_w_out = product_tn(mixed, grad_mid_low).astype(bf)
    shard_w_out = lax.psum_scatter(grad_w_out, AXES, scatter_dimension=0, tiled=True)
    grad_b_out = jnp.sum(grad_mid_low.astype(f32), axis=0)
    grad_heads = product_nt(grad_mid_low, w_out).astype(bf)

    def columns_of(whole, which):
        return lax.dynamic_slice_in_dim(whole, which * half, half, axis=1)

    grad_heads_other = swap(columns_of(grad_heads, 1 - side), 1, total)
    grad_heads_mine = ordered(columns_of(grad_heads, side), grad_heads_other, 0)
    grad_proj = attend_bwd(seq_long, projected, heads_mine, grad_heads_mine, log_total, 512)

    e_sent = product_nt(rows_of(grad_proj, 1 - side), w_mine).astype(bf)
    e_other = swap(e_sent, 1, total)
    grad_w_mine = product_tn(normed_one, grad_proj).astype(bf)
    shard_mine = scatter_dp(grad_w_mine, dp_size, scatter_order)
    shard_rows = shard_mine.reshape(2, shard_mine.shape[0] // 2, 3 * half)
    keep = lax.dynamic_index_in_dim(shard_rows, side, 0, keepdims=False)
    send = lax.dynamic_index_in_dim(shard_rows, 1 - side, 0, keepdims=False)
    taken = swap(send, 1, total)
    shard_w_qkv = ordered(
        keep.reshape(-1, 3, 1, half), taken.reshape(-1, 3, 1, half), 2
    ).reshape(-1, 3 * D)
    grad_b_mine = jnp.sum(grad_proj.astype(f32), axis=0).reshape(3, 1, half)
    zero_b = jnp.zeros_like(grad_b_mine)
    grad_b_qkv = ordered(grad_b_mine, zero_b, 1).reshape(3 * D)
    e_mine = product_nt(rows_of(grad_proj, side), w_mine) + e_other.astype(f32)
    unused, norm_pull_one = jax.vjp(layer_norm, wide_input, ln1_gain, ln1_bias)
    grad_in_norm, grad_ln1_gain, grad_ln1_bias = norm_pull_one(e_mine)
    input_grad = grad_middle + grad_in_norm

    early = (grad_b_out, grad_ln2_gain, grad_ln2_bias, grad_b_fc, grad_b_proj)
    late = (grad_ln1_gain, grad_ln1_bias, grad_b_qkv)

    def reduce_small(items):
        summed = sum_all(jnp.concatenate(items), total)
        begin = 0
        shards = []
        for item in items:
            size = item.shape[0] // total
            shards.append(lax.dynamic_slice(summed, (begin + size * flat,), (size,)))
            begin += item.shape[0]
        return shards

    shard_b_out, shard_ln2_gain, shard_ln2_bias, shard_b_fc, shard_b_proj = reduce_small(early)
    shard_ln1_gain, shard_ln1_bias, shard_b_qkv = reduce_small(late)
    return (
        block_output,
        input_grad,
        shard_ln1_gain,
        shard_ln1_bias,
        shard_w_qkv,
        shard_b_qkv,
        shard_w_out.astype(f32),
        shard_b_out,
        shard_ln2_gain,
        shard_ln2_bias,
        shard_w_fc.astype(f32),
        shard_b_fc,
        shard_w_proj.astype(f32),
        shard_b_proj,
    )


def solution(mesh):
    in_specs = (
        P(("dp", "fsdp"), None),
        P("dp"),
        P(("dp", "fsdp")),
        P(("dp", "fsdp")),
        P(("dp", "fsdp"), None),
        P(("dp", "fsdp")),
        P(("dp", "fsdp"), None),
        P(("dp", "fsdp")),
        P(("dp", "fsdp")),
        P(("dp", "fsdp")),
        P(("dp", "fsdp"), None),
        P(("dp", "fsdp")),
        P(("dp", "fsdp"), None),
        P(("dp", "fsdp")),
        P(("dp", "fsdp"), None),
    )
    out_specs = (
        P(("dp", "fsdp"), None),
        P(("dp", "fsdp"), None),
        P(("dp", "fsdp")),
        P(("dp", "fsdp")),
        P(("dp", "fsdp"), None),
        P(("dp", "fsdp")),
        P(("dp", "fsdp"), None),
        P(("dp", "fsdp")),
        P(("dp", "fsdp")),
        P(("dp", "fsdp")),
        P(("dp", "fsdp"), None),
        P(("dp", "fsdp")),
        P(("dp", "fsdp"), None),
        P(("dp", "fsdp")),
    )
    split_by_heads = (
        mesh.shape["fsdp"] == 2 and mesh.shape["dp"] & (mesh.shape["dp"] - 1) == 0
    )
    return jax.shard_map(
        functools.partial(on_device_pair, mesh.shape["dp"]) if split_by_heads else on_device_generic, mesh=mesh, in_specs=in_specs, out_specs=out_specs, check_vma=False
    )
```

```python
import functools
import math

import jax
import jax.numpy as jnp
from jax import lax
from jax.experimental import pallas as pl
from jax.experimental.pallas import tpu as pltpu
from jax.sharding import PartitionSpec as P

f32 = jnp.float32
bf = jnp.bfloat16


D = 768
HEADS = 12
HD = 64
FF = 3072
SEQ = 1024


EPS = 1e-05
FAR = -1e30


def layer_norm(rows_in, gain_vec, bias_vec):
    row_mean = jnp.mean(rows_in, axis=-1, keepdims=True)
    centred = rows_in - row_mean
    variance = jnp.mean(centred * centred, axis=-1, keepdims=True)
    return centred * lax.rsqrt(variance + EPS) * gain_vec + bias_vec


def product(left, right):
    return jnp.dot(left, right, preferred_element_type=jnp.float32)


def product_tn(left, right):
    return lax.dot_general(
        left, right, (((0,), (0,)), ((), ())), preferred_element_type=jnp.float32
    )


def product_nt(left, right):
    return lax.dot_general(
        left, right, (((1,), (1,)), ((), ())), preferred_element_type=jnp.float32
    )


def gather_first(kv_rows):
    return lax.all_gather(kv_rows, "fsdp", axis=0, tiled=True)


def gather_second(kv_rows):
    return lax.all_gather(kv_rows, "fsdp", axis=0, tiled=True)


def block_layout(kv_all):
    group_rows = kv_all.shape[0]
    key_block = math.gcd(group_rows, 512)
    block_count = group_rows // key_block
    kv_blocks = kv_all.reshape(block_count, key_block, 2, HEADS, HD)
    return (key_block, kv_blocks, jnp.arange(block_count, dtype=jnp.int32))


def block_allowed(query_pos, key_start, key_block, seq_length):
    key_pos = key_start + jnp.arange(key_block, dtype=jnp.int32)
    return (query_pos[:, None] // seq_length == key_pos[None, :] // seq_length) & (
        key_pos[None, :] <= query_pos[:, None]
    )


def block_useful(key_start, key_block, query_pos, first_valid):
    return (key_start <= query_pos[-1]) & (key_start + key_block - 1 >= first_valid)


def score_parts(queries, key_part):
    scores = jnp.einsum(
        "qhd,khd->hqk", queries, key_part, preferred_element_type=jnp.float32
    ) * HD ** (-0.5)
    return (scores, jnp.sqrt(scores * scores + 1.0))


def attend(queries, kv_all, query_pos, seq_length, first_valid):
    key_block, kv_blocks, block_ids = block_layout(kv_all)
    row_total = queries.shape[0]

    def stats_step(state_now, block_item):
        block_id, kv_part = block_item
        key_start = block_id * key_block

        def stats_compute(state_in):
            row_top, row_sum = state_in
            allowed = block_allowed(query_pos, key_start, key_block, seq_length)[None]
            scores, magnitude = score_parts(queries, kv_part[:, 0])
            masked = jnp.where(allowed, magnitude, FAR)
            new_top = jnp.maximum(row_top, jnp.max(masked, axis=-1))
            fresh = jnp.sum(jnp.where(allowed, jnp.exp(masked - new_top[:, :, None]), 0.0), axis=-1)
            return (new_top, row_sum * jnp.exp(row_top - new_top) + fresh)

        useful = block_useful(key_start, key_block, query_pos, first_valid)
        return (lax.cond(useful, stats_compute, lambda kept_state: kept_state, state_now), None)

    start_state = (
        jnp.full((HEADS, row_total), FAR, jnp.float32),
        jnp.zeros((HEADS, row_total), jnp.float32),
    )
    (row_top, row_sum), unused = lax.scan(stats_step, start_state, (block_ids, kv_blocks))
    log_total = row_top + jnp.log(row_sum)

    def value_step(accum_now, block_item):
        block_id, kv_part = block_item
        key_start = block_id * key_block

        def value_compute(accum_in):
            allowed = block_allowed(query_pos, key_start, key_block, seq_length)[None]
            scores, magnitude = score_parts(queries, kv_part[:, 0])
            weights = jnp.where(
                allowed, jnp.tanh(scores) * jnp.exp(magnitude - log_total[:, :, None]), 0.0
            ).astype(jnp.bfloat16)
            return accum_in + jnp.einsum(
                "hqk,khd->qhd", weights, kv_part[:, 1], preferred_element_type=jnp.float32
            )

        useful = block_useful(key_start, key_block, query_pos, first_valid)
        return (lax.cond(useful, value_compute, lambda kept_accum: kept_accum, accum_now), None)

    start_accum = jnp.zeros((row_total, HEADS, HD), jnp.float32)
    attn_heads, unused = lax.scan(value_step, start_accum, (block_ids, kv_blocks))
    return (attn_heads, log_total)


def attend_back(
    queries, kv_all, query_pos, seq_length, first_valid, log_total, attn_heads, grad_heads
):
    key_block, kv_blocks, block_ids = block_layout(kv_all)
    row_total = queries.shape[0]
    inner = jnp.transpose(jnp.sum(grad_heads.astype(jnp.float32) * attn_heads, axis=-1))

    def grad_step(dq_now, block_item):
        block_id, kv_part = block_item
        key_start = block_id * key_block

        def grad_compute(dq_in):
            allowed = block_allowed(query_pos, key_start, key_block, seq_length)[None]
            scores, magnitude = score_parts(queries, kv_part[:, 0])
            expo = jnp.where(allowed, jnp.exp(magnitude - log_total[:, :, None]), 0.0)
            tangent = jnp.tanh(scores)
            weights = (tangent * expo).astype(jnp.bfloat16)
            grad_v = jnp.einsum(
                "hqk,qhd->khd", weights, grad_heads, preferred_element_type=jnp.float32
            )
            grad_weight = jnp.einsum(
                "qhd,khd->hqk", grad_heads, kv_part[:, 1], preferred_element_type=jnp.float32
            )
            slope = scores / magnitude
            grad_scores = (
                expo
                * (
                    grad_weight * (1.0 - tangent * tangent + tangent * slope)
                    - slope * inner[:, :, None]
                )
            ).astype(jnp.bfloat16)
            dq_out = dq_in + jnp.einsum(
                "hqk,khd->qhd", grad_scores, kv_part[:, 0], preferred_element_type=jnp.float32
            ) * HD ** (-0.5)
            grad_k = jnp.einsum(
                "hqk,qhd->khd", grad_scores, queries, preferred_element_type=jnp.float32
            ) * HD ** (-0.5)
            return (
                dq_out,
                jnp.concatenate(
                    [grad_k.reshape(key_block, D), grad_v.reshape(key_block, D)], axis=1
                ),
            )

        def skip_block(dq_in):
            return (dq_in, jnp.zeros((key_block, 2 * D), jnp.float32))

        useful = block_useful(key_start, key_block, query_pos, first_valid)
        return lax.cond(useful, grad_compute, skip_block, dq_now)

    start_dq = jnp.zeros((row_total, HEADS, HD), jnp.float32)
    grad_q, kv_grads = lax.scan(grad_step, start_dq, (block_ids, kv_blocks))
    return (grad_q, kv_grads.reshape(kv_all.shape[0], 2 * D))


def forward(block_input, weight_set, long_flag, fsdp_index, gather_keys):
    (
        ln1_gain,
        ln1_bias,
        w_qkv,
        b_qkv,
        w_out,
        b_out,
        ln2_gain,
        ln2_bias,
        w_fc,
        b_fc,
        w_proj,
        b_proj,
    ) = weight_set
    row_total = block_input.shape[0]
    wide_input = block_input.astype(jnp.float32)
    normed_one = layer_norm(
        wide_input, ln1_gain.astype(jnp.float32), ln1_bias.astype(jnp.float32)
    ).astype(jnp.bfloat16)
    projected = (product(normed_one, w_qkv) + b_qkv.astype(jnp.float32)).astype(jnp.bfloat16)
    queries = projected[:, :D].reshape(row_total, HEADS, HD)
    kv_all = gather_keys(projected[:, D:])
    seq_length = jnp.where(long_flag == 1, 2 * SEQ, SEQ).astype(jnp.int32)
    query_pos = fsdp_index * row_total + jnp.arange(row_total, dtype=jnp.int32)
    first_valid = query_pos[0] // seq_length * seq_length
    attn_heads, log_total = attend(queries, kv_all, query_pos, seq_length, first_valid)
    mixed = attn_heads.reshape(row_total, D).astype(jnp.bfloat16)
    middle = wide_input + product(mixed, w_out) + b_out.astype(jnp.float32)
    normed_two = layer_norm(
        middle, ln2_gain.astype(jnp.float32), ln2_bias.astype(jnp.float32)
    ).astype(jnp.bfloat16)
    hidden_pre = product(normed_two, w_fc) + b_fc.astype(jnp.float32)
    hidden_act = jax.nn.gelu(hidden_pre).astype(jnp.bfloat16)
    block_out = middle + product(hidden_act, w_proj) + b_proj.astype(jnp.float32)
    return (
        block_out,
        normed_one,
        queries,
        kv_all,
        query_pos,
        seq_length,
        first_valid,
        attn_heads,
        log_total,
        mixed,
        middle,
        normed_two,
        hidden_pre,
        hidden_act,
    )


def backward(saved, weight_set, block_input, out_grad):
    (
        block_out,
        normed_one,
        queries,
        kv_all,
        query_pos,
        seq_length,
        first_valid,
        attn_heads,
        log_total,
        mixed,
        middle,
        normed_two,
        hidden_pre,
        hidden_act,
    ) = saved
    (
        ln1_gain,
        ln1_bias,
        w_qkv,
        b_qkv,
        w_out,
        b_out,
        ln2_gain,
        ln2_bias,
        w_fc,
        b_fc,
        w_proj,
        b_proj,
    ) = weight_set
    row_total = block_input.shape[0]
    grad_out = out_grad.astype(jnp.float32)
    grad_w_proj = product_tn(hidden_act, out_grad)
    grad_b_proj = jnp.sum(grad_out, axis=0)
    grad_act = product_nt(out_grad, w_proj)
    unused, gelu_pull = jax.vjp(jax.nn.gelu, hidden_pre)
    grad_pre = gelu_pull(grad_act)[0].astype(jnp.bfloat16)
    grad_w_fc = product_tn(normed_two, grad_pre)
    grad_b_fc = jnp.sum(grad_pre.astype(jnp.float32), axis=0)
    unused, norm_pull_two = jax.vjp(
        layer_norm, middle, ln2_gain.astype(jnp.float32), ln2_bias.astype(jnp.float32)
    )
    grad_mid_norm, grad_ln2_gain, grad_ln2_bias = norm_pull_two(product_nt(grad_pre, w_fc))
    grad_middle = grad_out + grad_mid_norm
    grad_mid_low = grad_middle.astype(jnp.bfloat16)
    grad_w_out = product_tn(mixed, grad_mid_low)
    grad_b_out = jnp.sum(grad_mid_low.astype(jnp.float32), axis=0)
    grad_heads = product_nt(grad_mid_low, w_out).astype(jnp.bfloat16).reshape(row_total, HEADS, HD)
    grad_q, kv_grads = attend_back(
        queries, kv_all, query_pos, seq_length, first_valid, log_total, attn_heads, grad_heads
    )
    kv_mine = lax.psum_scatter(
        kv_grads.astype(jnp.bfloat16), "fsdp", scatter_dimension=0, tiled=True
    ).astype(jnp.float32)
    grad_proj = jnp.concatenate([grad_q.reshape(row_total, D), kv_mine], axis=1).astype(
        jnp.bfloat16
    )
    grad_w_qkv = product_tn(normed_one, grad_proj)
    grad_b_qkv = jnp.sum(grad_proj.astype(jnp.float32), axis=0)
    unused, norm_pull_one = jax.vjp(
        layer_norm,
        block_input.astype(jnp.float32),
        ln1_gain.astype(jnp.float32),
        ln1_bias.astype(jnp.float32),
    )
    grad_in_norm, grad_ln1_gain, grad_ln1_bias = norm_pull_one(product_nt(grad_proj, w_qkv))
    input_grad = grad_middle + grad_in_norm
    grad_set = (
        grad_ln1_gain,
        grad_ln1_bias,
        grad_w_qkv,
        grad_b_qkv,
        grad_w_out,
        grad_b_out,
        grad_ln2_gain,
        grad_ln2_bias,
        grad_w_fc,
        grad_b_fc,
        grad_w_proj,
        grad_b_proj,
    )
    return (input_grad, grad_set)


def on_device_generic(
    block_input,
    seq_long,
    ln1_gain,
    ln1_bias,
    w_qkv,
    b_qkv,
    w_out,
    b_out,
    ln2_gain,
    ln2_bias,
    w_fc,
    b_fc,
    w_proj,
    b_proj,
    out_grad,
):
    long_flag = seq_long[0]
    fsdp_index = lax.axis_index("fsdp")
    weight_set = (
        lax.all_gather(ln1_gain, ("dp", "fsdp"), axis=0, tiled=True),
        lax.all_gather(ln1_bias, ("dp", "fsdp"), axis=0, tiled=True),
        lax.all_gather(w_qkv, ("dp", "fsdp"), axis=0, tiled=True),
        lax.all_gather(b_qkv, ("dp", "fsdp"), axis=0, tiled=True),
        lax.all_gather(w_out, ("dp", "fsdp"), axis=0, tiled=True),
        lax.all_gather(b_out, ("dp", "fsdp"), axis=0, tiled=True),
        lax.all_gather(ln2_gain, ("dp", "fsdp"), axis=0, tiled=True),
        lax.all_gather(ln2_bias, ("dp", "fsdp"), axis=0, tiled=True),
        lax.all_gather(w_fc, ("dp", "fsdp"), axis=0, tiled=True),
        lax.all_gather(b_fc, ("dp", "fsdp"), axis=0, tiled=True),
        lax.all_gather(w_proj, ("dp", "fsdp"), axis=0, tiled=True),
        lax.all_gather(b_proj, ("dp", "fsdp"), axis=0, tiled=True),
    )
    saved = forward(block_input, weight_set, long_flag, fsdp_index, gather_first)
    block_output = saved[0].astype(jnp.bfloat16)
    weight_set = (
        lax.all_gather(ln1_gain, ("dp", "fsdp"), axis=0, tiled=True),
        lax.all_gather(ln1_bias, ("dp", "fsdp"), axis=0, tiled=True),
        lax.all_gather(w_qkv, ("dp", "fsdp"), axis=0, tiled=True),
        lax.all_gather(b_qkv, ("dp", "fsdp"), axis=0, tiled=True),
        lax.all_gather(w_out, ("dp", "fsdp"), axis=0, tiled=True),
        lax.all_gather(b_out, ("dp", "fsdp"), axis=0, tiled=True),
        lax.all_gather(ln2_gain, ("dp", "fsdp"), axis=0, tiled=True),
        lax.all_gather(ln2_bias, ("dp", "fsdp"), axis=0, tiled=True),
        lax.all_gather(w_fc, ("dp", "fsdp"), axis=0, tiled=True),
        lax.all_gather(b_fc, ("dp", "fsdp"), axis=0, tiled=True),
        lax.all_gather(w_proj, ("dp", "fsdp"), axis=0, tiled=True),
        lax.all_gather(b_proj, ("dp", "fsdp"), axis=0, tiled=True),
    )
    saved = forward(block_input, weight_set, long_flag, fsdp_index, gather_second)
    input_grad, grad_set = backward(saved, weight_set, block_input, out_grad)
    grad_shards = (
        lax.psum_scatter(grad_set[0], ("dp", "fsdp"), scatter_dimension=0, tiled=True),
        lax.psum_scatter(grad_set[1], ("dp", "fsdp"), scatter_dimension=0, tiled=True),
        lax.psum_scatter(grad_set[2], ("dp", "fsdp"), scatter_dimension=0, tiled=True),
        lax.psum_scatter(grad_set[3], ("dp", "fsdp"), scatter_dimension=0, tiled=True),
        lax.psum_scatter(grad_set[4], ("dp", "fsdp"), scatter_dimension=0, tiled=True),
        lax.psum_scatter(grad_set[5], ("dp", "fsdp"), scatter_dimension=0, tiled=True),
        lax.psum_scatter(grad_set[6], ("dp", "fsdp"), scatter_dimension=0, tiled=True),
        lax.psum_scatter(grad_set[7], ("dp", "fsdp"), scatter_dimension=0, tiled=True),
        lax.psum_scatter(grad_set[8], ("dp", "fsdp"), scatter_dimension=0, tiled=True),
        lax.psum_scatter(grad_set[9], ("dp", "fsdp"), scatter_dimension=0, tiled=True),
        lax.psum_scatter(grad_set[10], ("dp", "fsdp"), scatter_dimension=0, tiled=True),
        lax.psum_scatter(grad_set[11], ("dp", "fsdp"), scatter_dimension=0, tiled=True),
    )
    return (block_output, input_grad) + tuple(grad_shards)


def nt(a, b): return lax.dot_general(a,b,(((1,),(1,)),((),())),preferred_element_type=f32)
def nn(a,b): return jnp.dot(a,b,preferred_element_type=f32)

def head_lanes(rows):
    return lax.broadcasted_iota(jnp.int32,(rows,128),1) < HD

def split_heads(pair):
    left = head_lanes(pair.shape[0])
    zero = jnp.zeros_like(pair)
    return (jnp.where(left,pair,zero), jnp.where(left,zero,pair))

def fwd_kernel(block, flag_ref, q_ref, k_ref, v_ref, o_ref, lse_ref, vt_ref):
    i = pl.program_id(0)
    pairs = q_ref.shape[1]//128
    @pl.when(i==0)
    def _():
        for p in range(pairs):
            vt_ref[p*128:(p+1)*128,:] = v_ref[:,p*128:(p+1)*128].astype(f32).T.astype(bf)
    per_seq = jnp.where(flag_ref[0]==1, 2*SEQ, SEQ)//block
    first = i//per_seq*per_seq
    qm=[]
    for p in range(pairs):
        qm.extend(split_heads(q_ref[:,p*128:(p+1)*128]))
    nh=2*pairs
    diag = lax.broadcasted_iota(jnp.int32,(block,block),0) <= lax.broadcasted_iota(jnp.int32,(block,block),1)
    def step(j, state, masked):
        start = pl.multiple_of(j*block, block)
        out=[]
        for h in range(nh):
            p=h//2
            s = nt(k_ref[pl.ds(start,block),p*128:(p+1)*128], qm[h])
            x = s*s+1.0
            mag = x*lax.rsqrt(x)
            if masked: mag = jnp.where(diag,mag,-1e30)
            top = jnp.max(mag,axis=0,keepdims=True)
            if state is not None:
                old_top, old_sum, old_acc = state[h]
                top = jnp.maximum(top, old_top)
            e = jnp.exp(mag-top)
            fresh = jnp.sum(e,axis=0,keepdims=True)
            w = (jnp.tanh(s)*e).astype(bf)
            part = nn(vt_ref[h*HD:(h+1)*HD,pl.ds(start,block)], w)
            if state is not None:
                alpha = jnp.exp(old_top-top)
                fresh = fresh + alpha*old_sum
                part = part + alpha*old_acc
            out.append((top,fresh,part))
        return tuple(out)
    state = step(i,None,True)
    state = lax.fori_loop(first,i,lambda j,st: step(j,st,False),state)
    for h in range(nh):
        top,total,acc = state[h]
        lse_ref[h:h+1,:] = top+jnp.log(total)
    for p in range(pairs):
        o2 = jnp.concatenate([state[2*p][2]/state[2*p][1], state[2*p+1][2]/state[2*p+1][1]],axis=0)
        o_ref[:,p*128:(p+1)*128] = o2.T.astype(bf)

def attend_fwd(flag, qkv, block):
    rows=qkv.shape[0]; width=qkv.shape[1]//3
    full=lambda c: pl.BlockSpec((rows,width),lambda i,f:(0,c))
    return pl.pallas_call(functools.partial(fwd_kernel,block),
        grid_spec=pltpu.PrefetchScalarGridSpec(num_scalar_prefetch=1,grid=(rows//block,),
            in_specs=[pl.BlockSpec((block,width),lambda i,f:(i,0)),full(1),full(2)],
            out_specs=[pl.BlockSpec((block,width),lambda i,f:(i,0)),pl.BlockSpec((8,block),lambda i,f:(0,i))],
            scratch_shapes=[pltpu.VMEM((width,rows),bf)]),
        out_shape=[jax.ShapeDtypeStruct((rows,width),bf),jax.ShapeDtypeStruct((8,rows),f32)],
        name="attend_fwd")(flag,qkv,qkv,qkv)

def bwd_kernel(block, flag_ref, q_ref, k_ref, v_ref, o_ref, do_ref, lse_ref, g_ref, dqt_ref, inner_ref):
    j = pl.program_id(0); last = pl.num_programs(0)-1
    width=k_ref.shape[1]; pairs=width//128; nh=2*pairs; rows=q_ref.shape[0]
    @pl.when(j==0)
    def _():
        dqt_ref[...]=jnp.zeros_like(dqt_ref)
        acc=jnp.zeros((8,rows),f32)
        for p in range(pairs):
            prod=o_ref[:,p*128:(p+1)*128].astype(f32)*do_ref[:,p*128:(p+1)*128].astype(f32)
            hrow=lax.broadcasted_iota(jnp.int32,(8,128),0); lane=lax.broadcasted_iota(jnp.int32,(8,128),1)
            sel=(hrow==2*p+lane//HD).astype(f32)
            acc=acc+lax.dot_general(sel,prod,(((1,),(1,)),((),())),precision=lax.Precision.HIGHEST,preferred_element_type=f32)
        inner_ref[...]=acc
    per_seq = jnp.where(flag_ref[0]==1, 2*SEQ, SEQ)//block
    stop = (j//per_seq+1)*per_seq
    km=[];vm=[];kt=[]
    for p in range(pairs):
        kp=k_ref[:,p*128:(p+1)*128]
        km.extend(split_heads(kp)); vm.extend(split_heads(v_ref[:,p*128:(p+1)*128]))
        ktp=kp.astype(f32).T.astype(bf)
        kt.extend((ktp[:HD],ktp[HD:]))
    diag = lax.broadcasted_iota(jnp.int32,(block,block),0) <= lax.broadcasted_iota(jnp.int32,(block,block),1)
    def step(i, state, masked):
        start = pl.multiple_of(i*block, block)
        out=[]
        for p in range(pairs):
            cols=slice(p*128,(p+1)*128)
            qp=q_ref[pl.ds(start,block),cols]; dop=do_ref[pl.ds(start,block),cols]
            qh=split_heads(qp); doh=split_heads(dop)
            dk=dv=None
            for a in range(2):
                h=2*p+a
                s=nt(km[h],qp)
                x=s*s+1.0
                r=lax.rsqrt(x)
                e=jnp.exp(x*r-lse_ref[h:h+1,pl.ds(start,block)])
                if masked: e=jnp.where(diag,e,0.0)
                t=jnp.tanh(s)
                w=(t*e).astype(bf)
                gw=nt(vm[h],dop)
                slope=s*r
                ds=(e*(gw*(1.0-t*t+t*slope)-slope*inner_ref[h:h+1,pl.ds(start,block)])).astype(bf)
                pv=nn(w,doh[a]); pk=nn(ds,qh[a])
                dv = pv if dv is None else dv+pv
                dk = pk if dk is None else dk+pk
                dqt_ref[h*HD:(h+1)*HD,pl.ds(start,block)] += nn(kt[h],ds)
            if state is not None:
                dk=dk+state[p][0]; dv=dv+state[p][1]
            out.append((dk,dv))
        return tuple(out)
    state=step(j,None,True)
    state=lax.fori_loop(j+1,stop,lambda i,st: step(i,st,False),state)
    mine=pl.ds(pl.multiple_of(j*block,block),block)
    for p in range(pairs):
        g_ref[mine,width+p*128:width+(p+1)*128]=state[p][0].astype(bf)
        g_ref[mine,2*width+p*128:2*width+(p+1)*128]=state[p][1].astype(bf)
    @pl.when(j==last)
    def _():
        for p in range(pairs):
            g_ref[:,p*128:(p+1)*128]=(dqt_ref[p*128:(p+1)*128,:]*HD**-0.5).T.astype(bf)

def attend_bwd(flag, qkv, heads_out, grad_heads, lse, block):
    rows=qkv.shape[0]; width=qkv.shape[1]//3
    full=lambda c: pl.BlockSpec((rows,width),lambda j,f:(0,c))
    part=lambda c: pl.BlockSpec((block,width),lambda j,f:(j,c))
    return pl.pallas_call(functools.partial(bwd_kernel,block),
        grid_spec=pltpu.PrefetchScalarGridSpec(num_scalar_prefetch=1,grid=(rows//block,),
            in_specs=[full(0),part(1),part(2),full(0),full(0),pl.BlockSpec((8,rows),lambda j,f:(0,0))],
            out_specs=pl.BlockSpec((rows,3*width),lambda j,f:(0,0)),
            scratch_shapes=[pltpu.VMEM((width,rows),f32),pltpu.VMEM((8,rows),f32)]),
        out_shape=jax.ShapeDtypeStruct((rows,3*width),bf),
        name="attend_bwd")(flag,qkv,qkv,qkv,heads_out,grad_heads,lse)


def tn(a, b):
    return lax.dot_general(a, b, (((0,), (0,)), ((), ())), preferred_element_type=f32)


def norm_stats(rows_in):
    mean = jnp.mean(rows_in, axis=-1, keepdims=True)
    centred = rows_in - mean
    variance = jnp.mean(centred * centred, axis=-1, keepdims=True)
    scale = lax.rsqrt(variance + EPS)
    return centred * scale, scale


def project_kernel(place_ref, own_ref, other_ref, gain_ref, bias_ref, w_ref, b_ref, n_ref, p_ref):
    per_side = pl.num_programs(0) // 2
    is_own = pl.program_id(0) // per_side == place_ref[0]
    rows = jnp.where(is_own, own_ref[...], other_ref[...]).astype(f32)
    unit, unused = norm_stats(rows)
    normed = (unit * gain_ref[...] + bias_ref[...]).astype(bf)
    n_ref[...] = normed
    width = p_ref.shape[1] // 3
    for c in range(3):
        cols = slice(c * width, (c + 1) * width)
        part = (nn(normed, w_ref[:, cols]) + b_ref[:, cols]).astype(bf)
        p_ref[:, cols] = part * jnp.asarray(HD**-0.5, bf) if c == 0 else part


def project(place, own, other, gain, bias, weight, w_bias, block=256):
    rows, width = own.shape
    per_side = rows // block
    cols = weight.shape[1]
    fixed = lambda shape: pl.BlockSpec(shape, lambda i, s: (0, 0))
    return pl.pallas_call(
        project_kernel,
        grid_spec=pltpu.PrefetchScalarGridSpec(
            num_scalar_prefetch=1,
            grid=(2 * per_side,),
            in_specs=[
                pl.BlockSpec(
                    (block, width), lambda i, s: (jnp.clip(i - s[0] * per_side, 0, per_side - 1), 0)
                ),
                pl.BlockSpec(
                    (block, width),
                    lambda i, s: (jnp.clip(i - (1 - s[0]) * per_side, 0, per_side - 1), 0),
                ),
                fixed((1, width)),
                fixed((1, width)),
                fixed(weight.shape),
                fixed((1, cols)),
            ],
            out_specs=[
                pl.BlockSpec((block, width), lambda i, s: (i, 0)),
                pl.BlockSpec((block, cols), lambda i, s: (i, 0)),
            ],
        ),
        out_shape=[
            jax.ShapeDtypeStruct((2 * rows, width), bf),
            jax.ShapeDtypeStruct((2 * rows, cols), bf),
        ],
        name="norm_project",
    )(place, own, other, gain, bias, weight, w_bias)


GELU_C = math.sqrt(2 / math.pi)


def mlp_kernel(
    place_ref,
    g_hbm,
    x_ref,
    og_ref,
    ha_ref,
    hb_ref,
    bout_ref,
    gain_ref,
    bias_ref,
    bfc_ref,
    bproj_ref,
    out_ref,
    mixed_ref,
    n2_ref,
    act_ref,
    gp_ref,
    gm_ref,
    gml_ref,
    keep_ref,
    send_ref,
    sums_ref,
    w_ref,
    sem,
):
    i = pl.program_id(0)
    devices = g_hbm.shape[0]
    sub = g_hbm.shape[2]
    width = devices * sub
    chunks = (g_hbm.shape[1] - 1) // 2

    def load(slot):
        return pltpu.make_async_copy(g_hbm.at[:, slot], w_ref.at[slot], sem.at[slot])

    order = [2 * chunks] + list(range(chunks, 2 * chunks))

    def load_proj():
        return pltpu.make_async_copy(
            g_hbm.at[:, pl.ds(0, chunks)], wp_view(), sem.at[0]
        )

    def wp_view():
        return w_ref.at[pl.ds(0, chunks)].reshape(devices, chunks, sub, width)

    @pl.when(i == 0)
    def _():
        for slot in order:
            load(slot).start()
        load_proj().start()
        for slot in order:
            load(slot).wait()
        load_proj().wait()
        sums_ref[...] = jnp.zeros_like(sums_ref)

    def weight(slot):
        return w_ref[slot].reshape(width, width)

    on_left = place_ref[0] == 0
    ha = ha_ref[...]
    hb = hb_ref[...]
    mixed = jnp.concatenate([jnp.where(on_left, ha, hb), jnp.where(on_left, hb, ha)], axis=1)
    mixed_ref[...] = mixed
    og_low = og_ref[...]
    og = og_low.astype(f32)
    middle = x_ref[...].astype(f32) + nn(mixed, weight(2 * chunks)) + bout_ref[...]
    unit, scale = norm_stats(middle)
    n2 = (unit * gain_ref[...] + bias_ref[...]).astype(bf)
    n2_ref[...] = n2
    out = middle + bproj_ref[...]
    e = jnp.zeros_like(middle)
    for c in range(chunks):
        cols = slice(c * width, (c + 1) * width)
        w_fc = weight(chunks + c)
        w_proj = weight(c)
        pre = nn(n2, w_fc) + bfc_ref[:, cols]
        square = pre * pre
        t = jnp.tanh(GELU_C * pre * (1.0 + 0.044715 * square))
        low_half = 0.5 * (1.0 + t)
        act = (pre * low_half).astype(bf)
        act_ref[:, cols] = act
        out = out + nn(act, w_proj)
        slope = low_half + 0.5 * pre * (1.0 - t * t) * (
            GELU_C * (1.0 + 3.0 * 0.044715 * square)
        )
        gp = (nt(og_low, w_proj) * slope).astype(bf)
        gp_ref[:, cols] = gp
        sums_ref[0:1, cols] += jnp.sum(gp.astype(f32), axis=0, keepdims=True)
        e = e + nt(gp, w_fc)
    out_ref[...] = out.astype(bf)
    sums_ref[1:2, 0:width] += jnp.sum(og, axis=0, keepdims=True)
    sums_ref[1:2, width : 2 * width] += jnp.sum(e * unit, axis=0, keepdims=True)
    sums_ref[1:2, 2 * width : 3 * width] += jnp.sum(e, axis=0, keepdims=True)
    eg = e * gain_ref[...]
    gm = og + scale * (
        eg
        - jnp.mean(eg, axis=-1, keepdims=True)
        - unit * jnp.mean(eg * unit, axis=-1, keepdims=True)
    )
    gm_ref[...] = gm
    gml = gm.astype(bf)
    gml_ref[...] = gml
    sums_ref[1:2, 3 * width : 4 * width] += jnp.sum(gml.astype(f32), axis=0, keepdims=True)
    gh = nt(gml, weight(2 * chunks)).astype(bf)
    half = width // 2
    left = gh[:, :half]
    right = gh[:, half:]
    keep_ref[...] = jnp.where(on_left, left, right)
    send_ref[...] = jnp.where(on_left, right, left)


def mlp(place, gathered, x, og, heads_mine, heads_other, b_out, gain, bias, b_fc, b_proj, block=256):
    rows, width = x.shape
    steps = rows // block
    hidden = b_fc.shape[1]
    row = lambda cols: pl.BlockSpec((block, cols), lambda i, s: (i, 0))
    fixed = lambda cols: pl.BlockSpec((1, cols), lambda i, s: (0, 0))
    shape = lambda cols, kind: jax.ShapeDtypeStruct((rows, cols), kind)
    return pl.pallas_call(
        mlp_kernel,
        grid_spec=pltpu.PrefetchScalarGridSpec(
            num_scalar_prefetch=1,
            grid=(steps,),
            in_specs=[
                pl.BlockSpec(memory_space=pl.ANY),
                row(width),
                row(width),
                pl.BlockSpec((block, width // 2), lambda i, s: (s[0] * steps + i, 0)),
                row(width // 2),
                fixed(width),
                fixed(width),
                fixed(width),
                fixed(hidden),
                fixed(width),
            ],
            out_specs=[
                row(width),
                row(width),
                row(width),
                row(hidden),
                row(hidden),
                row(width),
                row(width),
                row(width // 2),
                row(width // 2),
                pl.BlockSpec((8, hidden), lambda i, s: (0, 0)),
            ],
            scratch_shapes=[
                pltpu.VMEM((gathered.shape[1], gathered.shape[0], gathered.shape[2], width), bf),
                pltpu.SemaphoreType.DMA((gathered.shape[1],)),
            ],
        ),
        out_shape=[
            shape(width, bf),
            shape(width, bf),
            shape(width, bf),
            shape(hidden, bf),
            shape(hidden, bf),
            shape(width, f32),
            shape(width, bf),
            shape(width // 2, bf),
            shape(width // 2, bf),
            jax.ShapeDtypeStruct((8, hidden), f32),
        ],
        compiler_params=pltpu.CompilerParams(vmem_limit_bytes=56 * 1024 * 1024),
        name="mlp",
    )(place, gathered, x, og, heads_mine, heads_other, b_out, gain, bias, b_fc, b_proj)


def weight_grad_kernel(act_ref, gp_ref, og_ref, n2_ref, mixed_ref, gml_ref, out_hbm, buf_ref, sem):
    c = pl.program_id(0)
    last = pl.num_programs(0) - 1
    devices, slots, sub, width = out_hbm.shape
    chunks = (slots - 1) // 2
    group = devices // chunks
    slot = lax.rem(c, 2)

    def proj_copy(step, where):
        return pltpu.make_async_copy(
            buf_ref.at[where].reshape(group, chunks, sub, width),
            out_hbm.at[pl.ds(step * group, group), pl.ds(0, chunks)],
            sem.at[where],
        )

    def other_copy(step, where):
        return pltpu.make_async_copy(buf_ref.at[where], out_hbm.at[:, step], sem.at[where])

    @pl.when(c >= 2)
    def _():
        other_copy(chunks, slot).wait()

    def put(value):
        buf_ref[slot] = value.astype(bf).reshape(devices, sub, width)

    @pl.when(c < chunks)
    def _():
        put(tn(act_ref[...], og_ref[...]))
        proj_copy(c, slot).start()

    @pl.when((c >= chunks) & (c < 2 * chunks))
    def _():
        put(tn(n2_ref[...], gp_ref[...]))
        other_copy(c, slot).start()

    @pl.when(c == last)
    def _():
        put(tn(mixed_ref[...], gml_ref[...]))
        other_copy(c, slot).start()
        other_copy(chunks, 1 - slot).wait()
        other_copy(chunks, slot).wait()


def weight_grads(act, gp, og, n2, mixed, gml, devices):
    rows, width = og.shape
    chunks = act.shape[1] // width
    slots = 2 * chunks + 1
    sub = width // devices
    fixed = pl.BlockSpec((rows, width), lambda c: (0, 0))
    return pl.pallas_call(
        weight_grad_kernel,
        grid=(slots,),
        in_specs=[
            pl.BlockSpec((rows, width), lambda c: (0, jnp.minimum(c, chunks - 1))),
            pl.BlockSpec((rows, width), lambda c: (0, jnp.clip(c - chunks, 0, chunks - 1))),
            fixed,
            fixed,
            fixed,
            fixed,
        ],
        out_specs=pl.BlockSpec(memory_space=pl.ANY),
        out_shape=jax.ShapeDtypeStruct((devices, slots, sub, width), bf),
        scratch_shapes=[
            pltpu.VMEM((2, devices, sub, width), bf),
            pltpu.SemaphoreType.DMA((2,)),
        ],
        name="weight_grads",
    )(act, gp, og, n2, mixed, gml)


AXES = ("dp", "fsdp")


def swap(value, bit, total):
    return lax.ppermute(value, AXES, [(i, i ^ bit) for i in range(total)])


def gather_dp(shard, dp_size, order):
    me = lax.axis_index("dp")
    bits = dp_size.bit_length() - 1
    held = shard.reshape((1,) * bits + shard.shape)
    for bit in order:
        other = swap(held, 2 << bit, 2 * dp_size)
        low = (me >> bit) & 1 == 0
        held = jnp.concatenate(
            [jnp.where(low, held, other), jnp.where(low, other, held)], axis=bits - 1 - bit
        )
    return held.reshape((dp_size * shard.shape[0],) + shard.shape[1:])


def scatter_dp(whole, dp_size, order):
    me = lax.axis_index("dp")
    bits = dp_size.bit_length() - 1
    rows = whole.shape[0] // dp_size
    held = whole.reshape((2,) * bits + (rows,) + whole.shape[1:])
    for bit in order:
        axis = bits - 1 - bit
        low = (me >> bit) & 1 == 0
        first = lax.slice_in_dim(held, 0, 1, axis=axis)
        second = lax.slice_in_dim(held, 1, 2, axis=axis)
        mine = jnp.where(low, first, second)
        sent = jnp.where(low, second, first).astype(bf)
        held = mine.astype(f32) + swap(sent, 2 << bit, 2 * dp_size).astype(f32)
    return held.reshape((rows,) + whole.shape[1:])


def sum_all(vector, total):
    bit = 1
    while bit < total:
        vector = vector + swap(vector, bit, total)
        bit *= 2
    return vector


def on_device_pair(
    dp_size,
    block_input,
    seq_long,
    ln1_gain,
    ln1_bias,
    w_qkv,
    b_qkv,
    w_out,
    b_out,
    ln2_gain,
    ln2_bias,
    w_fc,
    b_fc,
    w_proj,
    b_proj,
    out_grad,
):
    total = 2 * dp_size
    side = lax.axis_index("fsdp")
    flat = lax.axis_index("dp") * 2 + side
    on_left = side == 0
    row_total = block_input.shape[0]
    half = D // 2
    dp_bits = list(range(dp_size.bit_length() - 1))
    gather_order = dp_bits[1:2] + dp_bits[:1:-1] + dp_bits[:1]
    scatter_order = dp_bits[:1] + dp_bits[2:] + dp_bits[1:2]

    def ordered(mine, other, axis):
        return jnp.concatenate(
            [jnp.where(on_left, mine, other), jnp.where(on_left, other, mine)], axis=axis
        )

    def head_columns(rows_in, which):
        three = rows_in.reshape(rows_in.shape[0], 3, 2, half)
        return lax.dynamic_slice_in_dim(three, which, 1, axis=2).reshape(
            rows_in.shape[0], 3 * half
        )

    small = (ln1_gain, ln1_bias, b_qkv, b_out, ln2_gain, ln2_bias, b_fc, b_proj)
    placed = jnp.concatenate(
        [
            lax.dynamic_update_slice(
                jnp.zeros((item.shape[0] * total,), bf), item, (item.shape[0] * flat,)
            )
            for item in small
        ]
    )
    gathered = sum_all(placed, total).astype(f32)
    pieces = []
    start = 0
    for item in small:
        pieces.append(gathered[start : start + item.shape[0] * total])
        start += item.shape[0] * total
    ln1_gain, ln1_bias, b_qkv, b_out, ln2_gain, ln2_bias, b_fc, b_proj = pieces

    other_input = swap(block_input, 1, total)
    received = swap(head_columns(w_qkv, 1 - side), 1, total)
    w_mine = gather_dp(ordered(head_columns(w_qkv, side), received, 0), dp_size, gather_order)
    sub = w_out.shape[0]
    chunks = FF // D
    packed = jnp.concatenate(
        [w_proj] + [w_fc[:, c * D : (c + 1) * D] for c in range(chunks)] + [w_out], axis=0
    )
    gathered_w = lax.all_gather(packed, AXES, axis=0, tiled=True)
    gathered_w = gathered_w.reshape(total, 2 * chunks + 1, sub, D)

    def as_row(vector):
        return vector.reshape(1, -1)

    def rows_of(whole, which):
        return lax.dynamic_slice_in_dim(whole, which * row_total, row_total, axis=0)

    place = side.astype(jnp.int32).reshape(1)
    b_mine = head_columns(as_row(b_qkv), side)
    normed_one, projected = project(
        place, block_input, other_input, as_row(ln1_gain), as_row(ln1_bias), w_mine, b_mine
    )
    heads_mine, log_total = attend_fwd(seq_long, projected, 512)
    heads_other = swap(rows_of(heads_mine, 1 - side), 1, total)
    (
        block_output,
        mixed,
        normed_two,
        hidden_act,
        grad_pre,
        grad_middle,
        grad_mid_low,
        grad_heads_keep,
        grad_heads_send,
        sums,
    ) = mlp(
        place,
        gathered_w,
        block_input,
        out_grad,
        heads_mine,
        heads_other,
        as_row(b_out),
        as_row(ln2_gain),
        as_row(ln2_bias),
        as_row(b_fc),
        as_row(b_proj),
    )
    grad_heads_other = swap(grad_heads_send, 1, total)
    packed_grads = weight_grads(
        hidden_act, grad_pre, out_grad, normed_two, mixed, grad_mid_low, total
    )
    shard = lax.psum_scatter(
        packed_grads.reshape(total * (2 * chunks + 1) * sub, D),
        AXES,
        scatter_dimension=0,
        tiled=True,
    ).astype(f32)
    shard_w_proj = shard[: chunks * sub]
    shard_w_fc = jnp.concatenate(
        [shard[(chunks + c) * sub : (chunks + c + 1) * sub] for c in range(chunks)], axis=1
    )
    shard_w_out = shard[2 * chunks * sub :]
    grad_b_fc = sums[0]
    grad_b_proj, grad_ln2_gain, grad_ln2_bias, grad_b_out = (
        sums[1, k * D : (k + 1) * D] for k in range(4)
    )
    grad_heads_mine = ordered(grad_heads_keep, grad_heads_other, 0)
    grad_proj = attend_bwd(seq_long, projected, heads_mine, grad_heads_mine, log_total, 512)

    wide_input = block_input.astype(f32)
    e_sent = product_nt(rows_of(grad_proj, 1 - side), w_mine).astype(bf)
    e_other = swap(e_sent, 1, total)
    grad_w_mine = product_tn(normed_one, grad_proj).astype(bf)
    shard_mine = scatter_dp(grad_w_mine, dp_size, scatter_order)
    shard_rows = shard_mine.reshape(2, shard_mine.shape[0] // 2, 3 * half)
    keep = lax.dynamic_index_in_dim(shard_rows, side, 0, keepdims=False)
    send = lax.dynamic_index_in_dim(shard_rows, 1 - side, 0, keepdims=False)
    taken = swap(send, 1, total)
    shard_w_qkv = ordered(
        keep.reshape(-1, 3, 1, half), taken.reshape(-1, 3, 1, half), 2
    ).reshape(-1, 3 * D)
    grad_b_mine = jnp.sum(grad_proj.astype(f32), axis=0).reshape(3, 1, half)
    zero_b = jnp.zeros_like(grad_b_mine)
    grad_b_qkv = ordered(grad_b_mine, zero_b, 1).reshape(3 * D)
    e_mine = product_nt(rows_of(grad_proj, side), w_mine) + e_other.astype(f32)
    unused, norm_pull_one = jax.vjp(layer_norm, wide_input, ln1_gain, ln1_bias)
    grad_in_norm, grad_ln1_gain, grad_ln1_bias = norm_pull_one(e_mine)
    input_grad = grad_middle + grad_in_norm

    early = (grad_b_out, grad_ln2_gain, grad_ln2_bias, grad_b_fc, grad_b_proj)
    late = (grad_ln1_gain, grad_ln1_bias, grad_b_qkv)

    def reduce_small(items):
        summed = sum_all(jnp.concatenate(items), total)
        begin = 0
        shards = []
        for item in items:
            size = item.shape[0] // total
            shards.append(lax.dynamic_slice(summed, (begin + size * flat,), (size,)))
            begin += item.shape[0]
        return shards

    shard_b_out, shard_ln2_gain, shard_ln2_bias, shard_b_fc, shard_b_proj = reduce_small(early)
    shard_ln1_gain, shard_ln1_bias, shard_b_qkv = reduce_small(late)
    return (
        block_output,
        input_grad,
        shard_ln1_gain,
        shard_ln1_bias,
        shard_w_qkv,
        shard_b_qkv,
        shard_w_out,
        shard_b_out,
        shard_ln2_gain,
        shard_ln2_bias,
        shard_w_fc,
        shard_b_fc,
        shard_w_proj,
        shard_b_proj,
    )


def solution(mesh):
    in_specs = (
        P(("dp", "fsdp"), None),
        P("dp"),
        P(("dp", "fsdp")),
        P(("dp", "fsdp")),
        P(("dp", "fsdp"), None),
        P(("dp", "fsdp")),
        P(("dp", "fsdp"), None),
        P(("dp", "fsdp")),
        P(("dp", "fsdp")),
        P(("dp", "fsdp")),
        P(("dp", "fsdp"), None),
        P(("dp", "fsdp")),
        P(("dp", "fsdp"), None),
        P(("dp", "fsdp")),
        P(("dp", "fsdp"), None),
    )
    out_specs = (
        P(("dp", "fsdp"), None),
        P(("dp", "fsdp"), None),
        P(("dp", "fsdp")),
        P(("dp", "fsdp")),
        P(("dp", "fsdp"), None),
        P(("dp", "fsdp")),
        P(("dp", "fsdp"), None),
        P(("dp", "fsdp")),
        P(("dp", "fsdp")),
        P(("dp", "fsdp")),
        P(("dp", "fsdp"), None),
        P(("dp", "fsdp")),
        P(("dp", "fsdp"), None),
        P(("dp", "fsdp")),
    )
    split_by_heads = (
        mesh.shape["fsdp"] == 2 and mesh.shape["dp"] & (mesh.shape["dp"] - 1) == 0
    )
    return jax.shard_map(
        functools.partial(on_device_pair, mesh.shape["dp"]) if split_by_heads else on_device_generic, mesh=mesh, in_specs=in_specs, out_specs=out_specs, check_vma=False
    )
```

```python
import functools
import math

import jax
import jax.numpy as jnp
from jax import lax
from jax.experimental import pallas as pl
from jax.experimental.pallas import tpu as pltpu
from jax.sharding import PartitionSpec as P


f32 = jnp.float32
bf = jnp.bfloat16


D = 768
HEADS = 12
HD = 64
FF = 3072
SEQ = 1024


EPS = 1e-05
FAR = -1e30


def layer_norm(rows_in, gain_vec, bias_vec):
    row_mean = jnp.mean(rows_in, axis=-1, keepdims=True)
    centred = rows_in - row_mean
    variance = jnp.mean(centred * centred, axis=-1, keepdims=True)
    return centred * lax.rsqrt(variance + EPS) * gain_vec + bias_vec


def product(left, right):
    return jnp.dot(left, right, preferred_element_type=jnp.float32)


def product_tn(left, right):
    return lax.dot_general(
        left, right, (((0,), (0,)), ((), ())), preferred_element_type=jnp.float32
    )


def product_nt(left, right):
    return lax.dot_general(
        left, right, (((1,), (1,)), ((), ())), preferred_element_type=jnp.float32
    )


def gather_first(kv_rows):
    return lax.all_gather(kv_rows, "fsdp", axis=0, tiled=True)


def gather_second(kv_rows):
    return lax.all_gather(kv_rows, "fsdp", axis=0, tiled=True)


def block_layout(kv_all):
    group_rows = kv_all.shape[0]
    key_block = math.gcd(group_rows, 512)
    block_count = group_rows // key_block
    kv_blocks = kv_all.reshape(block_count, key_block, 2, HEADS, HD)
    return (key_block, kv_blocks, jnp.arange(block_count, dtype=jnp.int32))


def block_allowed(query_pos, key_start, key_block, seq_length):
    key_pos = key_start + jnp.arange(key_block, dtype=jnp.int32)
    return (query_pos[:, None] // seq_length == key_pos[None, :] // seq_length) & (
        key_pos[None, :] <= query_pos[:, None]
    )


def block_useful(key_start, key_block, query_pos, first_valid):
    return (key_start <= query_pos[-1]) & (key_start + key_block - 1 >= first_valid)


def score_parts(queries, key_part):
    scores = jnp.einsum(
        "qhd,khd->hqk", queries, key_part, preferred_element_type=jnp.float32
    ) * HD ** (-0.5)
    return (scores, jnp.sqrt(scores * scores + 1.0))


def attend(queries, kv_all, query_pos, seq_length, first_valid):
    key_block, kv_blocks, block_ids = block_layout(kv_all)
    row_total = queries.shape[0]

    def stats_step(state_now, block_item):
        block_id, kv_part = block_item
        key_start = block_id * key_block

        def stats_compute(state_in):
            row_top, row_sum = state_in
            allowed = block_allowed(query_pos, key_start, key_block, seq_length)[None]
            _, magnitude = score_parts(queries, kv_part[:, 0])
            masked = jnp.where(allowed, magnitude, FAR)
            new_top = jnp.maximum(row_top, jnp.max(masked, axis=-1))
            fresh = jnp.sum(jnp.where(allowed, jnp.exp(masked - new_top[:, :, None]), 0.0), axis=-1)
            return (new_top, row_sum * jnp.exp(row_top - new_top) + fresh)

        useful = block_useful(key_start, key_block, query_pos, first_valid)
        return (lax.cond(useful, stats_compute, lambda kept_state: kept_state, state_now), None)

    start_state = (
        jnp.full((HEADS, row_total), FAR, jnp.float32),
        jnp.zeros((HEADS, row_total), jnp.float32),
    )
    (row_top, row_sum), unused = lax.scan(stats_step, start_state, (block_ids, kv_blocks))
    log_total = row_top + jnp.log(row_sum)

    def value_step(accum_now, block_item):
        block_id, kv_part = block_item
        key_start = block_id * key_block

        def value_compute(accum_in):
            allowed = block_allowed(query_pos, key_start, key_block, seq_length)[None]
            scores, magnitude = score_parts(queries, kv_part[:, 0])
            weights = jnp.where(
                allowed, jnp.tanh(scores) * jnp.exp(magnitude - log_total[:, :, None]), 0.0
            ).astype(jnp.bfloat16)
            return accum_in + jnp.einsum(
                "hqk,khd->qhd", weights, kv_part[:, 1], preferred_element_type=jnp.float32
            )

        useful = block_useful(key_start, key_block, query_pos, first_valid)
        return (lax.cond(useful, value_compute, lambda kept_accum: kept_accum, accum_now), None)

    start_accum = jnp.zeros((row_total, HEADS, HD), jnp.float32)
    attn_heads, unused = lax.scan(value_step, start_accum, (block_ids, kv_blocks))
    return (attn_heads, log_total)


def attend_back(
    queries, kv_all, query_pos, seq_length, first_valid, log_total, attn_heads, grad_heads
):
    key_block, kv_blocks, block_ids = block_layout(kv_all)
    row_total = queries.shape[0]
    inner = jnp.transpose(jnp.sum(grad_heads.astype(jnp.float32) * attn_heads, axis=-1))

    def grad_step(dq_now, block_item):
        block_id, kv_part = block_item
        key_start = block_id * key_block

        def grad_compute(dq_in):
            allowed = block_allowed(query_pos, key_start, key_block, seq_length)[None]
            scores, magnitude = score_parts(queries, kv_part[:, 0])
            expo = jnp.where(allowed, jnp.exp(magnitude - log_total[:, :, None]), 0.0)
            tangent = jnp.tanh(scores)
            weights = (tangent * expo).astype(jnp.bfloat16)
            grad_v = jnp.einsum(
                "hqk,qhd->khd", weights, grad_heads, preferred_element_type=jnp.float32
            )
            grad_weight = jnp.einsum(
                "qhd,khd->hqk", grad_heads, kv_part[:, 1], preferred_element_type=jnp.float32
            )
            slope = scores / magnitude
            grad_scores = (
                expo
                * (
                    grad_weight * (1.0 - tangent * tangent + tangent * slope)
                    - slope * inner[:, :, None]
                )
            ).astype(jnp.bfloat16)
            dq_out = dq_in + jnp.einsum(
                "hqk,khd->qhd", grad_scores, kv_part[:, 0], preferred_element_type=jnp.float32
            ) * HD ** (-0.5)
            grad_k = jnp.einsum(
                "hqk,qhd->khd", grad_scores, queries, preferred_element_type=jnp.float32
            ) * HD ** (-0.5)
            return (
                dq_out,
                jnp.concatenate(
                    [grad_k.reshape(key_block, D), grad_v.reshape(key_block, D)], axis=1
                ),
            )

        def skip_block(dq_in):
            return (dq_in, jnp.zeros((key_block, 2 * D), jnp.float32))

        useful = block_useful(key_start, key_block, query_pos, first_valid)
        return lax.cond(useful, grad_compute, skip_block, dq_now)

    start_dq = jnp.zeros((row_total, HEADS, HD), jnp.float32)
    grad_q, kv_grads = lax.scan(grad_step, start_dq, (block_ids, kv_blocks))
    return (grad_q, kv_grads.reshape(kv_all.shape[0], 2 * D))


def forward(block_input, weight_set, long_flag, fsdp_index, gather_keys):
    (
        ln1_gain,
        ln1_bias,
        w_qkv,
        b_qkv,
        w_out,
        b_out,
        ln2_gain,
        ln2_bias,
        w_fc,
        b_fc,
        w_proj,
        b_proj,
    ) = weight_set
    row_total = block_input.shape[0]
    wide_input = block_input.astype(jnp.float32)
    normed_one = layer_norm(
        wide_input, ln1_gain.astype(jnp.float32), ln1_bias.astype(jnp.float32)
    ).astype(jnp.bfloat16)
    projected = (product(normed_one, w_qkv) + b_qkv.astype(jnp.float32)).astype(jnp.bfloat16)
    queries = projected[:, :D].reshape(row_total, HEADS, HD)
    kv_all = gather_keys(projected[:, D:])
    seq_length = jnp.where(long_flag == 1, 2 * SEQ, SEQ).astype(jnp.int32)
    query_pos = fsdp_index * row_total + jnp.arange(row_total, dtype=jnp.int32)
    first_valid = query_pos[0] // seq_length * seq_length
    attn_heads, log_total = attend(queries, kv_all, query_pos, seq_length, first_valid)
    mixed = attn_heads.reshape(row_total, D).astype(jnp.bfloat16)
    middle = wide_input + product(mixed, w_out) + b_out.astype(jnp.float32)
    normed_two = layer_norm(
        middle, ln2_gain.astype(jnp.float32), ln2_bias.astype(jnp.float32)
    ).astype(jnp.bfloat16)
    hidden_pre = product(normed_two, w_fc) + b_fc.astype(jnp.float32)
    hidden_act = jax.nn.gelu(hidden_pre).astype(jnp.bfloat16)
    block_out = middle + product(hidden_act, w_proj) + b_proj.astype(jnp.float32)
    return (
        block_out,
        normed_one,
        queries,
        kv_all,
        query_pos,
        seq_length,
        first_valid,
        attn_heads,
        log_total,
        mixed,
        middle,
        normed_two,
        hidden_pre,
        hidden_act,
    )


def backward(saved, weight_set, block_input, out_grad):
    (
        _,
        normed_one,
        queries,
        kv_all,
        query_pos,
        seq_length,
        first_valid,
        attn_heads,
        log_total,
        mixed,
        middle,
        normed_two,
        hidden_pre,
        hidden_act,
    ) = saved
    (ln1_gain, ln1_bias, w_qkv, _, w_out, _, ln2_gain, ln2_bias, w_fc, _, w_proj, _) = weight_set
    row_total = block_input.shape[0]
    grad_out = out_grad.astype(jnp.float32)
    grad_w_proj = product_tn(hidden_act, out_grad)
    grad_b_proj = jnp.sum(grad_out, axis=0)
    grad_act = product_nt(out_grad, w_proj)
    unused, gelu_pull = jax.vjp(jax.nn.gelu, hidden_pre)
    grad_pre = gelu_pull(grad_act)[0].astype(jnp.bfloat16)
    grad_w_fc = product_tn(normed_two, grad_pre)
    grad_b_fc = jnp.sum(grad_pre.astype(jnp.float32), axis=0)
    unused, norm_pull_two = jax.vjp(
        layer_norm, middle, ln2_gain.astype(jnp.float32), ln2_bias.astype(jnp.float32)
    )
    grad_mid_norm, grad_ln2_gain, grad_ln2_bias = norm_pull_two(product_nt(grad_pre, w_fc))
    grad_middle = grad_out + grad_mid_norm
    grad_mid_low = grad_middle.astype(jnp.bfloat16)
    grad_w_out = product_tn(mixed, grad_mid_low)
    grad_b_out = jnp.sum(grad_mid_low.astype(jnp.float32), axis=0)
    grad_heads = product_nt(grad_mid_low, w_out).astype(jnp.bfloat16).reshape(row_total, HEADS, HD)
    grad_q, kv_grads = attend_back(
        queries, kv_all, query_pos, seq_length, first_valid, log_total, attn_heads, grad_heads
    )
    kv_mine = lax.psum_scatter(
        kv_grads.astype(jnp.bfloat16), "fsdp", scatter_dimension=0, tiled=True
    ).astype(jnp.float32)
    grad_proj = jnp.concatenate([grad_q.reshape(row_total, D), kv_mine], axis=1).astype(
        jnp.bfloat16
    )
    grad_w_qkv = product_tn(normed_one, grad_proj)
    grad_b_qkv = jnp.sum(grad_proj.astype(jnp.float32), axis=0)
    unused, norm_pull_one = jax.vjp(
        layer_norm,
        block_input.astype(jnp.float32),
        ln1_gain.astype(jnp.float32),
        ln1_bias.astype(jnp.float32),
    )
    grad_in_norm, grad_ln1_gain, grad_ln1_bias = norm_pull_one(product_nt(grad_proj, w_qkv))
    input_grad = grad_middle + grad_in_norm
    grad_set = (
        grad_ln1_gain,
        grad_ln1_bias,
        grad_w_qkv,
        grad_b_qkv,
        grad_w_out,
        grad_b_out,
        grad_ln2_gain,
        grad_ln2_bias,
        grad_w_fc,
        grad_b_fc,
        grad_w_proj,
        grad_b_proj,
    )
    return (input_grad, grad_set)


def on_device_generic(
    block_input,
    seq_long,
    ln1_gain,
    ln1_bias,
    w_qkv,
    b_qkv,
    w_out,
    b_out,
    ln2_gain,
    ln2_bias,
    w_fc,
    b_fc,
    w_proj,
    b_proj,
    out_grad,
):
    long_flag = seq_long[0]
    fsdp_index = lax.axis_index("fsdp")
    weight_set = (
        lax.all_gather(ln1_gain, ("dp", "fsdp"), axis=0, tiled=True),
        lax.all_gather(ln1_bias, ("dp", "fsdp"), axis=0, tiled=True),
        lax.all_gather(w_qkv, ("dp", "fsdp"), axis=0, tiled=True),
        lax.all_gather(b_qkv, ("dp", "fsdp"), axis=0, tiled=True),
        lax.all_gather(w_out, ("dp", "fsdp"), axis=0, tiled=True),
        lax.all_gather(b_out, ("dp", "fsdp"), axis=0, tiled=True),
        lax.all_gather(ln2_gain, ("dp", "fsdp"), axis=0, tiled=True),
        lax.all_gather(ln2_bias, ("dp", "fsdp"), axis=0, tiled=True),
        lax.all_gather(w_fc, ("dp", "fsdp"), axis=0, tiled=True),
        lax.all_gather(b_fc, ("dp", "fsdp"), axis=0, tiled=True),
        lax.all_gather(w_proj, ("dp", "fsdp"), axis=0, tiled=True),
        lax.all_gather(b_proj, ("dp", "fsdp"), axis=0, tiled=True),
    )
    saved = forward(block_input, weight_set, long_flag, fsdp_index, gather_first)
    block_output = saved[0].astype(jnp.bfloat16)
    weight_set = (
        lax.all_gather(ln1_gain, ("dp", "fsdp"), axis=0, tiled=True),
        lax.all_gather(ln1_bias, ("dp", "fsdp"), axis=0, tiled=True),
        lax.all_gather(w_qkv, ("dp", "fsdp"), axis=0, tiled=True),
        lax.all_gather(b_qkv, ("dp", "fsdp"), axis=0, tiled=True),
        lax.all_gather(w_out, ("dp", "fsdp"), axis=0, tiled=True),
        lax.all_gather(b_out, ("dp", "fsdp"), axis=0, tiled=True),
        lax.all_gather(ln2_gain, ("dp", "fsdp"), axis=0, tiled=True),
        lax.all_gather(ln2_bias, ("dp", "fsdp"), axis=0, tiled=True),
        lax.all_gather(w_fc, ("dp", "fsdp"), axis=0, tiled=True),
        lax.all_gather(b_fc, ("dp", "fsdp"), axis=0, tiled=True),
        lax.all_gather(w_proj, ("dp", "fsdp"), axis=0, tiled=True),
        lax.all_gather(b_proj, ("dp", "fsdp"), axis=0, tiled=True),
    )
    saved = forward(block_input, weight_set, long_flag, fsdp_index, gather_second)
    input_grad, grad_set = backward(saved, weight_set, block_input, out_grad)
    grad_shards = (
        lax.psum_scatter(grad_set[0], ("dp", "fsdp"), scatter_dimension=0, tiled=True),
        lax.psum_scatter(grad_set[1], ("dp", "fsdp"), scatter_dimension=0, tiled=True),
        lax.psum_scatter(grad_set[2], ("dp", "fsdp"), scatter_dimension=0, tiled=True),
        lax.psum_scatter(grad_set[3], ("dp", "fsdp"), scatter_dimension=0, tiled=True),
        lax.psum_scatter(grad_set[4], ("dp", "fsdp"), scatter_dimension=0, tiled=True),
        lax.psum_scatter(grad_set[5], ("dp", "fsdp"), scatter_dimension=0, tiled=True),
        lax.psum_scatter(grad_set[6], ("dp", "fsdp"), scatter_dimension=0, tiled=True),
        lax.psum_scatter(grad_set[7], ("dp", "fsdp"), scatter_dimension=0, tiled=True),
        lax.psum_scatter(grad_set[8], ("dp", "fsdp"), scatter_dimension=0, tiled=True),
        lax.psum_scatter(grad_set[9], ("dp", "fsdp"), scatter_dimension=0, tiled=True),
        lax.psum_scatter(grad_set[10], ("dp", "fsdp"), scatter_dimension=0, tiled=True),
        lax.psum_scatter(grad_set[11], ("dp", "fsdp"), scatter_dimension=0, tiled=True),
    )
    return (block_output, input_grad) + tuple(grad_shards)


def nt(a, b):
    return lax.dot_general(a, b, (((1,), (1,)), ((), ())), preferred_element_type=f32)


def nn(a, b):
    return jnp.dot(a, b, preferred_element_type=f32)


PAIR = 2 * HD


def busy(microseconds):
    return pl.CostEstimate(
        flops=int(microseconds * 1.15e9), bytes_accessed=int(microseconds * 1e6), transcendentals=0
    )


def split_heads(pair):
    left = lax.broadcasted_iota(jnp.int32, pair.shape, 1) < HD
    zero = jnp.zeros_like(pair)
    return (jnp.where(left, pair, zero), jnp.where(left, zero, pair))


def up_to(keys, queries):
    return lax.broadcasted_iota(jnp.int32, (keys, queries), 0) <= lax.broadcasted_iota(
        jnp.int32, (keys, queries), 1
    )


def attend_fwd_kernel(block, strips, flag_ref, q_ref, k_ref, v_ref, o_ref, lse_ref, vt_ref):
    i = pl.program_id(0)
    part = block // strips

    @pl.when(i == 0)
    def _():
        vt_ref[...] = v_ref[...].astype(f32).T.astype(bf)

    per_seq = jnp.where(flag_ref[0] == 1, 2 * SEQ, SEQ) // block
    first = i // per_seq * per_seq
    q_heads = split_heads(q_ref[...])

    def update(state, h, start, keys, low, mask):
        start = pl.multiple_of(start, part)
        s = nt(k_ref[pl.ds(start, keys), :], q_heads[h][low:, :])
        x = s * s + 1.0
        mag = x * lax.rsqrt(x)
        if mask is not None:
            mag = jnp.where(mask, mag, FAR)
        top = jnp.max(mag, axis=0, keepdims=True)
        if state is not None:
            old_top, old_sum, old_acc = state
            top = jnp.maximum(top, old_top)
        e = jnp.exp(mag - top)
        fresh = jnp.sum(e, axis=0, keepdims=True)
        w = (jnp.tanh(s) * e).astype(bf)
        acc = nn(vt_ref[h * HD : (h + 1) * HD, pl.ds(start, keys)], w)
        if state is not None:
            alpha = jnp.exp(old_top - top)
            fresh = fresh + alpha * old_sum
            acc = acc + alpha * old_acc
        return (top, fresh, acc)

    base = i * block
    states = []
    for h in range(2):
        state = update(None, h, base, part, 0, up_to(part, block))
        for m in range(1, strips):
            low = m * part
            tail = update(
                tuple(item[:, low:] for item in state),
                h,
                base + low,
                part,
                low,
                up_to(part, block - low),
            )
            state = tuple(
                jnp.concatenate([a[:, :low], b], axis=1) for a, b in zip(state, tail)
            )
        states.append(state)
    states = lax.fori_loop(
        first,
        i,
        lambda j, st: tuple(update(st[h], h, j * block, block, 0, None) for h in range(2)),
        tuple(states),
    )
    for h in range(2):
        top, total, _ = states[h]
        lse_ref[h : h + 1, :] = top + jnp.log(total)
    both = jnp.concatenate([states[h][2] / states[h][1] for h in range(2)], axis=0)
    o_ref[...] = both.T.astype(bf)


def attend_fwd(flag, projected, pair, block=1024, strips=4):
    rows = projected.shape[0]
    full = lambda c: pl.BlockSpec((rows, PAIR), lambda i, f: (0, 3 * pair + c))
    return pl.pallas_call(
        functools.partial(attend_fwd_kernel, block, strips),
        grid_spec=pltpu.PrefetchScalarGridSpec(
            num_scalar_prefetch=1,
            grid=(rows // block,),
            in_specs=[pl.BlockSpec((block, PAIR), lambda i, f: (i, 3 * pair)), full(1), full(2)],
            out_specs=[
                pl.BlockSpec((block, PAIR), lambda i, f: (i, 0)),
                pl.BlockSpec((8, block), lambda i, f: (0, i)),
            ],
            scratch_shapes=[pltpu.VMEM((PAIR, rows), bf)],
        ),
        out_shape=[
            jax.ShapeDtypeStruct((rows, PAIR), bf),
            jax.ShapeDtypeStruct((8, rows), f32),
        ],
        cost_estimate=busy(16),
        name="attend_fwd",
    )(flag, projected, projected, projected)


def attend_bwd_kernel(
    block,
    strips,
    flag_ref,
    place_ref,
    q_ref,
    k_ref,
    v_ref,
    o_ref,
    keep_ref,
    other_ref,
    lse_ref,
    g_ref,
    dqt_ref,
    inner_ref,
    do_ref,
):
    j = pl.program_id(0)
    last = pl.num_programs(0) - 1
    rows = q_ref.shape[0]
    side_rows = rows // 2
    part = block // strips

    @pl.when(j == 0)
    def _():
        dqt_ref[...] = jnp.zeros_like(dqt_ref)
        on_left = place_ref[0] == 0
        do_ref[:side_rows, :] = jnp.where(on_left, keep_ref[...], other_ref[...])
        do_ref[side_rows:, :] = jnp.where(on_left, other_ref[...], keep_ref[...])
        prod = o_ref[...].astype(f32) * do_ref[...].astype(f32)
        head = lax.broadcasted_iota(jnp.int32, (8, PAIR), 0)
        lane = lax.broadcasted_iota(jnp.int32, (8, PAIR), 1)
        inner_ref[...] = lax.dot_general(
            (head == lane // HD).astype(f32),
            prod,
            (((1,), (1,)), ((), ())),
            precision=lax.Precision.HIGHEST,
            preferred_element_type=f32,
        )

    per_seq = jnp.where(flag_ref[0] == 1, 2 * SEQ, SEQ) // block
    stop = (j // per_seq + 1) * per_seq
    k_pair = k_ref[...]
    k_heads = split_heads(k_pair)
    v_heads = split_heads(v_ref[...])
    k_turned = k_pair.astype(f32).T.astype(bf)

    def update(state, low_key, keys, start, queries, mask):
        cols = pl.ds(pl.multiple_of(start, part), queries)
        q_pair = q_ref[cols, :]
        do_pair = do_ref[cols, :]
        q_heads = split_heads(q_pair)
        do_heads = split_heads(do_pair)
        key_rows = slice(low_key, low_key + keys)
        dk, dv = (None, None) if state is None else state
        for h in range(2):
            head_rows = slice(h * HD, (h + 1) * HD)
            s = nt(k_heads[h][key_rows], q_pair)
            x = s * s + 1.0
            r = lax.rsqrt(x)
            e = jnp.exp(x * r - lse_ref[h : h + 1, cols])
            if mask is not None:
                e = jnp.where(mask, e, 0.0)
            t = jnp.tanh(s)
            slope = s * r
            w = (t * e).astype(bf)
            gw = nt(v_heads[h][key_rows], do_pair)
            ds = (
                e * (gw * (1.0 + t * (slope - t)) - slope * inner_ref[h : h + 1, cols])
            ).astype(bf)
            dv_part = nn(w, do_heads[h])
            dk_part = nn(ds, q_heads[h])
            dv = dv_part if dv is None else dv + dv_part
            dk = dk_part if dk is None else dk + dk_part
            dqt_ref[head_rows, cols] += nn(k_turned[head_rows, key_rows], ds)
        return (dk, dv)

    base = j * block
    strip_grads = [
        update(None, m * part, part, base + m * part, block - m * part, up_to(part, block - m * part))
        for m in range(strips)
    ]
    state = tuple(jnp.concatenate(items, axis=0) for items in zip(*strip_grads))
    dk, dv = lax.fori_loop(
        j + 1, stop, lambda i, st: update(st, 0, block, i * block, block, None), state
    )
    mine = pl.ds(pl.multiple_of(base, block), block)
    g_ref[mine, PAIR : 2 * PAIR] = dk.astype(bf)
    g_ref[mine, 2 * PAIR :] = dv.astype(bf)

    @pl.when(j == last)
    def _():
        g_ref[:, :PAIR] = (dqt_ref[...] * HD**-0.5).T.astype(bf)


def attend_bwd(flag, place, projected, pair, heads_out, keep, other, lse, block=1024, strips=4):
    rows = projected.shape[0]
    fixed = lambda r: pl.BlockSpec((r, PAIR), lambda j, f, s: (0, 0))
    part = lambda c: pl.BlockSpec((block, PAIR), lambda j, f, s: (j, 3 * pair + c))
    return pl.pallas_call(
        functools.partial(attend_bwd_kernel, block, strips),
        grid_spec=pltpu.PrefetchScalarGridSpec(
            num_scalar_prefetch=2,
            grid=(rows // block,),
            in_specs=[
                pl.BlockSpec((rows, PAIR), lambda j, f, s: (0, 3 * pair)),
                part(1),
                part(2),
                fixed(rows),
                fixed(rows // 2),
                fixed(rows // 2),
                pl.BlockSpec((8, rows), lambda j, f, s: (0, 0)),
            ],
            out_specs=pl.BlockSpec((rows, 3 * PAIR), lambda j, f, s: (0, 0)),
            scratch_shapes=[
                pltpu.VMEM((PAIR, rows), f32),
                pltpu.VMEM((8, rows), f32),
                pltpu.VMEM((rows, PAIR), bf),
            ],
        ),
        out_shape=jax.ShapeDtypeStruct((rows, 3 * PAIR), bf),
        cost_estimate=busy(25),
        name="attend_bwd",
    )(flag, place, projected, projected, projected, heads_out, keep, other, lse)


def tn(a, b):
    return lax.dot_general(a, b, (((0,), (0,)), ((), ())), preferred_element_type=f32)


def norm_stats(rows_in):
    mean = jnp.mean(rows_in, axis=-1, keepdims=True)
    centred = rows_in - mean
    variance = jnp.mean(centred * centred, axis=-1, keepdims=True)
    scale = lax.rsqrt(variance + EPS)
    return centred * scale, scale


def project_kernel(place_ref, own_ref, other_ref, gain_ref, bias_ref, w_ref, b_ref, n_ref, p_ref):
    per_side = pl.num_programs(0) // 2
    is_own = pl.program_id(0) // per_side == place_ref[0]
    rows = jnp.where(is_own, own_ref[...], other_ref[...]).astype(f32)
    unit, _ = norm_stats(rows)
    normed = (unit * gain_ref[...] + bias_ref[...]).astype(bf)
    n_ref[...] = normed
    for c in range(0, p_ref.shape[1], 3 * PAIR):
        cols = slice(c, c + 3 * PAIR)
        part = (nn(normed, w_ref[:, cols]) + b_ref[:, cols]).astype(bf)
        p_ref[:, c : c + PAIR] = part[:, :PAIR] * jnp.asarray(HD**-0.5, bf)
        p_ref[:, c + PAIR : c + 3 * PAIR] = part[:, PAIR:]


def project(place, own, other, gain, bias, weight, w_bias, block=256):
    rows, width = own.shape
    per_side = rows // block
    cols = weight.shape[1]
    fixed = lambda shape: pl.BlockSpec(shape, lambda i, s: (0, 0))
    return pl.pallas_call(
        project_kernel,
        grid_spec=pltpu.PrefetchScalarGridSpec(
            num_scalar_prefetch=1,
            grid=(2 * per_side,),
            in_specs=[
                pl.BlockSpec(
                    (block, width), lambda i, s: (jnp.clip(i - s[0] * per_side, 0, per_side - 1), 0)
                ),
                pl.BlockSpec(
                    (block, width),
                    lambda i, s: (jnp.clip(i - (1 - s[0]) * per_side, 0, per_side - 1), 0),
                ),
                fixed((1, width)),
                fixed((1, width)),
                fixed(weight.shape),
                fixed((1, cols)),
            ],
            out_specs=[
                pl.BlockSpec((block, width), lambda i, s: (i, 0)),
                pl.BlockSpec((block, cols), lambda i, s: (i, 0)),
            ],
        ),
        out_shape=[
            jax.ShapeDtypeStruct((2 * rows, width), bf),
            jax.ShapeDtypeStruct((2 * rows, cols), bf),
        ],
        cost_estimate=busy(11),
        name="norm_project",
    )(place, own, other, gain, bias, weight, w_bias)


GELU_C = math.sqrt(2 / math.pi)


def mlp_kernel(
    place_ref,
    g_hbm,
    x_ref,
    og_ref,
    ha0_ref,
    ha1_ref,
    ha2_ref,
    hb0_ref,
    hb1_ref,
    hb2_ref,
    bout_ref,
    gain_ref,
    bias_ref,
    bfc_ref,
    bproj_ref,
    out_ref,
    mixed_ref,
    n2_ref,
    act_ref,
    gp_ref,
    gm_ref,
    gml_ref,
    keep0_ref,
    keep1_ref,
    keep2_ref,
    send0_ref,
    send1_ref,
    send2_ref,
    sums_ref,
    w_ref,
    sem,
):
    i = pl.program_id(0)
    devices = g_hbm.shape[0]
    sub = g_hbm.shape[2]
    width = devices * sub
    chunks = (g_hbm.shape[1] - 1) // 2

    def load(slot):
        return pltpu.make_async_copy(g_hbm.at[:, slot], w_ref.at[slot], sem.at[slot])

    order = [2 * chunks] + list(range(chunks, 2 * chunks))

    def load_proj():
        return pltpu.make_async_copy(
            g_hbm.at[:, pl.ds(0, chunks)], wp_view(), sem.at[0]
        )

    def wp_view():
        return w_ref.at[pl.ds(0, chunks)].reshape(devices, chunks, sub, width)

    @pl.when(i == 0)
    def _():
        for slot in order:
            load(slot).start()
        load_proj().start()
        for slot in order:
            load(slot).wait()
        load_proj().wait()
        sums_ref[...] = jnp.zeros_like(sums_ref)

    def weight(slot):
        return w_ref[slot].reshape(width, width)

    on_left = place_ref[0] == 0
    ha = jnp.concatenate([ha0_ref[...], ha1_ref[...], ha2_ref[...]], axis=1)
    hb = jnp.concatenate([hb0_ref[...], hb1_ref[...], hb2_ref[...]], axis=1)
    mixed = jnp.concatenate([jnp.where(on_left, ha, hb), jnp.where(on_left, hb, ha)], axis=1)
    mixed_ref[...] = mixed
    og_low = og_ref[...]
    og = og_low.astype(f32)
    middle = x_ref[...].astype(f32) + nn(mixed, weight(2 * chunks)) + bout_ref[...]
    unit, scale = norm_stats(middle)
    n2 = (unit * gain_ref[...] + bias_ref[...]).astype(bf)
    n2_ref[...] = n2
    out = middle + bproj_ref[...]
    e = jnp.zeros_like(middle)
    for c in range(chunks):
        cols = slice(c * width, (c + 1) * width)
        w_fc = weight(chunks + c)
        w_proj = weight(c)
        pre = nn(n2, w_fc) + bfc_ref[:, cols]
        square = pre * pre
        t = jnp.tanh(GELU_C * pre * (1.0 + 0.044715 * square))
        low_half = 0.5 * (1.0 + t)
        act = (pre * low_half).astype(bf)
        act_ref[:, cols] = act
        out = out + nn(act, w_proj)
        slope = low_half + 0.5 * pre * (1.0 - t * t) * (
            GELU_C * (1.0 + 3.0 * 0.044715 * square)
        )
        gp = (nt(og_low, w_proj) * slope).astype(bf)
        gp_ref[:, cols] = gp
        sums_ref[0:1, cols] += jnp.sum(gp.astype(f32), axis=0, keepdims=True)
        e = e + nt(gp, w_fc)
    out_ref[...] = out.astype(bf)
    sums_ref[1:2, 0:width] += jnp.sum(og, axis=0, keepdims=True)
    sums_ref[1:2, width : 2 * width] += jnp.sum(e * unit, axis=0, keepdims=True)
    sums_ref[1:2, 2 * width : 3 * width] += jnp.sum(e, axis=0, keepdims=True)
    eg = e * gain_ref[...]
    gm = og + scale * (
        eg
        - jnp.mean(eg, axis=-1, keepdims=True)
        - unit * jnp.mean(eg * unit, axis=-1, keepdims=True)
    )
    gm_ref[...] = gm
    gml = gm.astype(bf)
    gml_ref[...] = gml
    sums_ref[1:2, 3 * width : 4 * width] += jnp.sum(gml.astype(f32), axis=0, keepdims=True)
    gh = nt(gml, weight(2 * chunks)).astype(bf)
    half = width // 2
    left = gh[:, :half]
    right = gh[:, half:]
    for p, (keep_ref, send_ref) in enumerate(
        ((keep0_ref, send0_ref), (keep1_ref, send1_ref), (keep2_ref, send2_ref))
    ):
        cols = slice(p * PAIR, (p + 1) * PAIR)
        keep_ref[...] = jnp.where(on_left, left[:, cols], right[:, cols])
        send_ref[...] = jnp.where(on_left, right[:, cols], left[:, cols])


def mlp(place, gathered, x, og, heads_mine, heads_other, b_out, gain, bias, b_fc, b_proj, block=256):
    rows, width = x.shape
    steps = rows // block
    hidden = b_fc.shape[1]
    row = lambda cols: pl.BlockSpec((block, cols), lambda i, s: (i, 0))
    fixed = lambda cols: pl.BlockSpec((1, cols), lambda i, s: (0, 0))
    shape = lambda cols, kind: jax.ShapeDtypeStruct((rows, cols), kind)
    return pl.pallas_call(
        mlp_kernel,
        grid_spec=pltpu.PrefetchScalarGridSpec(
            num_scalar_prefetch=1,
            grid=(steps,),
            in_specs=[
                pl.BlockSpec(memory_space=pl.ANY),
                row(width),
                row(width),
                *[pl.BlockSpec((block, PAIR), lambda i, s: (s[0] * steps + i, 0))] * 3,
                *[row(PAIR)] * 3,
                fixed(width),
                fixed(width),
                fixed(width),
                fixed(hidden),
                fixed(width),
            ],
            out_specs=[
                row(width),
                row(width),
                row(width),
                row(hidden),
                row(hidden),
                row(width),
                row(width),
                *[row(PAIR)] * 6,
                pl.BlockSpec((8, hidden), lambda i, s: (0, 0)),
            ],
            scratch_shapes=[
                pltpu.VMEM((gathered.shape[1], gathered.shape[0], gathered.shape[2], width), bf),
                pltpu.SemaphoreType.DMA((gathered.shape[1],)),
            ],
        ),
        out_shape=[
            shape(width, bf),
            shape(width, bf),
            shape(width, bf),
            shape(hidden, bf),
            shape(hidden, bf),
            shape(width, f32),
            shape(width, bf),
            *[shape(PAIR, bf)] * 6,
            jax.ShapeDtypeStruct((8, hidden), f32),
        ],
        compiler_params=pltpu.CompilerParams(vmem_limit_bytes=56 * 1024 * 1024),
        cost_estimate=busy(37),
        name="mlp",
    )(place, gathered, x, og, *heads_mine, *heads_other, b_out, gain, bias, b_fc, b_proj)


def weight_grad_kernel(act_ref, gp_ref, og_ref, n2_ref, mixed_ref, gml_ref, out_hbm, buf_ref, sem):
    c = pl.program_id(0)
    last = pl.num_programs(0) - 1
    devices, slots, sub, width = out_hbm.shape
    chunks = (slots - 1) // 2
    group = devices // chunks
    slot = lax.rem(c, 2)

    def proj_copy(step, where):
        return pltpu.make_async_copy(
            buf_ref.at[where].reshape(group, chunks, sub, width),
            out_hbm.at[pl.ds(step * group, group), pl.ds(0, chunks)],
            sem.at[where],
        )

    def other_copy(step, where):
        return pltpu.make_async_copy(buf_ref.at[where], out_hbm.at[:, step], sem.at[where])

    @pl.when(c >= 2)
    def _():
        other_copy(chunks, slot).wait()

    def put(value):
        buf_ref[slot] = value.astype(bf).reshape(devices, sub, width)

    @pl.when(c < chunks)
    def _():
        put(tn(act_ref[...], og_ref[...]))
        proj_copy(c, slot).start()

    @pl.when((c >= chunks) & (c < 2 * chunks))
    def _():
        put(tn(n2_ref[...], gp_ref[...]))
        other_copy(c, slot).start()

    @pl.when(c == last)
    def _():
        put(tn(mixed_ref[...], gml_ref[...]))
        other_copy(c, slot).start()
        other_copy(chunks, 1 - slot).wait()
        other_copy(chunks, slot).wait()


def weight_grads(act, gp, og, n2, mixed, gml, devices):
    rows, width = og.shape
    chunks = act.shape[1] // width
    slots = 2 * chunks + 1
    sub = width // devices
    fixed = pl.BlockSpec((rows, width), lambda c: (0, 0))
    return pl.pallas_call(
        weight_grad_kernel,
        grid=(slots,),
        in_specs=[
            pl.BlockSpec((rows, width), lambda c: (0, jnp.minimum(c, chunks - 1))),
            pl.BlockSpec((rows, width), lambda c: (0, jnp.clip(c - chunks, 0, chunks - 1))),
            fixed,
            fixed,
            fixed,
            fixed,
        ],
        out_specs=pl.BlockSpec(memory_space=pl.ANY),
        out_shape=jax.ShapeDtypeStruct((devices, slots, sub, width), bf),
        scratch_shapes=[
            pltpu.VMEM((2, devices, sub, width), bf),
            pltpu.SemaphoreType.DMA((2,)),
        ],
        cost_estimate=busy(19),
        name="weight_grads",
    )(act, gp, og, n2, mixed, gml)


def norm_sums_kernel(
    place_ref,
    own_ref,
    other_ref,
    g0_ref,
    g1_ref,
    g2_ref,
    r0_ref,
    r1_ref,
    w_ref,
    wo_ref,
    e_ref,
    sums_ref,
    bias_ref,
):
    i = pl.program_id(0)
    per_side = pl.num_programs(0) // 2
    is_own = i // per_side == place_ref[0]

    @pl.when(i == 0)
    def _():
        sums_ref[...] = jnp.zeros_like(sums_ref)
        bias_ref[...] = jnp.zeros_like(bias_ref)

    unit, _ = norm_stats(jnp.where(is_own, own_ref[...], other_ref[...]).astype(f32))
    wide = 3 * PAIR
    e = None
    for p, g_ref in enumerate((g0_ref, g1_ref, g2_ref)):
        cols = slice(p * wide, (p + 1) * wide)
        g = g_ref[...]
        part = nt(g, w_ref[:, cols])
        e = part if e is None else e + part
        bias_ref[0:1, cols] += jnp.sum(g.astype(f32), axis=0, keepdims=True)
    sums_ref[0:1, :] += jnp.sum(e * unit, axis=0, keepdims=True)
    sums_ref[1:2, :] += jnp.sum(e, axis=0, keepdims=True)

    @pl.when(is_own)
    def _():
        total = e
        for p, r_ref in enumerate((r0_ref, r1_ref)):
            total = total + nt(r_ref[...], wo_ref[:, p * wide : (p + 1) * wide])
        e_ref[...] = total


def norm_sums(place, own, other, grads, received, weight, weight_other, block=256):
    rows, width = own.shape
    per_side = rows // block
    cols = weight.shape[1]
    mine = lambda i, s: (jnp.clip(i - s[0] * per_side, 0, per_side - 1), 0)
    theirs = lambda i, s: (jnp.clip(i - (1 - s[0]) * per_side, 0, per_side - 1), 0)
    fixed = lambda shape: pl.BlockSpec(shape, lambda i, s: (0, 0))
    return pl.pallas_call(
        norm_sums_kernel,
        grid_spec=pltpu.PrefetchScalarGridSpec(
            num_scalar_prefetch=1,
            grid=(2 * per_side,),
            in_specs=[
                pl.BlockSpec((block, width), mine),
                pl.BlockSpec((block, width), theirs),
                *[pl.BlockSpec((block, 3 * PAIR), lambda i, s: (i, 0))] * 3,
                *[pl.BlockSpec((block, 3 * PAIR), mine)] * 2,
                fixed(weight.shape),
                fixed(weight.shape),
            ],
            out_specs=[pl.BlockSpec((block, width), mine), fixed((8, width)), fixed((8, cols))],
        ),
        out_shape=[
            jax.ShapeDtypeStruct((rows, width), f32),
            jax.ShapeDtypeStruct((8, width), f32),
            jax.ShapeDtypeStruct((8, cols), f32),
        ],
        cost_estimate=busy(13),
        name="norm_sums",
    )(place, own, other, *grads, *received, weight, weight_other)


def finish_kernel(x_ref, gm_ref, e_ref, r_ref, wo_ref, gain_ref, out_ref):
    unit, scale = norm_stats(x_ref[...].astype(f32))
    eg = (e_ref[...] + nt(r_ref[...], wo_ref[...])) * gain_ref[...]
    out_ref[...] = gm_ref[...] + scale * (
        eg
        - jnp.mean(eg, axis=-1, keepdims=True)
        - unit * jnp.mean(eg * unit, axis=-1, keepdims=True)
    )


def finish(x, grad_middle, e, received, weight_other, gain, block=256):
    rows, width = x.shape
    row = lambda cols: pl.BlockSpec((block, cols), lambda i: (i, 0))
    last = weight_other.shape[1] // (3 * PAIR) - 1
    return pl.pallas_call(
        finish_kernel,
        grid=(rows // block,),
        in_specs=[
            row(width),
            row(width),
            row(width),
            row(3 * PAIR),
            pl.BlockSpec((width, 3 * PAIR), lambda i: (0, last)),
            pl.BlockSpec((1, width), lambda i: (0, 0)),
        ],
        out_specs=row(width),
        out_shape=jax.ShapeDtypeStruct((rows, width), f32),
        cost_estimate=busy(6),
        name="finish",
    )(x, grad_middle, e, received, weight_other, gain)


AXES = ("dp", "fsdp")


def swap(value, bit, total):
    return lax.ppermute(value, AXES, [(i, i ^ bit) for i in range(total)])


def gather_dp(shard, dp_size, order):
    me = lax.axis_index("dp")
    bits = dp_size.bit_length() - 1
    held = shard.reshape((1,) * bits + shard.shape)
    for bit in order:
        other = swap(held, 2 << bit, 2 * dp_size)
        low = (me >> bit) & 1 == 0
        held = jnp.concatenate(
            [jnp.where(low, held, other), jnp.where(low, other, held)], axis=bits - 1 - bit
        )
    return held.reshape((dp_size * shard.shape[0],) + shard.shape[1:])


def scatter_dp(whole, dp_size, order):
    me = lax.axis_index("dp")
    bits = dp_size.bit_length() - 1
    rows = whole.shape[0] // dp_size
    held = whole.reshape((2,) * bits + (rows,) + whole.shape[1:])
    for bit in order:
        axis = bits - 1 - bit
        low = (me >> bit) & 1 == 0
        first = lax.slice_in_dim(held, 0, 1, axis=axis)
        second = lax.slice_in_dim(held, 1, 2, axis=axis)
        mine = jnp.where(low, first, second)
        sent = jnp.where(low, second, first).astype(bf)
        held = mine.astype(f32) + swap(sent, 2 << bit, 2 * dp_size).astype(
            f32
        )
    return held.reshape((rows,) + whole.shape[1:])


def sum_all(vector, total):
    bits = [1 << b for b in range(total.bit_length() - 1)]
    for bit in bits[1:] + bits[:1]:
        vector = vector + swap(vector, bit, total)
    return vector


def on_device_pair(
    dp_size,
    block_input,
    seq_long,
    ln1_gain,
    ln1_bias,
    w_qkv,
    b_qkv,
    w_out,
    b_out,
    ln2_gain,
    ln2_bias,
    w_fc,
    b_fc,
    w_proj,
    b_proj,
    out_grad,
):
    total = 2 * dp_size
    side = lax.axis_index("fsdp")
    flat = lax.axis_index("dp") * 2 + side
    on_left = side == 0
    row_total = block_input.shape[0]
    half = D // 2
    dp_bits = list(range(dp_size.bit_length() - 1))
    gather_order = dp_bits[1:2] + dp_bits[:1:-1] + dp_bits[:1]
    scatter_order = dp_bits[:1] + dp_bits[2:] + dp_bits[1:2]

    def ordered(mine, other, axis):
        return jnp.concatenate(
            [jnp.where(on_left, mine, other), jnp.where(on_left, other, mine)], axis=axis
        )

    pairs = half // PAIR

    def head_columns(rows_in, which):
        split = rows_in.reshape(rows_in.shape[0], 3, 2, pairs, PAIR)
        mine = lax.dynamic_index_in_dim(split, which, 2, keepdims=False)
        return jnp.transpose(mine, (0, 2, 1, 3)).reshape(rows_in.shape[0], 3 * half)

    def rows_of(whole, which):
        return lax.dynamic_slice_in_dim(whole, which * row_total, row_total, axis=0)

    small = (ln1_gain, ln1_bias, b_qkv, b_out, ln2_gain, ln2_bias, b_fc, b_proj)
    placed = jnp.concatenate(
        [
            lax.dynamic_update_slice(
                jnp.zeros((item.shape[0] * total,), bf), item, (item.shape[0] * flat,)
            )
            for item in small
        ]
    )
    gathered = sum_all(placed, total).astype(f32)
    pieces = []
    start = 0
    for item in small:
        pieces.append(gathered[start : start + item.shape[0] * total])
        start += item.shape[0] * total
    ln1_gain, ln1_bias, b_qkv, b_out, ln2_gain, ln2_bias, b_fc, b_proj = pieces

    other_input = swap(block_input, 1, total)
    received = swap(head_columns(w_qkv, 1 - side), 1, total)
    w_mine = gather_dp(ordered(head_columns(w_qkv, side), received, 0), dp_size, gather_order)
    w_other = swap(w_mine, 1, total)

    sub = w_out.shape[0]
    chunks = FF // D
    packed = jnp.concatenate(
        [w_proj] + [w_fc[:, c * D : (c + 1) * D] for c in range(chunks)] + [w_out], axis=0
    )
    gathered_w = lax.all_gather(packed, AXES, axis=0, tiled=True)
    gathered_w = gathered_w.reshape(total, 2 * chunks + 1, sub, D)

    def as_row(vector):
        return vector.reshape(1, -1)

    place = side.astype(jnp.int32).reshape(1)
    b_mine = head_columns(as_row(b_qkv), side)
    normed_one, projected = project(
        place, block_input, other_input, as_row(ln1_gain), as_row(ln1_bias), w_mine, b_mine
    )
    heads_mine = []
    heads_other = []
    log_totals = []
    for p in range(pairs):
        heads, log_total = attend_fwd(seq_long, projected, p)
        heads_mine.append(heads)
        log_totals.append(log_total)
        heads_other.append(swap(rows_of(heads, 1 - side), 1, total))
    (
        block_output,
        mixed,
        normed_two,
        hidden_act,
        grad_pre,
        grad_middle,
        grad_mid_low,
        *rest,
    ) = mlp(
        place,
        gathered_w,
        block_input,
        out_grad,
        heads_mine,
        heads_other,
        as_row(b_out),
        as_row(ln2_gain),
        as_row(ln2_bias),
        as_row(b_fc),
        as_row(b_proj),
    )
    grad_keep = rest[:pairs]
    grad_other = [swap(item, 1, total) for item in rest[pairs : 2 * pairs]]
    sums = rest[2 * pairs]
    packed_grads = weight_grads(
        hidden_act, grad_pre, out_grad, normed_two, mixed, grad_mid_low, total
    )
    shard = lax.psum_scatter(
        packed_grads.reshape(total * (2 * chunks + 1) * sub, D),
        AXES,
        scatter_dimension=0,
        tiled=True,
    ).astype(f32)
    shard_w_proj = shard[: chunks * sub]
    shard_w_fc = jnp.concatenate(
        [shard[(chunks + c) * sub : (chunks + c + 1) * sub] for c in range(chunks)], axis=1
    )
    shard_w_out = shard[2 * chunks * sub :]
    grad_b_fc = sums[0]
    grad_b_proj, grad_ln2_gain, grad_ln2_bias, grad_b_out = (
        sums[1, k * D : (k + 1) * D] for k in range(4)
    )
    grads = []
    grads_other = []
    shards = []
    for p in range(pairs):
        grad_pair = attend_bwd(
            seq_long,
            place,
            projected,
            p,
            heads_mine[p],
            grad_keep[p],
            grad_other[p],
            log_totals[p],
        )
        grads.append(grad_pair)
        grads_other.append(swap(rows_of(grad_pair, 1 - side), 1, total))
        shards.append(scatter_dp(product_tn(normed_one, grad_pair), dp_size, scatter_order))

    e_partial, norm_one_sums, grad_b_mine = norm_sums(
        place, block_input, other_input, grads, grads_other[:-1], w_mine, w_other
    )
    input_grad = finish(
        block_input, grad_middle, e_partial, grads_other[-1], w_other, as_row(ln1_gain)
    )

    shard_rows = jnp.concatenate(shards, axis=1).reshape(2, -1, 3 * half)
    keep = lax.dynamic_index_in_dim(shard_rows, side, 0, keepdims=False)
    send = lax.dynamic_index_in_dim(shard_rows, 1 - side, 0, keepdims=False)
    taken = swap(send, 1, total)

    def by_part(rows_in):
        split = rows_in.reshape(rows_in.shape[0], pairs, 3, PAIR)
        return jnp.transpose(split, (0, 2, 1, 3)).reshape(rows_in.shape[0], 3, 1, half)

    shard_w_qkv = ordered(by_part(keep), by_part(taken), 2).reshape(-1, 3 * D)
    grad_b_part = by_part(grad_b_mine[0:1])
    grad_b_qkv = ordered(grad_b_part, jnp.zeros_like(grad_b_part), 2).reshape(3 * D)
    grad_vectors = (
        grad_b_out,
        grad_ln2_gain,
        grad_ln2_bias,
        grad_b_fc,
        grad_b_proj,
        norm_one_sums[0],
        norm_one_sums[1],
        grad_b_qkv,
    )
    summed = sum_all(jnp.concatenate(grad_vectors), total)
    begin = 0
    vector_shards = []
    for item in grad_vectors:
        size = item.shape[0] // total
        vector_shards.append(lax.dynamic_slice(summed, (begin + size * flat,), (size,)))
        begin += item.shape[0]
    (
        shard_b_out,
        shard_ln2_gain,
        shard_ln2_bias,
        shard_b_fc,
        shard_b_proj,
        shard_ln1_gain,
        shard_ln1_bias,
        shard_b_qkv,
    ) = vector_shards
    return (
        block_output,
        input_grad,
        shard_ln1_gain,
        shard_ln1_bias,
        shard_w_qkv,
        shard_b_qkv,
        shard_w_out,
        shard_b_out,
        shard_ln2_gain,
        shard_ln2_bias,
        shard_w_fc,
        shard_b_fc,
        shard_w_proj,
        shard_b_proj,
    )


def solution(mesh):
    in_specs = (
        P(("dp", "fsdp"), None),
        P("dp"),
        P(("dp", "fsdp")),
        P(("dp", "fsdp")),
        P(("dp", "fsdp"), None),
        P(("dp", "fsdp")),
        P(("dp", "fsdp"), None),
        P(("dp", "fsdp")),
        P(("dp", "fsdp")),
        P(("dp", "fsdp")),
        P(("dp", "fsdp"), None),
        P(("dp", "fsdp")),
        P(("dp", "fsdp"), None),
        P(("dp", "fsdp")),
        P(("dp", "fsdp"), None),
    )
    out_specs = (
        P(("dp", "fsdp"), None),
        P(("dp", "fsdp"), None),
        P(("dp", "fsdp")),
        P(("dp", "fsdp")),
        P(("dp", "fsdp"), None),
        P(("dp", "fsdp")),
        P(("dp", "fsdp"), None),
        P(("dp", "fsdp")),
        P(("dp", "fsdp")),
        P(("dp", "fsdp")),
        P(("dp", "fsdp"), None),
        P(("dp", "fsdp")),
        P(("dp", "fsdp"), None),
        P(("dp", "fsdp")),
    )
    whole_slice = dict(mesh=mesh, in_specs=in_specs, out_specs=out_specs, check_vma=False)
    dp_size = mesh.shape["dp"]
    if mesh.shape["fsdp"] != 2 or dp_size < 8 or dp_size & (dp_size - 1):
        return jax.shard_map(on_device_generic, **whole_slice)

    def on_device(*args):
        return on_device_pair(dp_size, *args)

    return jax.shard_map(on_device, **whole_slice)
```

```python
import functools
import math

import jax
import jax.numpy as jnp
from jax import lax
from jax.experimental import pallas as pl
from jax.experimental.pallas import tpu as pltpu
from jax.sharding import PartitionSpec as P


f32 = jnp.float32
bf = jnp.bfloat16

D = 768
HEADS = 12
HD = 64
FF = 3072
SEQ = 1024


EPS = 1e-05
FAR = -1e30
AXES = ("dp", "fsdp")


def layer_norm(rows_in, gain_vec, bias_vec):
    row_mean = jnp.mean(rows_in, axis=-1, keepdims=True)
    centred = rows_in - row_mean
    variance = jnp.mean(centred * centred, axis=-1, keepdims=True)
    return centred * lax.rsqrt(variance + EPS) * gain_vec + bias_vec


def product(left, right):
    return jnp.dot(left, right, preferred_element_type=jnp.float32)


def product_tn(left, right):
    return lax.dot_general(
        left, right, (((0,), (0,)), ((), ())), preferred_element_type=jnp.float32
    )


def product_nt(left, right):
    return lax.dot_general(
        left, right, (((1,), (1,)), ((), ())), preferred_element_type=jnp.float32
    )


def gather_first(kv_rows):
    return lax.all_gather(kv_rows, "fsdp", axis=0, tiled=True)


def gather_second(kv_rows):
    return lax.all_gather(kv_rows, "fsdp", axis=0, tiled=True)


def block_layout(kv_all):
    group_rows = kv_all.shape[0]
    key_block = math.gcd(group_rows, 512)
    block_count = group_rows // key_block
    kv_blocks = kv_all.reshape(block_count, key_block, 2, HEADS, HD)
    return (key_block, kv_blocks, jnp.arange(block_count, dtype=jnp.int32))


def block_allowed(query_pos, key_start, key_block, seq_length):
    key_pos = key_start + jnp.arange(key_block, dtype=jnp.int32)
    return (query_pos[:, None] // seq_length == key_pos[None, :] // seq_length) & (
        key_pos[None, :] <= query_pos[:, None]
    )


def block_useful(key_start, key_block, query_pos, first_valid):
    return (key_start <= query_pos[-1]) & (key_start + key_block - 1 >= first_valid)


def score_parts(queries, key_part):
    scores = jnp.einsum(
        "qhd,khd->hqk", queries, key_part, preferred_element_type=jnp.float32
    ) * HD ** (-0.5)
    return (scores, jnp.sqrt(scores * scores + 1.0))


def attend(queries, kv_all, query_pos, seq_length, first_valid):
    key_block, kv_blocks, block_ids = block_layout(kv_all)
    row_total = queries.shape[0]

    def stats_step(state_now, block_item):
        block_id, kv_part = block_item
        key_start = block_id * key_block

        def stats_compute(state_in):
            row_top, row_sum = state_in
            allowed = block_allowed(query_pos, key_start, key_block, seq_length)[None]
            _, magnitude = score_parts(queries, kv_part[:, 0])
            masked = jnp.where(allowed, magnitude, FAR)
            new_top = jnp.maximum(row_top, jnp.max(masked, axis=-1))
            fresh = jnp.sum(jnp.where(allowed, jnp.exp(masked - new_top[:, :, None]), 0.0), axis=-1)
            return (new_top, row_sum * jnp.exp(row_top - new_top) + fresh)

        useful = block_useful(key_start, key_block, query_pos, first_valid)
        return (lax.cond(useful, stats_compute, lambda kept_state: kept_state, state_now), None)

    start_state = (
        jnp.full((HEADS, row_total), FAR, jnp.float32),
        jnp.zeros((HEADS, row_total), jnp.float32),
    )
    (row_top, row_sum), unused = lax.scan(stats_step, start_state, (block_ids, kv_blocks))
    log_total = row_top + jnp.log(row_sum)

    def value_step(accum_now, block_item):
        block_id, kv_part = block_item
        key_start = block_id * key_block

        def value_compute(accum_in):
            allowed = block_allowed(query_pos, key_start, key_block, seq_length)[None]
            scores, magnitude = score_parts(queries, kv_part[:, 0])
            weights = jnp.where(
                allowed, jnp.tanh(scores) * jnp.exp(magnitude - log_total[:, :, None]), 0.0
            ).astype(jnp.bfloat16)
            return accum_in + jnp.einsum(
                "hqk,khd->qhd", weights, kv_part[:, 1], preferred_element_type=jnp.float32
            )

        useful = block_useful(key_start, key_block, query_pos, first_valid)
        return (lax.cond(useful, value_compute, lambda kept_accum: kept_accum, accum_now), None)

    start_accum = jnp.zeros((row_total, HEADS, HD), jnp.float32)
    attn_heads, unused = lax.scan(value_step, start_accum, (block_ids, kv_blocks))
    return (attn_heads, log_total)


def attend_back(
    queries, kv_all, query_pos, seq_length, first_valid, log_total, attn_heads, grad_heads
):
    key_block, kv_blocks, block_ids = block_layout(kv_all)
    row_total = queries.shape[0]
    inner = jnp.transpose(jnp.sum(grad_heads.astype(jnp.float32) * attn_heads, axis=-1))

    def grad_step(dq_now, block_item):
        block_id, kv_part = block_item
        key_start = block_id * key_block

        def grad_compute(dq_in):
            allowed = block_allowed(query_pos, key_start, key_block, seq_length)[None]
            scores, magnitude = score_parts(queries, kv_part[:, 0])
            expo = jnp.where(allowed, jnp.exp(magnitude - log_total[:, :, None]), 0.0)
            tangent = jnp.tanh(scores)
            weights = (tangent * expo).astype(jnp.bfloat16)
            grad_v = jnp.einsum(
                "hqk,qhd->khd", weights, grad_heads, preferred_element_type=jnp.float32
            )
            grad_weight = jnp.einsum(
                "qhd,khd->hqk", grad_heads, kv_part[:, 1], preferred_element_type=jnp.float32
            )
            slope = scores / magnitude
            grad_scores = (
                expo
                * (
                    grad_weight * (1.0 - tangent * tangent + tangent * slope)
                    - slope * inner[:, :, None]
                )
            ).astype(jnp.bfloat16)
            dq_out = dq_in + jnp.einsum(
                "hqk,khd->qhd", grad_scores, kv_part[:, 0], preferred_element_type=jnp.float32
            ) * HD ** (-0.5)
            grad_k = jnp.einsum(
                "hqk,qhd->khd", grad_scores, queries, preferred_element_type=jnp.float32
            ) * HD ** (-0.5)
            return (
                dq_out,
                jnp.concatenate(
                    [grad_k.reshape(key_block, D), grad_v.reshape(key_block, D)], axis=1
                ),
            )

        def skip_block(dq_in):
            return (dq_in, jnp.zeros((key_block, 2 * D), jnp.float32))

        useful = block_useful(key_start, key_block, query_pos, first_valid)
        return lax.cond(useful, grad_compute, skip_block, dq_now)

    start_dq = jnp.zeros((row_total, HEADS, HD), jnp.float32)
    grad_q, kv_grads = lax.scan(grad_step, start_dq, (block_ids, kv_blocks))
    return (grad_q, kv_grads.reshape(kv_all.shape[0], 2 * D))


def forward(block_input, weight_set, long_flag, fsdp_index, gather_keys):
    (
        ln1_gain,
        ln1_bias,
        w_qkv,
        b_qkv,
        w_out,
        b_out,
        ln2_gain,
        ln2_bias,
        w_fc,
        b_fc,
        w_proj,
        b_proj,
    ) = weight_set
    row_total = block_input.shape[0]
    wide_input = block_input.astype(jnp.float32)
    normed_one = layer_norm(
        wide_input, ln1_gain.astype(jnp.float32), ln1_bias.astype(jnp.float32)
    ).astype(jnp.bfloat16)
    projected = (product(normed_one, w_qkv) + b_qkv.astype(jnp.float32)).astype(jnp.bfloat16)
    queries = projected[:, :D].reshape(row_total, HEADS, HD)
    kv_all = gather_keys(projected[:, D:])
    seq_length = jnp.where(long_flag == 1, 2 * SEQ, SEQ).astype(jnp.int32)
    query_pos = fsdp_index * row_total + jnp.arange(row_total, dtype=jnp.int32)
    first_valid = query_pos[0] // seq_length * seq_length
    attn_heads, log_total = attend(queries, kv_all, query_pos, seq_length, first_valid)
    mixed = attn_heads.reshape(row_total, D).astype(jnp.bfloat16)
    middle = wide_input + product(mixed, w_out) + b_out.astype(jnp.float32)
    normed_two = layer_norm(
        middle, ln2_gain.astype(jnp.float32), ln2_bias.astype(jnp.float32)
    ).astype(jnp.bfloat16)
    hidden_pre = product(normed_two, w_fc) + b_fc.astype(jnp.float32)
    hidden_act = jax.nn.gelu(hidden_pre).astype(jnp.bfloat16)
    block_out = middle + product(hidden_act, w_proj) + b_proj.astype(jnp.float32)
    return (
        block_out,
        normed_one,
        queries,
        kv_all,
        query_pos,
        seq_length,
        first_valid,
        attn_heads,
        log_total,
        mixed,
        middle,
        normed_two,
        hidden_pre,
        hidden_act,
    )


def backward(saved, weight_set, block_input, out_grad):
    (
        _,
        normed_one,
        queries,
        kv_all,
        query_pos,
        seq_length,
        first_valid,
        attn_heads,
        log_total,
        mixed,
        middle,
        normed_two,
        hidden_pre,
        hidden_act,
    ) = saved
    (ln1_gain, ln1_bias, w_qkv, _, w_out, _, ln2_gain, ln2_bias, w_fc, _, w_proj, _) = weight_set
    row_total = block_input.shape[0]
    grad_out = out_grad.astype(jnp.float32)
    grad_w_proj = product_tn(hidden_act, out_grad)
    grad_b_proj = jnp.sum(grad_out, axis=0)
    grad_act = product_nt(out_grad, w_proj)
    unused, gelu_pull = jax.vjp(jax.nn.gelu, hidden_pre)
    grad_pre = gelu_pull(grad_act)[0].astype(jnp.bfloat16)
    grad_w_fc = product_tn(normed_two, grad_pre)
    grad_b_fc = jnp.sum(grad_pre.astype(jnp.float32), axis=0)
    unused, norm_pull_two = jax.vjp(
        layer_norm, middle, ln2_gain.astype(jnp.float32), ln2_bias.astype(jnp.float32)
    )
    grad_mid_norm, grad_ln2_gain, grad_ln2_bias = norm_pull_two(product_nt(grad_pre, w_fc))
    grad_middle = grad_out + grad_mid_norm
    grad_mid_low = grad_middle.astype(jnp.bfloat16)
    grad_w_out = product_tn(mixed, grad_mid_low)
    grad_b_out = jnp.sum(grad_mid_low.astype(jnp.float32), axis=0)
    grad_heads = product_nt(grad_mid_low, w_out).astype(jnp.bfloat16).reshape(row_total, HEADS, HD)
    grad_q, kv_grads = attend_back(
        queries, kv_all, query_pos, seq_length, first_valid, log_total, attn_heads, grad_heads
    )
    kv_mine = lax.psum_scatter(
        kv_grads.astype(jnp.bfloat16), "fsdp", scatter_dimension=0, tiled=True
    ).astype(jnp.float32)
    grad_proj = jnp.concatenate([grad_q.reshape(row_total, D), kv_mine], axis=1).astype(
        jnp.bfloat16
    )
    grad_w_qkv = product_tn(normed_one, grad_proj)
    grad_b_qkv = jnp.sum(grad_proj.astype(jnp.float32), axis=0)
    unused, norm_pull_one = jax.vjp(
        layer_norm,
        block_input.astype(jnp.float32),
        ln1_gain.astype(jnp.float32),
        ln1_bias.astype(jnp.float32),
    )
    grad_in_norm, grad_ln1_gain, grad_ln1_bias = norm_pull_one(product_nt(grad_proj, w_qkv))
    input_grad = grad_middle + grad_in_norm
    grad_set = (
        grad_ln1_gain,
        grad_ln1_bias,
        grad_w_qkv,
        grad_b_qkv,
        grad_w_out,
        grad_b_out,
        grad_ln2_gain,
        grad_ln2_bias,
        grad_w_fc,
        grad_b_fc,
        grad_w_proj,
        grad_b_proj,
    )
    return (input_grad, grad_set)


def on_device_generic(
    block_input,
    seq_long,
    ln1_gain,
    ln1_bias,
    w_qkv,
    b_qkv,
    w_out,
    b_out,
    ln2_gain,
    ln2_bias,
    w_fc,
    b_fc,
    w_proj,
    b_proj,
    out_grad,
):
    long_flag = seq_long[0]
    fsdp_index = lax.axis_index("fsdp")
    weight_set = (
        lax.all_gather(ln1_gain, AXES, axis=0, tiled=True),
        lax.all_gather(ln1_bias, AXES, axis=0, tiled=True),
        lax.all_gather(w_qkv, AXES, axis=0, tiled=True),
        lax.all_gather(b_qkv, AXES, axis=0, tiled=True),
        lax.all_gather(w_out, AXES, axis=0, tiled=True),
        lax.all_gather(b_out, AXES, axis=0, tiled=True),
        lax.all_gather(ln2_gain, AXES, axis=0, tiled=True),
        lax.all_gather(ln2_bias, AXES, axis=0, tiled=True),
        lax.all_gather(w_fc, AXES, axis=0, tiled=True),
        lax.all_gather(b_fc, AXES, axis=0, tiled=True),
        lax.all_gather(w_proj, AXES, axis=0, tiled=True),
        lax.all_gather(b_proj, AXES, axis=0, tiled=True),
    )
    saved = forward(block_input, weight_set, long_flag, fsdp_index, gather_first)
    block_output = saved[0].astype(jnp.bfloat16)
    weight_set = (
        lax.all_gather(ln1_gain, AXES, axis=0, tiled=True),
        lax.all_gather(ln1_bias, AXES, axis=0, tiled=True),
        lax.all_gather(w_qkv, AXES, axis=0, tiled=True),
        lax.all_gather(b_qkv, AXES, axis=0, tiled=True),
        lax.all_gather(w_out, AXES, axis=0, tiled=True),
        lax.all_gather(b_out, AXES, axis=0, tiled=True),
        lax.all_gather(ln2_gain, AXES, axis=0, tiled=True),
        lax.all_gather(ln2_bias, AXES, axis=0, tiled=True),
        lax.all_gather(w_fc, AXES, axis=0, tiled=True),
        lax.all_gather(b_fc, AXES, axis=0, tiled=True),
        lax.all_gather(w_proj, AXES, axis=0, tiled=True),
        lax.all_gather(b_proj, AXES, axis=0, tiled=True),
    )
    saved = forward(block_input, weight_set, long_flag, fsdp_index, gather_second)
    input_grad, grad_set = backward(saved, weight_set, block_input, out_grad)
    grad_shards = (
        lax.psum_scatter(grad_set[0], AXES, scatter_dimension=0, tiled=True),
        lax.psum_scatter(grad_set[1], AXES, scatter_dimension=0, tiled=True),
        lax.psum_scatter(grad_set[2], AXES, scatter_dimension=0, tiled=True),
        lax.psum_scatter(grad_set[3], AXES, scatter_dimension=0, tiled=True),
        lax.psum_scatter(grad_set[4], AXES, scatter_dimension=0, tiled=True),
        lax.psum_scatter(grad_set[5], AXES, scatter_dimension=0, tiled=True),
        lax.psum_scatter(grad_set[6], AXES, scatter_dimension=0, tiled=True),
        lax.psum_scatter(grad_set[7], AXES, scatter_dimension=0, tiled=True),
        lax.psum_scatter(grad_set[8], AXES, scatter_dimension=0, tiled=True),
        lax.psum_scatter(grad_set[9], AXES, scatter_dimension=0, tiled=True),
        lax.psum_scatter(grad_set[10], AXES, scatter_dimension=0, tiled=True),
        lax.psum_scatter(grad_set[11], AXES, scatter_dimension=0, tiled=True),
    )
    return (block_output, input_grad) + tuple(grad_shards)


def nt(a, b):
    return lax.dot_general(a, b, (((1,), (1,)), ((), ())), preferred_element_type=f32)


def nn(a, b):
    return jnp.dot(a, b, preferred_element_type=f32)


PAIR = 2 * HD


def busy(microseconds):
    return pl.CostEstimate(
        flops=int(microseconds * 1.15e9), bytes_accessed=int(microseconds * 1e6), transcendentals=0
    )


def split_heads(pair):
    left = lax.broadcasted_iota(jnp.int32, pair.shape, 1) < HD
    zero = jnp.zeros_like(pair)
    return (jnp.where(left, pair, zero), jnp.where(left, zero, pair))


def up_to(keys, queries):
    return lax.broadcasted_iota(jnp.int32, (keys, queries), 0) <= lax.broadcasted_iota(
        jnp.int32, (keys, queries), 1
    )


def attend_fwd_kernel(
    block, strips, flag_ref, place_ref, q_ref, k_ref, v_ref, o_ref, send_ref, lse_ref, vt_ref
):
    i = pl.program_id(0)
    part = block // strips

    @pl.when(i == 0)
    def _():
        vt_ref[...] = v_ref[...].astype(f32).T.astype(bf)

    per_seq = jnp.where(flag_ref[0] == 1, 2 * SEQ, SEQ) // block
    first = i // per_seq * per_seq
    q_heads = split_heads(q_ref[...])

    def update(state, h, start, keys, low, mask):
        start = pl.multiple_of(start, part)
        s = nt(k_ref[pl.ds(start, keys), :], q_heads[h][low:, :])
        x = s * s + 1.0
        mag = x * lax.rsqrt(x)
        if mask is not None:
            mag = jnp.where(mask, mag, FAR)
        top = jnp.max(mag, axis=0, keepdims=True)
        if state is not None:
            old_top, old_sum, old_acc = state
            top = jnp.maximum(top, old_top)
        e = jnp.exp(mag - top)
        fresh = jnp.sum(e, axis=0, keepdims=True)
        w = (jnp.tanh(s) * e).astype(bf)
        acc = nn(vt_ref[h * HD : (h + 1) * HD, pl.ds(start, keys)], w)
        if state is not None:
            alpha = jnp.exp(old_top - top)
            fresh = fresh + alpha * old_sum
            acc = acc + alpha * old_acc
        return (top, fresh, acc)

    base = i * block
    states = []
    for h in range(2):
        state = update(None, h, base, part, 0, up_to(part, block))
        for m in range(1, strips):
            low = m * part
            tail = update(
                tuple(item[:, low:] for item in state),
                h,
                base + low,
                part,
                low,
                up_to(part, block - low),
            )
            state = tuple(
                jnp.concatenate([a[:, :low], b], axis=1) for a, b in zip(state, tail)
            )
        states.append(state)
    states = lax.fori_loop(
        first,
        i,
        lambda j, st: tuple(update(st[h], h, j * block, block, 0, None) for h in range(2)),
        tuple(states),
    )
    for h in range(2):
        top, total, _ = states[h]
        lse_ref[h : h + 1, :] = top + jnp.log(total)
    both = jnp.concatenate([states[h][2] / states[h][1] for h in range(2)], axis=0)
    heads = both.T.astype(bf)
    o_ref[...] = heads

    @pl.when(i // (pl.num_programs(0) // 2) != place_ref[0])
    def _():
        send_ref[pl.ds(pl.multiple_of(i % (pl.num_programs(0) // 2) * block, block), block), :] = heads


def attend_fwd(flag, place, projected, pair, block=1024, strips=4):
    rows = projected.shape[0]
    full = lambda c: pl.BlockSpec((rows, PAIR), lambda i, f, s: (0, 3 * pair + c))
    return pl.pallas_call(
        functools.partial(attend_fwd_kernel, block, strips),
        grid_spec=pltpu.PrefetchScalarGridSpec(
            num_scalar_prefetch=2,
            grid=(rows // block,),
            in_specs=[pl.BlockSpec((block, PAIR), lambda i, f, s: (i, 3 * pair)), full(1), full(2)],
            out_specs=[
                pl.BlockSpec((block, PAIR), lambda i, f, s: (i, 0)),
                pl.BlockSpec((rows // 2, PAIR), lambda i, f, s: (0, 0)),
                pl.BlockSpec((8, block), lambda i, f, s: (0, i)),
            ],
            scratch_shapes=[pltpu.VMEM((PAIR, rows), bf)],
        ),
        out_shape=[
            jax.ShapeDtypeStruct((rows, PAIR), bf),
            jax.ShapeDtypeStruct((rows // 2, PAIR), bf),
            jax.ShapeDtypeStruct((8, rows), f32),
        ],
        cost_estimate=busy(16),
        name="attend_fwd",
    )(flag, place, projected, projected, projected)


def attend_bwd_kernel(
    block,
    strips,
    flag_ref,
    place_ref,
    q_ref,
    k_ref,
    v_ref,
    o_ref,
    keep_ref,
    other_ref,
    lse_ref,
    g_ref,
    send_ref,
    dqt_ref,
    inner_ref,
    do_ref,
):
    j = pl.program_id(0)
    last = pl.num_programs(0) - 1
    rows = q_ref.shape[0]
    side_rows = rows // 2
    part = block // strips

    @pl.when(j == 0)
    def _():
        dqt_ref[...] = jnp.zeros_like(dqt_ref)
        on_left = place_ref[0] == 0
        do_ref[:side_rows, :] = jnp.where(on_left, keep_ref[...], other_ref[...])
        do_ref[side_rows:, :] = jnp.where(on_left, other_ref[...], keep_ref[...])
        prod = o_ref[...].astype(f32) * do_ref[...].astype(f32)
        head = lax.broadcasted_iota(jnp.int32, (8, PAIR), 0)
        lane = lax.broadcasted_iota(jnp.int32, (8, PAIR), 1)
        inner_ref[...] = lax.dot_general(
            (head == lane // HD).astype(f32),
            prod,
            (((1,), (1,)), ((), ())),
            precision=lax.Precision.HIGHEST,
            preferred_element_type=f32,
        )

    per_seq = jnp.where(flag_ref[0] == 1, 2 * SEQ, SEQ) // block
    stop = (j // per_seq + 1) * per_seq
    k_pair = k_ref[...]
    k_heads = split_heads(k_pair)
    v_heads = split_heads(v_ref[...])
    k_turned = k_pair.astype(f32).T.astype(bf)

    def update(state, low_key, keys, start, queries, mask):
        cols = pl.ds(pl.multiple_of(start, part), queries)
        q_pair = q_ref[cols, :]
        do_pair = do_ref[cols, :]
        q_heads = split_heads(q_pair)
        do_heads = split_heads(do_pair)
        key_rows = slice(low_key, low_key + keys)
        dk, dv = (None, None) if state is None else state
        for h in range(2):
            head_rows = slice(h * HD, (h + 1) * HD)
            s = nt(k_heads[h][key_rows], q_pair)
            x = s * s + 1.0
            r = lax.rsqrt(x)
            e = jnp.exp(x * r - lse_ref[h : h + 1, cols])
            if mask is not None:
                e = jnp.where(mask, e, 0.0)
            t = jnp.tanh(s)
            slope = s * r
            w = (t * e).astype(bf)
            gw = nt(v_heads[h][key_rows], do_pair)
            ds = (
                e * (gw * (1.0 + t * (slope - t)) - slope * inner_ref[h : h + 1, cols])
            ).astype(bf)
            dv_part = nn(w, do_heads[h])
            dk_part = nn(ds, q_heads[h])
            dv = dv_part if dv is None else dv + dv_part
            dk = dk_part if dk is None else dk + dk_part
            dqt_ref[head_rows, cols] += nn(k_turned[head_rows, key_rows], ds)
        return (dk, dv)

    base = j * block
    strip_grads = [
        update(None, m * part, part, base + m * part, block - m * part, up_to(part, block - m * part))
        for m in range(strips)
    ]
    state = tuple(jnp.concatenate(items, axis=0) for items in zip(*strip_grads))
    dk, dv = lax.fori_loop(
        j + 1, stop, lambda i, st: update(st, 0, block, i * block, block, None), state
    )
    mine = pl.ds(pl.multiple_of(base, block), block)
    g_ref[mine, PAIR : 2 * PAIR] = dk.astype(bf)
    g_ref[mine, 2 * PAIR :] = dv.astype(bf)

    @pl.when(j == last)
    def _():
        g_ref[:, :PAIR] = (dqt_ref[...] * HD**-0.5).T.astype(bf)
        theirs = pl.multiple_of((1 - place_ref[0]) * side_rows, side_rows)
        send_ref[...] = g_ref[pl.ds(theirs, side_rows), :]


def attend_bwd(flag, place, projected, pair, heads_out, keep, other, lse, block=1024, strips=4):
    rows = projected.shape[0]
    fixed = lambda r: pl.BlockSpec((r, PAIR), lambda j, f, s: (0, 0))
    part = lambda c: pl.BlockSpec((block, PAIR), lambda j, f, s: (j, 3 * pair + c))
    return pl.pallas_call(
        functools.partial(attend_bwd_kernel, block, strips),
        grid_spec=pltpu.PrefetchScalarGridSpec(
            num_scalar_prefetch=2,
            grid=(rows // block,),
            in_specs=[
                pl.BlockSpec((rows, PAIR), lambda j, f, s: (0, 3 * pair)),
                part(1),
                part(2),
                fixed(rows),
                pl.BlockSpec((rows // 2, PAIR), lambda j, f, s: (0, pair)),
                pl.BlockSpec((rows // 2, PAIR), lambda j, f, s: (0, pair)),
                pl.BlockSpec((8, rows), lambda j, f, s: (0, 0)),
            ],
            out_specs=[
                pl.BlockSpec((rows, 3 * PAIR), lambda j, f, s: (0, 0)),
                pl.BlockSpec((rows // 2, 3 * PAIR), lambda j, f, s: (0, 0)),
            ],
            scratch_shapes=[
                pltpu.VMEM((PAIR, rows), f32),
                pltpu.VMEM((8, rows), f32),
                pltpu.VMEM((rows, PAIR), bf),
            ],
        ),
        out_shape=[
            jax.ShapeDtypeStruct((rows, 3 * PAIR), bf),
            jax.ShapeDtypeStruct((rows // 2, 3 * PAIR), bf),
        ],
        cost_estimate=busy(25),
        name="attend_bwd",
    )(flag, place, projected, projected, projected, heads_out, keep, other, lse)


def tn(a, b):
    return lax.dot_general(a, b, (((0,), (0,)), ((), ())), preferred_element_type=f32)


def norm_stats(rows_in):
    mean = jnp.mean(rows_in, axis=-1, keepdims=True)
    centred = rows_in - mean
    variance = jnp.mean(centred * centred, axis=-1, keepdims=True)
    scale = lax.rsqrt(variance + EPS)
    return centred * scale, scale


def project_kernel(place_ref, own_ref, other_ref, gain_ref, bias_ref, w_ref, b_ref, n_ref, p_ref):
    per_side = pl.num_programs(0) // 2
    is_own = pl.program_id(0) // per_side == place_ref[0]
    rows = jnp.where(is_own, own_ref[...], other_ref[...]).astype(f32)
    piece = rows.shape[0] // 4
    for r in range(0, rows.shape[0], piece):
        here = slice(r, r + piece)
        unit, _ = norm_stats(rows[here])
        normed = (unit * gain_ref[...] + bias_ref[...]).astype(bf)
        n_ref[here, :] = normed
        for c in range(0, p_ref.shape[1], 3 * PAIR):
            cols = slice(c, c + 3 * PAIR)
            part = (nn(normed, w_ref[:, cols]) + b_ref[:, cols]).astype(bf)
            p_ref[here, c : c + PAIR] = part[:, :PAIR] * jnp.asarray(HD**-0.5, bf)
            p_ref[here, c + PAIR : c + 3 * PAIR] = part[:, PAIR:]


def project(place, own, other, gain, bias, weight, w_bias, block=512):
    rows, width = own.shape
    per_side = rows // block
    cols = weight.shape[1]
    fixed = lambda shape: pl.BlockSpec(shape, lambda i, s: (0, 0))
    return pl.pallas_call(
        project_kernel,
        grid_spec=pltpu.PrefetchScalarGridSpec(
            num_scalar_prefetch=1,
            grid=(2 * per_side,),
            in_specs=[
                pl.BlockSpec(
                    (block, width), lambda i, s: (jnp.clip(i - s[0] * per_side, 0, per_side - 1), 0)
                ),
                pl.BlockSpec(
                    (block, width),
                    lambda i, s: (jnp.clip(i - (1 - s[0]) * per_side, 0, per_side - 1), 0),
                ),
                fixed((1, width)),
                fixed((1, width)),
                fixed(weight.shape),
                fixed((1, cols)),
            ],
            out_specs=[
                pl.BlockSpec((block, width), lambda i, s: (i, 0)),
                pl.BlockSpec((block, cols), lambda i, s: (i, 0)),
            ],
        ),
        out_shape=[
            jax.ShapeDtypeStruct((2 * rows, width), bf),
            jax.ShapeDtypeStruct((2 * rows, cols), bf),
        ],
        cost_estimate=busy(11),
        name="norm_project",
    )(place, own, other, gain, bias, weight, w_bias)


GELU_C = math.sqrt(2 / math.pi)


def mlp_kernel(
    place_ref,
    g_hbm,
    x_ref,
    og_ref,
    ha0_ref,
    ha1_ref,
    ha2_ref,
    hb0_ref,
    hb1_ref,
    hb2_ref,
    bout_ref,
    gain_ref,
    bias_ref,
    bfc_ref,
    bproj_ref,
    out_ref,
    mixed_ref,
    n2_ref,
    act_ref,
    gp_ref,
    gm_ref,
    gml_ref,
    keep_ref,
    send_ref,
    sums_ref,
    w_ref,
    sem,
):
    i = pl.program_id(0)
    devices = g_hbm.shape[0]
    sub = g_hbm.shape[2]
    width = devices * sub
    chunks = (g_hbm.shape[1] - 1) // 2

    def load(slot):
        return pltpu.make_async_copy(g_hbm.at[:, slot], w_ref.at[slot], sem.at[slot])

    order = [2 * chunks] + list(range(chunks, 2 * chunks))

    def load_proj():
        return pltpu.make_async_copy(
            g_hbm.at[:, pl.ds(0, chunks)], wp_view(), sem.at[0]
        )

    def wp_view():
        return w_ref.at[pl.ds(0, chunks)].reshape(devices, chunks, sub, width)

    @pl.when(i == 0)
    def _():
        load(order[0]).start()
        load(order[1]).start()
        load_proj().start()
        for slot in order[2:]:
            load(slot).start()
        sums_ref[...] = jnp.zeros_like(sums_ref)

    def arrive(copy):
        @pl.when(i == 0)
        def _():
            copy.wait()

    def weight(slot):
        return w_ref[slot].reshape(width, width)

    on_left = place_ref[0] == 0
    ha = jnp.concatenate([ha0_ref[...], ha1_ref[...], ha2_ref[...]], axis=1)
    hb = jnp.concatenate([hb0_ref[...], hb1_ref[...], hb2_ref[...]], axis=1)
    mixed = jnp.concatenate([jnp.where(on_left, ha, hb), jnp.where(on_left, hb, ha)], axis=1)
    mixed_ref[...] = mixed
    arrive(load(order[0]))
    og_low = og_ref[...]
    og = og_low.astype(f32)
    middle = x_ref[...].astype(f32) + nn(mixed, weight(2 * chunks)) + bout_ref[...]
    unit, scale = norm_stats(middle)
    n2 = (unit * gain_ref[...] + bias_ref[...]).astype(bf)
    n2_ref[...] = n2
    out = middle + bproj_ref[...]
    e = jnp.zeros_like(middle)
    for c in range(chunks):
        cols = slice(c * width, (c + 1) * width)
        arrive(load(order[1 + c]))
        w_fc = weight(chunks + c)
        pre = nn(n2, w_fc) + bfc_ref[:, cols]
        if c == 0:
            arrive(load_proj())
        square = pre * pre
        t = jnp.tanh(GELU_C * pre * (1.0 + 0.044715 * square))
        low_half = 0.5 * (1.0 + t)
        act = (pre * low_half).astype(bf)
        act_ref[:, cols] = act
        w_proj = weight(c)
        out = out + nn(act, w_proj)
        slope = low_half + 0.5 * pre * (1.0 - t * t) * (
            GELU_C * (1.0 + 3.0 * 0.044715 * square)
        )
        gp = (nt(og_low, w_proj) * slope).astype(bf)
        gp_ref[:, cols] = gp
        sums_ref[0:1, cols] += jnp.sum(gp.astype(f32), axis=0, keepdims=True)
        e = e + nt(gp, w_fc)
    out_ref[...] = out.astype(bf)
    sums_ref[1:2, 0:width] += jnp.sum(og, axis=0, keepdims=True)
    sums_ref[1:2, width : 2 * width] += jnp.sum(e * unit, axis=0, keepdims=True)
    sums_ref[1:2, 2 * width : 3 * width] += jnp.sum(e, axis=0, keepdims=True)
    eg = e * gain_ref[...]
    gm = og + scale * (
        eg
        - jnp.mean(eg, axis=-1, keepdims=True)
        - unit * jnp.mean(eg * unit, axis=-1, keepdims=True)
    )
    gm_ref[...] = gm
    gml = gm.astype(bf)
    gml_ref[...] = gml
    sums_ref[1:2, 3 * width : 4 * width] += jnp.sum(gml.astype(f32), axis=0, keepdims=True)
    gh = nt(gml, weight(2 * chunks)).astype(bf)
    half = width // 2
    left = gh[:, :half]
    right = gh[:, half:]
    keep_ref[...] = jnp.where(on_left, left, right)
    send_ref[...] = jnp.where(on_left, right, left)


def mlp(place, gathered, x, og, heads_mine, heads_other, b_out, gain, bias, b_fc, b_proj, block=256):
    rows, width = x.shape
    steps = rows // block
    hidden = b_fc.shape[1]
    row = lambda cols: pl.BlockSpec((block, cols), lambda i, s: (i, 0))
    fixed = lambda cols: pl.BlockSpec((1, cols), lambda i, s: (0, 0))
    shape = lambda cols, kind: jax.ShapeDtypeStruct((rows, cols), kind)
    return pl.pallas_call(
        mlp_kernel,
        grid_spec=pltpu.PrefetchScalarGridSpec(
            num_scalar_prefetch=1,
            grid=(steps,),
            in_specs=[
                pl.BlockSpec(memory_space=pl.ANY),
                row(width),
                row(width),
                *[pl.BlockSpec((block, PAIR), lambda i, s: (s[0] * steps + i, 0))] * 3,
                *[row(PAIR)] * 3,
                fixed(width),
                fixed(width),
                fixed(width),
                fixed(hidden),
                fixed(width),
            ],
            out_specs=[
                row(width),
                row(width),
                row(width),
                row(hidden),
                row(hidden),
                row(width),
                row(width),
                *[row(width // 2)] * 2,
                pl.BlockSpec((8, hidden), lambda i, s: (0, 0)),
            ],
            scratch_shapes=[
                pltpu.VMEM((gathered.shape[1], gathered.shape[0], gathered.shape[2], width), bf),
                pltpu.SemaphoreType.DMA((gathered.shape[1],)),
            ],
        ),
        out_shape=[
            shape(width, bf),
            shape(width, bf),
            shape(width, bf),
            shape(hidden, bf),
            shape(hidden, bf),
            shape(width, f32),
            shape(width, bf),
            *[shape(width // 2, bf)] * 2,
            jax.ShapeDtypeStruct((8, hidden), f32),
        ],
        compiler_params=pltpu.CompilerParams(vmem_limit_bytes=56 * 1024 * 1024),
        cost_estimate=busy(37),
        name="mlp",
    )(place, gathered, x, og, *heads_mine, *heads_other, b_out, gain, bias, b_fc, b_proj)


def weight_grad_kernel(act_ref, gp_ref, og_ref, n2_ref, mixed_ref, gml_ref, out_hbm, buf_ref, sem):
    c = pl.program_id(0)
    last = pl.num_programs(0) - 1
    devices, slots, sub, width = out_hbm.shape
    chunks = (slots - 1) // 2
    group = devices // chunks
    slot = lax.rem(c, 2)

    def proj_copy(step, where):
        return pltpu.make_async_copy(
            buf_ref.at[where].reshape(group, chunks, sub, width),
            out_hbm.at[pl.ds(step * group, group), pl.ds(0, chunks)],
            sem.at[where],
        )

    def other_copy(step, where):
        return pltpu.make_async_copy(buf_ref.at[where], out_hbm.at[:, step], sem.at[where])

    @pl.when(c >= 2)
    def _():
        other_copy(chunks, slot).wait()

    def put(value):
        buf_ref[slot] = value.astype(bf).reshape(devices, sub, width)

    @pl.when(c < chunks)
    def _():
        put(tn(act_ref[...], og_ref[...]))
        proj_copy(c, slot).start()

    @pl.when((c >= chunks) & (c < 2 * chunks))
    def _():
        put(tn(n2_ref[...], gp_ref[...]))
        other_copy(c, slot).start()

    @pl.when(c == last)
    def _():
        put(tn(mixed_ref[...], gml_ref[...]))
        other_copy(c, slot).start()
        other_copy(chunks, 1 - slot).wait()
        other_copy(chunks, slot).wait()


def weight_grads(act, gp, og, n2, mixed, gml, devices):
    rows, width = og.shape
    chunks = act.shape[1] // width
    slots = 2 * chunks + 1
    sub = width // devices
    fixed = pl.BlockSpec((rows, width), lambda c: (0, 0))
    return pl.pallas_call(
        weight_grad_kernel,
        grid=(slots,),
        in_specs=[
            pl.BlockSpec((rows, width), lambda c: (0, jnp.minimum(c, chunks - 1))),
            pl.BlockSpec((rows, width), lambda c: (0, jnp.clip(c - chunks, 0, chunks - 1))),
            fixed,
            fixed,
            fixed,
            fixed,
        ],
        out_specs=pl.BlockSpec(memory_space=pl.ANY),
        out_shape=jax.ShapeDtypeStruct((devices, slots, sub, width), bf),
        scratch_shapes=[
            pltpu.VMEM((2, devices, sub, width), bf),
            pltpu.SemaphoreType.DMA((2,)),
        ],
        cost_estimate=busy(19),
        name="weight_grads",
    )(act, gp, og, n2, mixed, gml)


def norm_sums_kernel(
    place_ref,
    own_ref,
    other_ref,
    g0_ref,
    g1_ref,
    g2_ref,
    r0_ref,
    r1_ref,
    w_ref,
    wo_ref,
    e_ref,
    sums_ref,
    bias_ref,
):
    i = pl.program_id(0)
    per_side = pl.num_programs(0) // 2
    is_own = i // per_side == place_ref[0]

    @pl.when(i == 0)
    def _():
        sums_ref[...] = jnp.zeros_like(sums_ref)
        bias_ref[...] = jnp.zeros_like(bias_ref)

    unit, _ = norm_stats(jnp.where(is_own, own_ref[...], other_ref[...]).astype(f32))
    wide = 3 * PAIR
    e = None
    for p, g_ref in enumerate((g0_ref, g1_ref, g2_ref)):
        cols = slice(p * wide, (p + 1) * wide)
        g = g_ref[...]
        part = nt(g, w_ref[:, cols])
        e = part if e is None else e + part
        bias_ref[0:1, cols] += jnp.sum(g.astype(f32), axis=0, keepdims=True)
    sums_ref[0:1, :] += jnp.sum(e * unit, axis=0, keepdims=True)
    sums_ref[1:2, :] += jnp.sum(e, axis=0, keepdims=True)

    @pl.when(is_own)
    def _():
        total = e
        for p, r_ref in enumerate((r0_ref, r1_ref)):
            total = total + nt(r_ref[...], wo_ref[:, p * wide : (p + 1) * wide])
        e_ref[...] = total


def norm_sums(place, own, other, grads, received, weight, weight_other, block=256):
    rows, width = own.shape
    per_side = rows // block
    cols = weight.shape[1]
    mine = lambda i, s: (jnp.clip(i - s[0] * per_side, 0, per_side - 1), 0)
    theirs = lambda i, s: (jnp.clip(i - (1 - s[0]) * per_side, 0, per_side - 1), 0)
    fixed = lambda shape: pl.BlockSpec(shape, lambda i, s: (0, 0))
    return pl.pallas_call(
        norm_sums_kernel,
        grid_spec=pltpu.PrefetchScalarGridSpec(
            num_scalar_prefetch=1,
            grid=(2 * per_side,),
            in_specs=[
                pl.BlockSpec((block, width), mine),
                pl.BlockSpec((block, width), theirs),
                *[pl.BlockSpec((block, 3 * PAIR), lambda i, s: (i, 0))] * 3,
                *[pl.BlockSpec((block, 3 * PAIR), mine)] * 2,
                fixed(weight.shape),
                fixed(weight.shape),
            ],
            out_specs=[pl.BlockSpec((block, width), mine), fixed((8, width)), fixed((8, cols))],
        ),
        out_shape=[
            jax.ShapeDtypeStruct((rows, width), f32),
            jax.ShapeDtypeStruct((8, width), f32),
            jax.ShapeDtypeStruct((8, cols), f32),
        ],
        cost_estimate=busy(13),
        name="norm_sums",
    )(place, own, other, *grads, *received, weight, weight_other)


def finish_kernel(x_ref, gm_ref, e_ref, r_ref, wo_ref, gain_ref, out_ref):
    unit, scale = norm_stats(x_ref[...].astype(f32))
    eg = (e_ref[...] + nt(r_ref[...], wo_ref[...])) * gain_ref[...]
    out_ref[...] = gm_ref[...] + scale * (
        eg
        - jnp.mean(eg, axis=-1, keepdims=True)
        - unit * jnp.mean(eg * unit, axis=-1, keepdims=True)
    )


def finish(x, grad_middle, e, received, weight_other, gain, block=256):
    rows, width = x.shape
    row = lambda cols: pl.BlockSpec((block, cols), lambda i: (i, 0))
    last = weight_other.shape[1] // (3 * PAIR) - 1
    return pl.pallas_call(
        finish_kernel,
        grid=(rows // block,),
        in_specs=[
            row(width),
            row(width),
            row(width),
            row(3 * PAIR),
            pl.BlockSpec((width, 3 * PAIR), lambda i: (0, last)),
            pl.BlockSpec((1, width), lambda i: (0, 0)),
        ],
        out_specs=row(width),
        out_shape=jax.ShapeDtypeStruct((rows, width), f32),
        cost_estimate=busy(6),
        name="finish",
    )(x, grad_middle, e, received, weight_other, gain)


def swap(value, bit, total):
    return lax.ppermute(value, AXES, [(i, i ^ bit) for i in range(total)])


def gather_dp(shard, dp_size, order):
    me = lax.axis_index("dp")
    bits = dp_size.bit_length() - 1
    held = shard.reshape((1,) * bits + shard.shape)
    for bit in order:
        other = swap(held, 2 << bit, 2 * dp_size)
        low = (me >> bit) & 1 == 0
        held = jnp.concatenate(
            [jnp.where(low, held, other), jnp.where(low, other, held)], axis=bits - 1 - bit
        )
    return held.reshape((dp_size * shard.shape[0],) + shard.shape[1:])


def scatter_dp(whole, dp_size, order):
    me = lax.axis_index("dp")
    bits = dp_size.bit_length() - 1
    rows = whole.shape[0] // dp_size
    held = whole.reshape((2,) * bits + (rows,) + whole.shape[1:])
    for bit in order:
        axis = bits - 1 - bit
        low = (me >> bit) & 1 == 0
        first = lax.slice_in_dim(held, 0, 1, axis=axis)
        second = lax.slice_in_dim(held, 1, 2, axis=axis)
        mine = jnp.where(low, first, second)
        sent = jnp.where(low, second, first).astype(bf)
        held = mine.astype(f32) + swap(sent, 2 << bit, 2 * dp_size).astype(
            f32
        )
    return held.reshape((rows,) + whole.shape[1:])


def sum_all(vector, order, total):
    for bit in [2 << bit for bit in order] + [1]:
        vector = vector + swap(vector, bit, total)
    return vector


def on_device_pair(
    dp_size,
    block_input,
    seq_long,
    ln1_gain,
    ln1_bias,
    w_qkv,
    b_qkv,
    w_out,
    b_out,
    ln2_gain,
    ln2_bias,
    w_fc,
    b_fc,
    w_proj,
    b_proj,
    out_grad,
):
    total = 2 * dp_size
    side = lax.axis_index("fsdp")
    flat = lax.axis_index("dp") * 2 + side
    on_left = side == 0
    half = D // 2
    dp_bits = list(range(dp_size.bit_length() - 1))
    gather_order = dp_bits[1:2] + dp_bits[:1:-1] + dp_bits[:1]
    scatter_order = dp_bits[:1] + dp_bits[2:] + dp_bits[1:2]

    def ordered(mine, other, axis):
        return jnp.concatenate(
            [jnp.where(on_left, mine, other), jnp.where(on_left, other, mine)], axis=axis
        )

    pairs = half // PAIR

    def head_columns(rows_in, which):
        split = rows_in.reshape(rows_in.shape[0], 3, 2, pairs, PAIR)
        mine = lax.dynamic_index_in_dim(split, which, 2, keepdims=False)
        return jnp.transpose(mine, (0, 2, 1, 3)).reshape(rows_in.shape[0], 3 * half)

    small = (ln1_gain, ln1_bias, b_qkv, b_out, ln2_gain, ln2_bias, b_fc, b_proj)
    placed = jnp.concatenate(
        [
            lax.dynamic_update_slice(
                jnp.zeros((item.shape[0] * total,), bf), item, (item.shape[0] * flat,)
            )
            for item in small
        ]
    )
    gathered = sum_all(placed, gather_order, total).astype(f32)
    pieces = []
    start = 0
    for item in small:
        pieces.append(gathered[start : start + item.shape[0] * total])
        start += item.shape[0] * total
    ln1_gain, ln1_bias, b_qkv, b_out, ln2_gain, ln2_bias, b_fc, b_proj = pieces

    other_input = swap(block_input, 1, total)
    received = swap(head_columns(w_qkv, 1 - side), 1, total)
    w_mine = gather_dp(ordered(head_columns(w_qkv, side), received, 0), dp_size, gather_order)
    w_other = swap(w_mine, 1, total)

    sub = w_out.shape[0]
    chunks = FF // D
    packed = jnp.concatenate(
        [w_proj] + [w_fc[:, c * D : (c + 1) * D] for c in range(chunks)] + [w_out], axis=0
    )
    gathered_w = lax.all_gather(packed, AXES, axis=0, tiled=True)
    gathered_w = gathered_w.reshape(total, 2 * chunks + 1, sub, D)

    def as_row(vector):
        return vector.reshape(1, -1)

    place = side.astype(jnp.int32).reshape(1)
    b_mine = head_columns(as_row(b_qkv), side)
    normed_one, projected = project(
        place, block_input, other_input, as_row(ln1_gain), as_row(ln1_bias), w_mine, b_mine
    )
    heads_mine = []
    heads_other = []
    log_totals = []
    for p in range(pairs):
        heads, heads_sent, log_total = attend_fwd(seq_long, place, projected, p)
        heads_mine.append(heads)
        log_totals.append(log_total)
        heads_other.append(swap(heads_sent, 1, total))
    (
        block_output,
        mixed,
        normed_two,
        hidden_act,
        grad_pre,
        grad_middle,
        grad_mid_low,
        *rest,
    ) = mlp(
        place,
        gathered_w,
        block_input,
        out_grad,
        heads_mine,
        heads_other,
        as_row(b_out),
        as_row(ln2_gain),
        as_row(ln2_bias),
        as_row(b_fc),
        as_row(b_proj),
    )
    grad_keep, grad_sent, sums = rest
    grad_other = swap(grad_sent, 1, total)
    packed_grads = weight_grads(
        hidden_act, grad_pre, out_grad, normed_two, mixed, grad_mid_low, total
    )
    shard = lax.psum_scatter(
        packed_grads.reshape(total * (2 * chunks + 1) * sub, D),
        AXES,
        scatter_dimension=0,
        tiled=True,
    ).astype(f32)
    shard_w_proj = shard[: chunks * sub]
    shard_w_fc = jnp.concatenate(
        [shard[(chunks + c) * sub : (chunks + c + 1) * sub] for c in range(chunks)], axis=1
    )
    shard_w_out = shard[2 * chunks * sub :]
    grad_b_fc = sums[0]
    grad_b_proj, grad_ln2_gain, grad_ln2_bias, grad_b_out = (
        sums[1, k * D : (k + 1) * D] for k in range(4)
    )
    grads = []
    grads_other = []
    columns = []
    for p in range(pairs):
        grad_pair, pair_sent = attend_bwd(
            seq_long,
            place,
            projected,
            p,
            heads_mine[p],
            grad_keep,
            grad_other,
            log_totals[p],
        )
        grads.append(grad_pair)
        grads_other.append(swap(pair_sent, 1, total))
        columns.append(product_tn(normed_one, grad_pair).astype(bf))
    shards = [
        scatter_dp(jnp.concatenate(columns[:-1], axis=1), dp_size, scatter_order),
        scatter_dp(columns[-1], dp_size, scatter_order),
    ]

    e_partial, norm_one_sums, grad_b_mine = norm_sums(
        place, block_input, other_input, grads, grads_other[:-1], w_mine, w_other
    )
    input_grad = finish(
        block_input, grad_middle, e_partial, grads_other[-1], w_other, as_row(ln1_gain)
    )

    shard_rows = jnp.concatenate(shards, axis=1).reshape(2, -1, 3 * half)
    keep = lax.dynamic_index_in_dim(shard_rows, side, 0, keepdims=False)
    send = lax.dynamic_index_in_dim(shard_rows, 1 - side, 0, keepdims=False)
    taken = swap(send, 1, total)

    def by_part(rows_in):
        split = rows_in.reshape(rows_in.shape[0], pairs, 3, PAIR)
        return jnp.transpose(split, (0, 2, 1, 3)).reshape(rows_in.shape[0], 3, 1, half)

    shard_w_qkv = ordered(by_part(keep), by_part(taken), 2).reshape(-1, 3 * D)
    grad_b_part = by_part(grad_b_mine[0:1])
    grad_b_qkv = ordered(grad_b_part, jnp.zeros_like(grad_b_part), 2).reshape(3 * D)
    grad_vectors = (
        grad_b_out,
        grad_ln2_gain,
        grad_ln2_bias,
        grad_b_fc,
        grad_b_proj,
        norm_one_sums[0],
        norm_one_sums[1],
        grad_b_qkv,
    )
    summed = sum_all(jnp.concatenate(grad_vectors), scatter_order, total)
    begin = 0
    vector_shards = []
    for item in grad_vectors:
        size = item.shape[0] // total
        vector_shards.append(lax.dynamic_slice(summed, (begin + size * flat,), (size,)))
        begin += item.shape[0]
    (
        shard_b_out,
        shard_ln2_gain,
        shard_ln2_bias,
        shard_b_fc,
        shard_b_proj,
        shard_ln1_gain,
        shard_ln1_bias,
        shard_b_qkv,
    ) = vector_shards
    return (
        block_output,
        input_grad,
        shard_ln1_gain,
        shard_ln1_bias,
        shard_w_qkv,
        shard_b_qkv,
        shard_w_out,
        shard_b_out,
        shard_ln2_gain,
        shard_ln2_bias,
        shard_w_fc,
        shard_b_fc,
        shard_w_proj,
        shard_b_proj,
    )


def solution(mesh):
    rows, vector, flags = (P(AXES, None), P(AXES), P("dp"))
    weights = (vector, vector, rows, vector, rows, vector, vector, vector, rows, vector, rows, vector)
    whole_slice = dict(
        mesh=mesh,
        in_specs=(rows, flags) + weights + (rows,),
        out_specs=(rows, rows) + weights,
        check_vma=False,
    )
    dp_size = mesh.shape["dp"]
    if mesh.shape["fsdp"] != 2 or dp_size < 8 or dp_size & (dp_size - 1):
        return jax.shard_map(on_device_generic, **whole_slice)

    def on_device(*args):
        return on_device_pair(dp_size, *args)

    return jax.shard_map(on_device, **whole_slice)
```

```python
import functools
import math

import jax
import jax.numpy as jnp
from jax import lax
from jax.experimental import pallas as pl
from jax.experimental.pallas import tpu as pltpu
from jax.sharding import PartitionSpec as P


f32 = jnp.float32
bf = jnp.bfloat16

D = 768
HEADS = 12
HD = 64
FF = 3072
SEQ = 1024


EPS = 1e-05
FAR = -1e30
AXES = ("dp", "fsdp")


def layer_norm(rows_in, gain_vec, bias_vec):
    row_mean = jnp.mean(rows_in, axis=-1, keepdims=True)
    centred = rows_in - row_mean
    variance = jnp.mean(centred * centred, axis=-1, keepdims=True)
    return centred * lax.rsqrt(variance + EPS) * gain_vec + bias_vec


def product(left, right):
    return jnp.dot(left, right, preferred_element_type=jnp.float32)


def product_tn(left, right):
    return lax.dot_general(
        left, right, (((0,), (0,)), ((), ())), preferred_element_type=jnp.float32
    )


def product_nt(left, right):
    return lax.dot_general(
        left, right, (((1,), (1,)), ((), ())), preferred_element_type=jnp.float32
    )


def gather_first(kv_rows):
    return lax.all_gather(kv_rows, "fsdp", axis=0, tiled=True)


def gather_second(kv_rows):
    return lax.all_gather(kv_rows, "fsdp", axis=0, tiled=True)


def block_layout(kv_all):
    group_rows = kv_all.shape[0]
    key_block = math.gcd(group_rows, 512)
    block_count = group_rows // key_block
    kv_blocks = kv_all.reshape(block_count, key_block, 2, HEADS, HD)
    return (key_block, kv_blocks, jnp.arange(block_count, dtype=jnp.int32))


def block_allowed(query_pos, key_start, key_block, seq_length):
    key_pos = key_start + jnp.arange(key_block, dtype=jnp.int32)
    return (query_pos[:, None] // seq_length == key_pos[None, :] // seq_length) & (
        key_pos[None, :] <= query_pos[:, None]
    )


def block_useful(key_start, key_block, query_pos, first_valid):
    return (key_start <= query_pos[-1]) & (key_start + key_block - 1 >= first_valid)


def score_parts(queries, key_part):
    scores = jnp.einsum(
        "qhd,khd->hqk", queries, key_part, preferred_element_type=jnp.float32
    ) * HD ** (-0.5)
    return (scores, jnp.sqrt(scores * scores + 1.0))


def attend(queries, kv_all, query_pos, seq_length, first_valid):
    key_block, kv_blocks, block_ids = block_layout(kv_all)
    row_total = queries.shape[0]

    def stats_step(state_now, block_item):
        block_id, kv_part = block_item
        key_start = block_id * key_block

        def stats_compute(state_in):
            row_top, row_sum = state_in
            allowed = block_allowed(query_pos, key_start, key_block, seq_length)[None]
            _, magnitude = score_parts(queries, kv_part[:, 0])
            masked = jnp.where(allowed, magnitude, FAR)
            new_top = jnp.maximum(row_top, jnp.max(masked, axis=-1))
            fresh = jnp.sum(jnp.where(allowed, jnp.exp(masked - new_top[:, :, None]), 0.0), axis=-1)
            return (new_top, row_sum * jnp.exp(row_top - new_top) + fresh)

        useful = block_useful(key_start, key_block, query_pos, first_valid)
        return (lax.cond(useful, stats_compute, lambda kept_state: kept_state, state_now), None)

    start_state = (
        jnp.full((HEADS, row_total), FAR, jnp.float32),
        jnp.zeros((HEADS, row_total), jnp.float32),
    )
    (row_top, row_sum), unused = lax.scan(stats_step, start_state, (block_ids, kv_blocks))
    log_total = row_top + jnp.log(row_sum)

    def value_step(accum_now, block_item):
        block_id, kv_part = block_item
        key_start = block_id * key_block

        def value_compute(accum_in):
            allowed = block_allowed(query_pos, key_start, key_block, seq_length)[None]
            scores, magnitude = score_parts(queries, kv_part[:, 0])
            weights = jnp.where(
                allowed, jnp.tanh(scores) * jnp.exp(magnitude - log_total[:, :, None]), 0.0
            ).astype(jnp.bfloat16)
            return accum_in + jnp.einsum(
                "hqk,khd->qhd", weights, kv_part[:, 1], preferred_element_type=jnp.float32
            )

        useful = block_useful(key_start, key_block, query_pos, first_valid)
        return (lax.cond(useful, value_compute, lambda kept_accum: kept_accum, accum_now), None)

    start_accum = jnp.zeros((row_total, HEADS, HD), jnp.float32)
    attn_heads, unused = lax.scan(value_step, start_accum, (block_ids, kv_blocks))
    return (attn_heads, log_total)


def attend_back(
    queries, kv_all, query_pos, seq_length, first_valid, log_total, attn_heads, grad_heads
):
    key_block, kv_blocks, block_ids = block_layout(kv_all)
    row_total = queries.shape[0]
    inner = jnp.transpose(jnp.sum(grad_heads.astype(jnp.float32) * attn_heads, axis=-1))

    def grad_step(dq_now, block_item):
        block_id, kv_part = block_item
        key_start = block_id * key_block

        def grad_compute(dq_in):
            allowed = block_allowed(query_pos, key_start, key_block, seq_length)[None]
            scores, magnitude = score_parts(queries, kv_part[:, 0])
            expo = jnp.where(allowed, jnp.exp(magnitude - log_total[:, :, None]), 0.0)
            tangent = jnp.tanh(scores)
            weights = (tangent * expo).astype(jnp.bfloat16)
            grad_v = jnp.einsum(
                "hqk,qhd->khd", weights, grad_heads, preferred_element_type=jnp.float32
            )
            grad_weight = jnp.einsum(
                "qhd,khd->hqk", grad_heads, kv_part[:, 1], preferred_element_type=jnp.float32
            )
            slope = scores / magnitude
            grad_scores = (
                expo
                * (
                    grad_weight * (1.0 - tangent * tangent + tangent * slope)
                    - slope * inner[:, :, None]
                )
            ).astype(jnp.bfloat16)
            dq_out = dq_in + jnp.einsum(
                "hqk,khd->qhd", grad_scores, kv_part[:, 0], preferred_element_type=jnp.float32
            ) * HD ** (-0.5)
            grad_k = jnp.einsum(
                "hqk,qhd->khd", grad_scores, queries, preferred_element_type=jnp.float32
            ) * HD ** (-0.5)
            return (
                dq_out,
                jnp.concatenate(
                    [grad_k.reshape(key_block, D), grad_v.reshape(key_block, D)], axis=1
                ),
            )

        def skip_block(dq_in):
            return (dq_in, jnp.zeros((key_block, 2 * D), jnp.float32))

        useful = block_useful(key_start, key_block, query_pos, first_valid)
        return lax.cond(useful, grad_compute, skip_block, dq_now)

    start_dq = jnp.zeros((row_total, HEADS, HD), jnp.float32)
    grad_q, kv_grads = lax.scan(grad_step, start_dq, (block_ids, kv_blocks))
    return (grad_q, kv_grads.reshape(kv_all.shape[0], 2 * D))


def forward(block_input, weight_set, long_flag, fsdp_index, gather_keys):
    (
        ln1_gain,
        ln1_bias,
        w_qkv,
        b_qkv,
        w_out,
        b_out,
        ln2_gain,
        ln2_bias,
        w_fc,
        b_fc,
        w_proj,
        b_proj,
    ) = weight_set
    row_total = block_input.shape[0]
    wide_input = block_input.astype(jnp.float32)
    normed_one = layer_norm(
        wide_input, ln1_gain.astype(jnp.float32), ln1_bias.astype(jnp.float32)
    ).astype(jnp.bfloat16)
    projected = (product(normed_one, w_qkv) + b_qkv.astype(jnp.float32)).astype(jnp.bfloat16)
    queries = projected[:, :D].reshape(row_total, HEADS, HD)
    kv_all = gather_keys(projected[:, D:])
    seq_length = jnp.where(long_flag == 1, 2 * SEQ, SEQ).astype(jnp.int32)
    query_pos = fsdp_index * row_total + jnp.arange(row_total, dtype=jnp.int32)
    first_valid = query_pos[0] // seq_length * seq_length
    attn_heads, log_total = attend(queries, kv_all, query_pos, seq_length, first_valid)
    mixed = attn_heads.reshape(row_total, D).astype(jnp.bfloat16)
    middle = wide_input + product(mixed, w_out) + b_out.astype(jnp.float32)
    normed_two = layer_norm(
        middle, ln2_gain.astype(jnp.float32), ln2_bias.astype(jnp.float32)
    ).astype(jnp.bfloat16)
    hidden_pre = product(normed_two, w_fc) + b_fc.astype(jnp.float32)
    hidden_act = jax.nn.gelu(hidden_pre).astype(jnp.bfloat16)
    block_out = middle + product(hidden_act, w_proj) + b_proj.astype(jnp.float32)
    return (
        block_out,
        normed_one,
        queries,
        kv_all,
        query_pos,
        seq_length,
        first_valid,
        attn_heads,
        log_total,
        mixed,
        middle,
        normed_two,
        hidden_pre,
        hidden_act,
    )


def backward(saved, weight_set, block_input, out_grad):
    (
        _,
        normed_one,
        queries,
        kv_all,
        query_pos,
        seq_length,
        first_valid,
        attn_heads,
        log_total,
        mixed,
        middle,
        normed_two,
        hidden_pre,
        hidden_act,
    ) = saved
    (ln1_gain, ln1_bias, w_qkv, _, w_out, _, ln2_gain, ln2_bias, w_fc, _, w_proj, _) = weight_set
    row_total = block_input.shape[0]
    grad_out = out_grad.astype(jnp.float32)
    grad_w_proj = product_tn(hidden_act, out_grad)
    grad_b_proj = jnp.sum(grad_out, axis=0)
    grad_act = product_nt(out_grad, w_proj)
    unused, gelu_pull = jax.vjp(jax.nn.gelu, hidden_pre)
    grad_pre = gelu_pull(grad_act)[0].astype(jnp.bfloat16)
    grad_w_fc = product_tn(normed_two, grad_pre)
    grad_b_fc = jnp.sum(grad_pre.astype(jnp.float32), axis=0)
    unused, norm_pull_two = jax.vjp(
        layer_norm, middle, ln2_gain.astype(jnp.float32), ln2_bias.astype(jnp.float32)
    )
    grad_mid_norm, grad_ln2_gain, grad_ln2_bias = norm_pull_two(product_nt(grad_pre, w_fc))
    grad_middle = grad_out + grad_mid_norm
    grad_mid_low = grad_middle.astype(jnp.bfloat16)
    grad_w_out = product_tn(mixed, grad_mid_low)
    grad_b_out = jnp.sum(grad_mid_low.astype(jnp.float32), axis=0)
    grad_heads = product_nt(grad_mid_low, w_out).astype(jnp.bfloat16).reshape(row_total, HEADS, HD)
    grad_q, kv_grads = attend_back(
        queries, kv_all, query_pos, seq_length, first_valid, log_total, attn_heads, grad_heads
    )
    kv_mine = lax.psum_scatter(
        kv_grads.astype(jnp.bfloat16), "fsdp", scatter_dimension=0, tiled=True
    ).astype(jnp.float32)
    grad_proj = jnp.concatenate([grad_q.reshape(row_total, D), kv_mine], axis=1).astype(
        jnp.bfloat16
    )
    grad_w_qkv = product_tn(normed_one, grad_proj)
    grad_b_qkv = jnp.sum(grad_proj.astype(jnp.float32), axis=0)
    unused, norm_pull_one = jax.vjp(
        layer_norm,
        block_input.astype(jnp.float32),
        ln1_gain.astype(jnp.float32),
        ln1_bias.astype(jnp.float32),
    )
    grad_in_norm, grad_ln1_gain, grad_ln1_bias = norm_pull_one(product_nt(grad_proj, w_qkv))
    input_grad = grad_middle + grad_in_norm
    grad_set = (
        grad_ln1_gain,
        grad_ln1_bias,
        grad_w_qkv,
        grad_b_qkv,
        grad_w_out,
        grad_b_out,
        grad_ln2_gain,
        grad_ln2_bias,
        grad_w_fc,
        grad_b_fc,
        grad_w_proj,
        grad_b_proj,
    )
    return (input_grad, grad_set)


def on_device_generic(
    block_input,
    seq_long,
    ln1_gain,
    ln1_bias,
    w_qkv,
    b_qkv,
    w_out,
    b_out,
    ln2_gain,
    ln2_bias,
    w_fc,
    b_fc,
    w_proj,
    b_proj,
    out_grad,
):
    long_flag = seq_long[0]
    fsdp_index = lax.axis_index("fsdp")
    weight_set = (
        lax.all_gather(ln1_gain, AXES, axis=0, tiled=True),
        lax.all_gather(ln1_bias, AXES, axis=0, tiled=True),
        lax.all_gather(w_qkv, AXES, axis=0, tiled=True),
        lax.all_gather(b_qkv, AXES, axis=0, tiled=True),
        lax.all_gather(w_out, AXES, axis=0, tiled=True),
        lax.all_gather(b_out, AXES, axis=0, tiled=True),
        lax.all_gather(ln2_gain, AXES, axis=0, tiled=True),
        lax.all_gather(ln2_bias, AXES, axis=0, tiled=True),
        lax.all_gather(w_fc, AXES, axis=0, tiled=True),
        lax.all_gather(b_fc, AXES, axis=0, tiled=True),
        lax.all_gather(w_proj, AXES, axis=0, tiled=True),
        lax.all_gather(b_proj, AXES, axis=0, tiled=True),
    )
    saved = forward(block_input, weight_set, long_flag, fsdp_index, gather_first)
    block_output = saved[0].astype(jnp.bfloat16)
    weight_set = (
        lax.all_gather(ln1_gain, AXES, axis=0, tiled=True),
        lax.all_gather(ln1_bias, AXES, axis=0, tiled=True),
        lax.all_gather(w_qkv, AXES, axis=0, tiled=True),
        lax.all_gather(b_qkv, AXES, axis=0, tiled=True),
        lax.all_gather(w_out, AXES, axis=0, tiled=True),
        lax.all_gather(b_out, AXES, axis=0, tiled=True),
        lax.all_gather(ln2_gain, AXES, axis=0, tiled=True),
        lax.all_gather(ln2_bias, AXES, axis=0, tiled=True),
        lax.all_gather(w_fc, AXES, axis=0, tiled=True),
        lax.all_gather(b_fc, AXES, axis=0, tiled=True),
        lax.all_gather(w_proj, AXES, axis=0, tiled=True),
        lax.all_gather(b_proj, AXES, axis=0, tiled=True),
    )
    saved = forward(block_input, weight_set, long_flag, fsdp_index, gather_second)
    input_grad, grad_set = backward(saved, weight_set, block_input, out_grad)
    grad_shards = (
        lax.psum_scatter(grad_set[0], AXES, scatter_dimension=0, tiled=True),
        lax.psum_scatter(grad_set[1], AXES, scatter_dimension=0, tiled=True),
        lax.psum_scatter(grad_set[2], AXES, scatter_dimension=0, tiled=True),
        lax.psum_scatter(grad_set[3], AXES, scatter_dimension=0, tiled=True),
        lax.psum_scatter(grad_set[4], AXES, scatter_dimension=0, tiled=True),
        lax.psum_scatter(grad_set[5], AXES, scatter_dimension=0, tiled=True),
        lax.psum_scatter(grad_set[6], AXES, scatter_dimension=0, tiled=True),
        lax.psum_scatter(grad_set[7], AXES, scatter_dimension=0, tiled=True),
        lax.psum_scatter(grad_set[8], AXES, scatter_dimension=0, tiled=True),
        lax.psum_scatter(grad_set[9], AXES, scatter_dimension=0, tiled=True),
        lax.psum_scatter(grad_set[10], AXES, scatter_dimension=0, tiled=True),
        lax.psum_scatter(grad_set[11], AXES, scatter_dimension=0, tiled=True),
    )
    return (block_output, input_grad) + tuple(grad_shards)


def nt(a, b):
    return lax.dot_general(a, b, (((1,), (1,)), ((), ())), preferred_element_type=f32)


def nn(a, b):
    return jnp.dot(a, b, preferred_element_type=f32)


PAIR = 2 * HD


def busy(microseconds):
    return pl.CostEstimate(
        flops=int(microseconds * 1.15e9), bytes_accessed=int(microseconds * 1e6), transcendentals=0
    )


def split_heads(pair):
    left = lax.broadcasted_iota(jnp.int32, pair.shape, 1) < HD
    zero = jnp.zeros_like(pair)
    return (jnp.where(left, pair, zero), jnp.where(left, zero, pair))


def up_to(keys, queries):
    return lax.broadcasted_iota(jnp.int32, (keys, queries), 0) <= lax.broadcasted_iota(
        jnp.int32, (keys, queries), 1
    )


def attend_fwd_kernel(
    block, strips, flag_ref, place_ref, q_ref, k_ref, v_ref, o_ref, send_ref, lse_ref, vt_ref
):
    i = pl.program_id(0)
    part = block // strips

    @pl.when(i == 0)
    def _():
        vt_ref[...] = v_ref[...].astype(f32).T.astype(bf)

    per_seq = jnp.where(flag_ref[0] == 1, 2 * SEQ, SEQ) // block
    first = i // per_seq * per_seq
    q_heads = split_heads(q_ref[...])

    def update(state, h, start, keys, low, mask):
        start = pl.multiple_of(start, part)
        s = nt(k_ref[pl.ds(start, keys), :], q_heads[h][low:, :])
        x = s * s + 1.0
        mag = x * lax.rsqrt(x)
        if mask is not None:
            mag = jnp.where(mask, mag, FAR)
        top = jnp.max(mag, axis=0, keepdims=True)
        if state is not None:
            old_top, old_sum, old_acc = state
            top = jnp.maximum(top, old_top)
        e = jnp.exp(mag - top)
        fresh = jnp.sum(e, axis=0, keepdims=True)
        w = (jnp.tanh(s) * e).astype(bf)
        acc = nn(vt_ref[h * HD : (h + 1) * HD, pl.ds(start, keys)], w)
        if state is not None:
            alpha = jnp.exp(old_top - top)
            fresh = fresh + alpha * old_sum
            acc = acc + alpha * old_acc
        return (top, fresh, acc)

    base = i * block
    states = []
    for h in range(2):
        state = update(None, h, base, part, 0, up_to(part, block))
        for m in range(1, strips):
            low = m * part
            tail = update(
                tuple(item[:, low:] for item in state),
                h,
                base + low,
                part,
                low,
                up_to(part, block - low),
            )
            state = tuple(
                jnp.concatenate([a[:, :low], b], axis=1) for a, b in zip(state, tail)
            )
        states.append(state)
    states = lax.fori_loop(
        first,
        i,
        lambda j, st: tuple(update(st[h], h, j * block, block, 0, None) for h in range(2)),
        tuple(states),
    )
    for h in range(2):
        top, total, _ = states[h]
        lse_ref[h : h + 1, :] = top + jnp.log(total)
    both = jnp.concatenate([states[h][2] / states[h][1] for h in range(2)], axis=0)
    heads = both.T.astype(bf)
    o_ref[...] = heads

    @pl.when(i // (pl.num_programs(0) // 2) != place_ref[0])
    def _():
        send_ref[pl.ds(pl.multiple_of(i % (pl.num_programs(0) // 2) * block, block), block), :] = heads


def attend_fwd(flag, place, projected, pair, block=1024, strips=4):
    rows = projected.shape[0]
    full = lambda c: pl.BlockSpec((rows, PAIR), lambda i, f, s: (0, 3 * pair + c))
    return pl.pallas_call(
        functools.partial(attend_fwd_kernel, block, strips),
        grid_spec=pltpu.PrefetchScalarGridSpec(
            num_scalar_prefetch=2,
            grid=(rows // block,),
            in_specs=[pl.BlockSpec((block, PAIR), lambda i, f, s: (i, 3 * pair)), full(1), full(2)],
            out_specs=[
                pl.BlockSpec((block, PAIR), lambda i, f, s: (i, 0)),
                pl.BlockSpec((rows // 2, PAIR), lambda i, f, s: (0, 0)),
                pl.BlockSpec((8, block), lambda i, f, s: (0, i)),
            ],
            scratch_shapes=[pltpu.VMEM((PAIR, rows), bf)],
        ),
        out_shape=[
            jax.ShapeDtypeStruct((rows, PAIR), bf),
            jax.ShapeDtypeStruct((rows // 2, PAIR), bf),
            jax.ShapeDtypeStruct((8, rows), f32),
        ],
        cost_estimate=busy(16),
        name="attend_fwd",
    )(flag, place, projected, projected, projected)


def attend_bwd_kernel(
    block,
    strips,
    flag_ref,
    place_ref,
    q_ref,
    k_ref,
    v_ref,
    o_ref,
    keep_ref,
    other_ref,
    lse_ref,
    g_ref,
    send_ref,
    dqt_ref,
    inner_ref,
    do_ref,
):
    j = pl.program_id(0)
    last = pl.num_programs(0) - 1
    rows = q_ref.shape[0]
    side_rows = rows // 2
    part = block // strips

    @pl.when(j == 0)
    def _():
        dqt_ref[...] = jnp.zeros_like(dqt_ref)
        on_left = place_ref[0] == 0
        do_ref[:side_rows, :] = jnp.where(on_left, keep_ref[...], other_ref[...])
        do_ref[side_rows:, :] = jnp.where(on_left, other_ref[...], keep_ref[...])
        prod = o_ref[...].astype(f32) * do_ref[...].astype(f32)
        head = lax.broadcasted_iota(jnp.int32, (8, PAIR), 0)
        lane = lax.broadcasted_iota(jnp.int32, (8, PAIR), 1)
        inner_ref[...] = lax.dot_general(
            (head == lane // HD).astype(f32),
            prod,
            (((1,), (1,)), ((), ())),
            precision=lax.Precision.HIGHEST,
            preferred_element_type=f32,
        )

    per_seq = jnp.where(flag_ref[0] == 1, 2 * SEQ, SEQ) // block
    stop = (j // per_seq + 1) * per_seq
    k_pair = k_ref[...]
    k_heads = split_heads(k_pair)
    v_heads = split_heads(v_ref[...])
    k_turned = k_pair.astype(f32).T.astype(bf)

    def update(state, low_key, keys, start, queries, mask):
        cols = pl.ds(pl.multiple_of(start, part), queries)
        q_pair = q_ref[cols, :]
        do_pair = do_ref[cols, :]
        q_heads = split_heads(q_pair)
        do_heads = split_heads(do_pair)
        key_rows = slice(low_key, low_key + keys)
        dk, dv = (None, None) if state is None else state
        for h in range(2):
            head_rows = slice(h * HD, (h + 1) * HD)
            s = nt(k_heads[h][key_rows], q_pair)
            x = s * s + 1.0
            r = lax.rsqrt(x)
            e = jnp.exp(x * r - lse_ref[h : h + 1, cols])
            if mask is not None:
                e = jnp.where(mask, e, 0.0)
            t = jnp.tanh(s)
            slope = s * r
            w = (t * e).astype(bf)
            gw = nt(v_heads[h][key_rows], do_pair)
            ds = (
                e * (gw * (1.0 + t * (slope - t)) - slope * inner_ref[h : h + 1, cols])
            ).astype(bf)
            dv_part = nn(w, do_heads[h])
            dk_part = nn(ds, q_heads[h])
            dv = dv_part if dv is None else dv + dv_part
            dk = dk_part if dk is None else dk + dk_part
            dqt_ref[head_rows, cols] += nn(k_turned[head_rows, key_rows], ds)
        return (dk, dv)

    base = j * block
    strip_grads = [
        update(None, m * part, part, base + m * part, block - m * part, up_to(part, block - m * part))
        for m in range(strips)
    ]
    state = tuple(jnp.concatenate(items, axis=0) for items in zip(*strip_grads))
    dk, dv = lax.fori_loop(
        j + 1, stop, lambda i, st: update(st, 0, block, i * block, block, None), state
    )
    mine = pl.ds(pl.multiple_of(base, block), block)
    g_ref[mine, PAIR : 2 * PAIR] = dk.astype(bf)
    g_ref[mine, 2 * PAIR :] = dv.astype(bf)

    @pl.when(j == last)
    def _():
        g_ref[:, :PAIR] = (dqt_ref[...] * HD**-0.5).T.astype(bf)
        theirs = pl.multiple_of((1 - place_ref[0]) * side_rows, side_rows)
        send_ref[...] = g_ref[pl.ds(theirs, side_rows), :]


def attend_bwd(flag, place, projected, pair, heads_out, keep, other, lse, block=1024, strips=4):
    rows = projected.shape[0]
    fixed = lambda r: pl.BlockSpec((r, PAIR), lambda j, f, s: (0, 0))
    part = lambda c: pl.BlockSpec((block, PAIR), lambda j, f, s: (j, 3 * pair + c))
    return pl.pallas_call(
        functools.partial(attend_bwd_kernel, block, strips),
        grid_spec=pltpu.PrefetchScalarGridSpec(
            num_scalar_prefetch=2,
            grid=(rows // block,),
            in_specs=[
                pl.BlockSpec((rows, PAIR), lambda j, f, s: (0, 3 * pair)),
                part(1),
                part(2),
                fixed(rows),
                pl.BlockSpec((rows // 2, PAIR), lambda j, f, s: (0, pair)),
                pl.BlockSpec((rows // 2, PAIR), lambda j, f, s: (0, pair)),
                pl.BlockSpec((8, rows), lambda j, f, s: (0, 0)),
            ],
            out_specs=[
                pl.BlockSpec((rows, 3 * PAIR), lambda j, f, s: (0, 0)),
                pl.BlockSpec((rows // 2, 3 * PAIR), lambda j, f, s: (0, 0)),
            ],
            scratch_shapes=[
                pltpu.VMEM((PAIR, rows), f32),
                pltpu.VMEM((8, rows), f32),
                pltpu.VMEM((rows, PAIR), bf),
            ],
        ),
        out_shape=[
            jax.ShapeDtypeStruct((rows, 3 * PAIR), bf),
            jax.ShapeDtypeStruct((rows // 2, 3 * PAIR), bf),
        ],
        cost_estimate=busy(25),
        name="attend_bwd",
    )(flag, place, projected, projected, projected, heads_out, keep, other, lse)


def tn(a, b):
    return lax.dot_general(a, b, (((0,), (0,)), ((), ())), preferred_element_type=f32)


def norm_stats(rows_in):
    mean = jnp.mean(rows_in, axis=-1, keepdims=True)
    centred = rows_in - mean
    variance = jnp.mean(centred * centred, axis=-1, keepdims=True)
    scale = lax.rsqrt(variance + EPS)
    return centred * scale, scale


def project_kernel(place_ref, own_ref, other_ref, gain_ref, bias_ref, w_ref, b_ref, n_ref, p_ref):
    per_side = pl.num_programs(0) // 2
    is_own = pl.program_id(0) // per_side == place_ref[0]
    rows = jnp.where(is_own, own_ref[...], other_ref[...]).astype(f32)
    piece = rows.shape[0] // 4
    for r in range(0, rows.shape[0], piece):
        here = slice(r, r + piece)
        unit, _ = norm_stats(rows[here])
        normed = (unit * gain_ref[...] + bias_ref[...]).astype(bf)
        n_ref[here, :] = normed
        for c in range(0, p_ref.shape[1], 3 * PAIR):
            cols = slice(c, c + 3 * PAIR)
            part = (nn(normed, w_ref[:, cols]) + b_ref[:, cols]).astype(bf)
            p_ref[here, c : c + PAIR] = part[:, :PAIR] * jnp.asarray(HD**-0.5, bf)
            p_ref[here, c + PAIR : c + 3 * PAIR] = part[:, PAIR:]


def project(place, own, other, gain, bias, weight, w_bias, block=512):
    rows, width = own.shape
    per_side = rows // block
    cols = weight.shape[1]
    fixed = lambda shape: pl.BlockSpec(shape, lambda i, s: (0, 0))
    return pl.pallas_call(
        project_kernel,
        grid_spec=pltpu.PrefetchScalarGridSpec(
            num_scalar_prefetch=1,
            grid=(2 * per_side,),
            in_specs=[
                pl.BlockSpec(
                    (block, width), lambda i, s: (jnp.clip(i - s[0] * per_side, 0, per_side - 1), 0)
                ),
                pl.BlockSpec(
                    (block, width),
                    lambda i, s: (jnp.clip(i - (1 - s[0]) * per_side, 0, per_side - 1), 0),
                ),
                fixed((1, width)),
                fixed((1, width)),
                fixed(weight.shape),
                fixed((1, cols)),
            ],
            out_specs=[
                pl.BlockSpec((block, width), lambda i, s: (i, 0)),
                pl.BlockSpec((block, cols), lambda i, s: (i, 0)),
            ],
        ),
        out_shape=[
            jax.ShapeDtypeStruct((2 * rows, width), bf),
            jax.ShapeDtypeStruct((2 * rows, cols), bf),
        ],
        cost_estimate=busy(11),
        name="norm_project",
    )(place, own, other, gain, bias, weight, w_bias)


GELU_C = math.sqrt(2 / math.pi)


def mlp_kernel(
    place_ref,
    g_hbm,
    x_ref,
    og_ref,
    ha0_ref,
    ha1_ref,
    ha2_ref,
    hb0_ref,
    hb1_ref,
    hb2_ref,
    bout_ref,
    gain_ref,
    bias_ref,
    bfc_ref,
    bproj_ref,
    out_ref,
    mixed_ref,
    n2_ref,
    act_ref,
    gp_ref,
    gm_ref,
    gml_ref,
    keep_ref,
    send_ref,
    sums_ref,
    w_ref,
    sem,
):
    i = pl.program_id(0)
    devices = g_hbm.shape[0]
    sub = g_hbm.shape[2]
    width = devices * sub
    chunks = (g_hbm.shape[1] - 1) // 2

    def load(slot):
        return pltpu.make_async_copy(g_hbm.at[:, slot], w_ref.at[slot], sem.at[slot])

    order = [2 * chunks] + list(range(chunks, 2 * chunks))

    def load_proj():
        return pltpu.make_async_copy(
            g_hbm.at[:, pl.ds(0, chunks)], wp_view(), sem.at[0]
        )

    def wp_view():
        return w_ref.at[pl.ds(0, chunks)].reshape(devices, chunks, sub, width)

    @pl.when(i == 0)
    def _():
        load(order[0]).start()
        load(order[1]).start()
        load_proj().start()
        for slot in order[2:]:
            load(slot).start()
        sums_ref[...] = jnp.zeros_like(sums_ref)

    def arrive(copy):
        @pl.when(i == 0)
        def _():
            copy.wait()

    def weight(slot):
        return w_ref[slot].reshape(width, width)

    on_left = place_ref[0] == 0
    ha = jnp.concatenate([ha0_ref[...], ha1_ref[...], ha2_ref[...]], axis=1)
    hb = jnp.concatenate([hb0_ref[...], hb1_ref[...], hb2_ref[...]], axis=1)
    mixed = jnp.concatenate([jnp.where(on_left, ha, hb), jnp.where(on_left, hb, ha)], axis=1)
    mixed_ref[...] = mixed
    arrive(load(order[0]))
    og_low = og_ref[...]
    og = og_low.astype(f32)
    middle = x_ref[...].astype(f32) + nn(mixed, weight(2 * chunks)) + bout_ref[...]
    unit, scale = norm_stats(middle)
    n2 = (unit * gain_ref[...] + bias_ref[...]).astype(bf)
    n2_ref[...] = n2
    out = middle + bproj_ref[...]
    e = jnp.zeros_like(middle)
    for c in range(chunks):
        cols = slice(c * width, (c + 1) * width)
        arrive(load(order[1 + c]))
        w_fc = weight(chunks + c)
        pre = nn(n2, w_fc) + bfc_ref[:, cols]
        if c == 0:
            arrive(load_proj())
        square = pre * pre
        t = jnp.tanh(GELU_C * pre * (1.0 + 0.044715 * square))
        low_half = 0.5 * (1.0 + t)
        act = (pre * low_half).astype(bf)
        act_ref[:, cols] = act
        w_proj = weight(c)
        out = out + nn(act, w_proj)
        slope = low_half + 0.5 * pre * (1.0 - t * t) * (
            GELU_C * (1.0 + 3.0 * 0.044715 * square)
        )
        gp = (nt(og_low, w_proj) * slope).astype(bf)
        gp_ref[:, cols] = gp
        sums_ref[0:1, cols] += jnp.sum(gp.astype(f32), axis=0, keepdims=True)
        e = e + nt(gp, w_fc)
    out_ref[...] = out.astype(bf)
    sums_ref[1:2, 0:width] += jnp.sum(og, axis=0, keepdims=True)
    sums_ref[1:2, width : 2 * width] += jnp.sum(e * unit, axis=0, keepdims=True)
    sums_ref[1:2, 2 * width : 3 * width] += jnp.sum(e, axis=0, keepdims=True)
    eg = e * gain_ref[...]
    gm = og + scale * (
        eg
        - jnp.mean(eg, axis=-1, keepdims=True)
        - unit * jnp.mean(eg * unit, axis=-1, keepdims=True)
    )
    gm_ref[...] = gm
    gml = gm.astype(bf)
    gml_ref[...] = gml
    sums_ref[1:2, 3 * width : 4 * width] += jnp.sum(gml.astype(f32), axis=0, keepdims=True)
    gh = nt(gml, weight(2 * chunks)).astype(bf)
    half = width // 2
    left = gh[:, :half]
    right = gh[:, half:]
    keep_ref[...] = jnp.where(on_left, left, right)
    send_ref[...] = jnp.where(on_left, right, left)


def mlp(place, gathered, x, og, heads_mine, heads_other, b_out, gain, bias, b_fc, b_proj, block=512):
    rows, width = x.shape
    steps = rows // block
    hidden = b_fc.shape[1]
    row = lambda cols: pl.BlockSpec((block, cols), lambda i, s: (i, 0))
    fixed = lambda cols: pl.BlockSpec((1, cols), lambda i, s: (0, 0))
    shape = lambda cols, kind: jax.ShapeDtypeStruct((rows, cols), kind)
    return pl.pallas_call(
        mlp_kernel,
        grid_spec=pltpu.PrefetchScalarGridSpec(
            num_scalar_prefetch=1,
            grid=(steps,),
            in_specs=[
                pl.BlockSpec(memory_space=pl.ANY),
                row(width),
                row(width),
                *[pl.BlockSpec((block, PAIR), lambda i, s: (s[0] * steps + i, 0))] * 3,
                *[row(PAIR)] * 3,
                fixed(width),
                fixed(width),
                fixed(width),
                fixed(hidden),
                fixed(width),
            ],
            out_specs=[
                row(width),
                row(width),
                row(width),
                row(hidden),
                row(hidden),
                row(width),
                row(width),
                *[row(width // 2)] * 2,
                pl.BlockSpec((8, hidden), lambda i, s: (0, 0)),
            ],
            scratch_shapes=[
                pltpu.VMEM((gathered.shape[1], gathered.shape[0], gathered.shape[2], width), bf),
                pltpu.SemaphoreType.DMA((gathered.shape[1],)),
            ],
        ),
        out_shape=[
            shape(width, bf),
            shape(width, bf),
            shape(width, bf),
            shape(hidden, bf),
            shape(hidden, bf),
            shape(width, f32),
            shape(width, bf),
            *[shape(width // 2, bf)] * 2,
            jax.ShapeDtypeStruct((8, hidden), f32),
        ],
        compiler_params=pltpu.CompilerParams(vmem_limit_bytes=56 * 1024 * 1024),
        cost_estimate=busy(37),
        name="mlp",
    )(place, gathered, x, og, *heads_mine, *heads_other, b_out, gain, bias, b_fc, b_proj)


def weight_grad_kernel(act_ref, gp_ref, og_ref, n2_ref, mixed_ref, gml_ref, out_hbm, buf_ref, sem):
    c = pl.program_id(0)
    last = pl.num_programs(0) - 1
    devices, slots, sub, width = out_hbm.shape
    chunks = (slots - 1) // 2
    group = devices // chunks
    slot = lax.rem(c, 2)

    def proj_copy(step, where):
        return pltpu.make_async_copy(
            buf_ref.at[where].reshape(group, chunks, sub, width),
            out_hbm.at[pl.ds(step * group, group), pl.ds(0, chunks)],
            sem.at[where],
        )

    def other_copy(step, where):
        return pltpu.make_async_copy(buf_ref.at[where], out_hbm.at[:, step], sem.at[where])

    @pl.when(c >= 2)
    def _():
        other_copy(chunks, slot).wait()

    def put(value):
        buf_ref[slot] = value.astype(bf).reshape(devices, sub, width)

    @pl.when(c < chunks)
    def _():
        put(tn(act_ref[...], og_ref[...]))
        proj_copy(c, slot).start()

    @pl.when((c >= chunks) & (c < 2 * chunks))
    def _():
        put(tn(n2_ref[...], gp_ref[...]))
        other_copy(c, slot).start()

    @pl.when(c == last)
    def _():
        put(tn(mixed_ref[...], gml_ref[...]))
        other_copy(c, slot).start()
        other_copy(chunks, 1 - slot).wait()
        other_copy(chunks, slot).wait()


def weight_grads(act, gp, og, n2, mixed, gml, devices):
    rows, width = og.shape
    chunks = act.shape[1] // width
    slots = 2 * chunks + 1
    sub = width // devices
    fixed = pl.BlockSpec((rows, width), lambda c: (0, 0))
    return pl.pallas_call(
        weight_grad_kernel,
        grid=(slots,),
        in_specs=[
            pl.BlockSpec((rows, width), lambda c: (0, jnp.minimum(c, chunks - 1))),
            pl.BlockSpec((rows, width), lambda c: (0, jnp.clip(c - chunks, 0, chunks - 1))),
            fixed,
            fixed,
            fixed,
            fixed,
        ],
        out_specs=pl.BlockSpec(memory_space=pl.ANY),
        out_shape=jax.ShapeDtypeStruct((devices, slots, sub, width), bf),
        scratch_shapes=[
            pltpu.VMEM((2, devices, sub, width), bf),
            pltpu.SemaphoreType.DMA((2,)),
        ],
        cost_estimate=busy(19),
        name="weight_grads",
    )(act, gp, og, n2, mixed, gml)


def norm_sums_kernel(
    place_ref,
    own_ref,
    other_ref,
    g0_ref,
    g1_ref,
    g2_ref,
    r0_ref,
    r1_ref,
    w_ref,
    wo_ref,
    e_ref,
    sums_ref,
    bias_ref,
):
    i = pl.program_id(0)
    per_side = pl.num_programs(0) // 2
    is_own = i // per_side == place_ref[0]

    @pl.when(i == 0)
    def _():
        sums_ref[...] = jnp.zeros_like(sums_ref)
        bias_ref[...] = jnp.zeros_like(bias_ref)

    unit, _ = norm_stats(jnp.where(is_own, own_ref[...], other_ref[...]).astype(f32))
    wide = 3 * PAIR
    e = None
    for p, g_ref in enumerate((g0_ref, g1_ref, g2_ref)):
        cols = slice(p * wide, (p + 1) * wide)
        g = g_ref[...]
        part = nt(g, w_ref[:, cols])
        e = part if e is None else e + part
        bias_ref[0:1, cols] += jnp.sum(g.astype(f32), axis=0, keepdims=True)
    sums_ref[0:1, :] += jnp.sum(e * unit, axis=0, keepdims=True)
    sums_ref[1:2, :] += jnp.sum(e, axis=0, keepdims=True)

    @pl.when(is_own)
    def _():
        total = e
        for p, r_ref in enumerate((r0_ref, r1_ref)):
            total = total + nt(r_ref[...], wo_ref[:, p * wide : (p + 1) * wide])
        e_ref[...] = total


def norm_sums(place, own, other, grads, received, weight, weight_other, block=256):
    rows, width = own.shape
    per_side = rows // block
    cols = weight.shape[1]
    mine = lambda i, s: (jnp.clip(i - s[0] * per_side, 0, per_side - 1), 0)
    theirs = lambda i, s: (jnp.clip(i - (1 - s[0]) * per_side, 0, per_side - 1), 0)
    fixed = lambda shape: pl.BlockSpec(shape, lambda i, s: (0, 0))
    return pl.pallas_call(
        norm_sums_kernel,
        grid_spec=pltpu.PrefetchScalarGridSpec(
            num_scalar_prefetch=1,
            grid=(2 * per_side,),
            in_specs=[
                pl.BlockSpec((block, width), mine),
                pl.BlockSpec((block, width), theirs),
                *[pl.BlockSpec((block, 3 * PAIR), lambda i, s: (i, 0))] * 3,
                *[pl.BlockSpec((block, 3 * PAIR), mine)] * 2,
                fixed(weight.shape),
                fixed(weight.shape),
            ],
            out_specs=[pl.BlockSpec((block, width), mine), fixed((8, width)), fixed((8, cols))],
        ),
        out_shape=[
            jax.ShapeDtypeStruct((rows, width), f32),
            jax.ShapeDtypeStruct((8, width), f32),
            jax.ShapeDtypeStruct((8, cols), f32),
        ],
        cost_estimate=busy(13),
        name="norm_sums",
    )(place, own, other, *grads, *received, weight, weight_other)


def finish_kernel(x_ref, gm_ref, e_ref, r_ref, wo_ref, gain_ref, out_ref):
    unit, scale = norm_stats(x_ref[...].astype(f32))
    eg = (e_ref[...] + nt(r_ref[...], wo_ref[...])) * gain_ref[...]
    out_ref[...] = gm_ref[...] + scale * (
        eg
        - jnp.mean(eg, axis=-1, keepdims=True)
        - unit * jnp.mean(eg * unit, axis=-1, keepdims=True)
    )


def finish(x, grad_middle, e, received, weight_other, gain, block=256):
    rows, width = x.shape
    row = lambda cols: pl.BlockSpec((block, cols), lambda i: (i, 0))
    last = weight_other.shape[1] // (3 * PAIR) - 1
    return pl.pallas_call(
        finish_kernel,
        grid=(rows // block,),
        in_specs=[
            row(width),
            row(width),
            row(width),
            row(3 * PAIR),
            pl.BlockSpec((width, 3 * PAIR), lambda i: (0, last)),
            pl.BlockSpec((1, width), lambda i: (0, 0)),
        ],
        out_specs=row(width),
        out_shape=jax.ShapeDtypeStruct((rows, width), f32),
        cost_estimate=busy(6),
        name="finish",
    )(x, grad_middle, e, received, weight_other, gain)


def swap(value, bit, total):
    return lax.ppermute(value, AXES, [(i, i ^ bit) for i in range(total)])


def gather_dp(shard, dp_size, order, arrivals):
    me = lax.axis_index("dp")
    bits = dp_size.bit_length() - 1
    held = shard.reshape((1,) * bits + shard.shape)
    for bit in order:
        other = swap(held, 2 << bit, 2 * dp_size)
        arrivals.append(other)
        low = (me >> bit) & 1 == 0
        held = jnp.concatenate(
            [jnp.where(low, held, other), jnp.where(low, other, held)], axis=bits - 1 - bit
        )
    return held.reshape((dp_size * shard.shape[0],) + shard.shape[1:])


def scatter_dp(whole, dp_size, order):
    me = lax.axis_index("dp")
    bits = dp_size.bit_length() - 1
    rows = whole.shape[0] // dp_size
    held = whole.reshape((2,) * bits + (rows,) + whole.shape[1:])
    for bit in order:
        axis = bits - 1 - bit
        low = (me >> bit) & 1 == 0
        first = lax.slice_in_dim(held, 0, 1, axis=axis)
        second = lax.slice_in_dim(held, 1, 2, axis=axis)
        mine = jnp.where(low, first, second)
        sent = jnp.where(low, second, first).astype(bf)
        held = mine.astype(f32) + swap(sent, 2 << bit, 2 * dp_size).astype(
            f32
        )
    return held.reshape((rows,) + whole.shape[1:])


def sum_all(vector, order, total):
    for bit in [2 << bit for bit in order] + [1]:
        vector = vector + swap(vector, bit, total)
    return vector


def on_device_pair(
    dp_size,
    block_input,
    seq_long,
    ln1_gain,
    ln1_bias,
    w_qkv,
    b_qkv,
    w_out,
    b_out,
    ln2_gain,
    ln2_bias,
    w_fc,
    b_fc,
    w_proj,
    b_proj,
    out_grad,
):
    total = 2 * dp_size
    side = lax.axis_index("fsdp")
    flat = lax.axis_index("dp") * 2 + side
    on_left = side == 0
    half = D // 2
    dp_bits = list(range(dp_size.bit_length() - 1))
    gather_order = dp_bits[1:2] + dp_bits[:1:-1] + dp_bits[:1]
    scatter_order = dp_bits[:1] + dp_bits[2:] + dp_bits[1:2]

    def ordered(mine, other, axis):
        return jnp.concatenate(
            [jnp.where(on_left, mine, other), jnp.where(on_left, other, mine)], axis=axis
        )

    pairs = half // PAIR

    def head_columns(rows_in, which):
        split = rows_in.reshape(rows_in.shape[0], 3, 2, pairs, PAIR)
        mine = lax.dynamic_index_in_dim(split, which, 2, keepdims=False)
        return jnp.transpose(mine, (0, 2, 1, 3)).reshape(rows_in.shape[0], 3 * half)

    small = (ln1_gain, ln1_bias, b_qkv, b_out, ln2_gain, ln2_bias, b_fc, b_proj)
    placed = jnp.concatenate(
        [
            lax.dynamic_update_slice(
                jnp.zeros((item.shape[0] * total,), bf), item, (item.shape[0] * flat,)
            )
            for item in small
        ]
    )
    gathered = sum_all(placed, gather_order, total).astype(f32)
    pieces = []
    start = 0
    for item in small:
        pieces.append(gathered[start : start + item.shape[0] * total])
        start += item.shape[0] * total
    ln1_gain, ln1_bias, b_qkv, b_out, ln2_gain, ln2_bias, b_fc, b_proj = pieces

    other_input = swap(block_input, 1, total)
    received = swap(head_columns(w_qkv, 1 - side), 1, total)
    arrivals = [received]
    w_mine = gather_dp(
        ordered(head_columns(w_qkv, side), received, 0), dp_size, gather_order, arrivals
    )
    w_other = swap(w_mine, 1, total)

    sub = w_out.shape[0]
    chunks = FF // D
    packed = jnp.concatenate(
        [w_proj] + [w_fc[:, c * D : (c + 1) * D] for c in range(chunks)] + [w_out], axis=0
    )
    packed, _ = lax.optimization_barrier((packed, arrivals[1]))
    gathered_w = lax.all_gather(packed, AXES, axis=0, tiled=True)
    gathered_w = gathered_w.reshape(total, 2 * chunks + 1, sub, D)

    def as_row(vector):
        return vector.reshape(1, -1)

    place = side.astype(jnp.int32).reshape(1)
    b_mine = head_columns(as_row(b_qkv), side)
    normed_one, projected = project(
        place, block_input, other_input, as_row(ln1_gain), as_row(ln1_bias), w_mine, b_mine
    )
    heads_mine = []
    heads_other = []
    log_totals = []
    for p in range(pairs):
        heads, heads_sent, log_total = attend_fwd(seq_long, place, projected, p)
        heads_mine.append(heads)
        log_totals.append(log_total)
        heads_other.append(swap(heads_sent, 1, total))
    (
        block_output,
        mixed,
        normed_two,
        hidden_act,
        grad_pre,
        grad_middle,
        grad_mid_low,
        *rest,
    ) = mlp(
        place,
        gathered_w,
        block_input,
        out_grad,
        heads_mine,
        heads_other,
        as_row(b_out),
        as_row(ln2_gain),
        as_row(ln2_bias),
        as_row(b_fc),
        as_row(b_proj),
    )
    grad_keep, grad_sent, sums = rest
    grad_other = swap(grad_sent, 1, total)
    packed_grads = weight_grads(
        hidden_act, grad_pre, out_grad, normed_two, mixed, grad_mid_low, total
    )
    shard = lax.psum_scatter(
        packed_grads.reshape(total * (2 * chunks + 1) * sub, D),
        AXES,
        scatter_dimension=0,
        tiled=True,
    ).astype(f32)
    shard_w_proj = shard[: chunks * sub]
    shard_w_fc = jnp.concatenate(
        [shard[(chunks + c) * sub : (chunks + c + 1) * sub] for c in range(chunks)], axis=1
    )
    shard_w_out = shard[2 * chunks * sub :]
    grad_b_fc = sums[0]
    grad_b_proj, grad_ln2_gain, grad_ln2_bias, grad_b_out = (
        sums[1, k * D : (k + 1) * D] for k in range(4)
    )
    grads = []
    grads_other = []
    columns = []
    for p in range(pairs):
        grad_pair, pair_sent = attend_bwd(
            seq_long,
            place,
            projected,
            p,
            heads_mine[p],
            grad_keep,
            grad_other,
            log_totals[p],
        )
        grads.append(grad_pair)
        grads_other.append(swap(pair_sent, 1, total))
        columns.append(product_tn(normed_one, grad_pair).astype(bf))
    shards = [
        scatter_dp(jnp.concatenate(columns[:-1], axis=1), dp_size, scatter_order),
        scatter_dp(columns[-1], dp_size, scatter_order),
    ]

    e_partial, norm_one_sums, grad_b_mine = norm_sums(
        place, block_input, other_input, grads, grads_other[:-1], w_mine, w_other
    )
    input_grad = finish(
        block_input, grad_middle, e_partial, grads_other[-1], w_other, as_row(ln1_gain)
    )

    shard_rows = jnp.concatenate(shards, axis=1).reshape(2, -1, 3 * half)
    keep = lax.dynamic_index_in_dim(shard_rows, side, 0, keepdims=False)
    send = lax.dynamic_index_in_dim(shard_rows, 1 - side, 0, keepdims=False)
    taken = swap(send, 1, total)

    def by_part(rows_in):
        split = rows_in.reshape(rows_in.shape[0], pairs, 3, PAIR)
        return jnp.transpose(split, (0, 2, 1, 3)).reshape(rows_in.shape[0], 3, 1, half)

    shard_w_qkv = ordered(by_part(keep), by_part(taken), 2).reshape(-1, 3 * D)
    grad_b_part = by_part(grad_b_mine[0:1])
    grad_b_qkv = ordered(grad_b_part, jnp.zeros_like(grad_b_part), 2).reshape(3 * D)
    grad_vectors = (
        grad_b_out,
        grad_ln2_gain,
        grad_ln2_bias,
        grad_b_fc,
        grad_b_proj,
        norm_one_sums[0],
        norm_one_sums[1],
        grad_b_qkv,
    )
    summed = sum_all(jnp.concatenate(grad_vectors), scatter_order, total)
    begin = 0
    vector_shards = []
    for item in grad_vectors:
        size = item.shape[0] // total
        vector_shards.append(lax.dynamic_slice(summed, (begin + size * flat,), (size,)))
        begin += item.shape[0]
    (
        shard_b_out,
        shard_ln2_gain,
        shard_ln2_bias,
        shard_b_fc,
        shard_b_proj,
        shard_ln1_gain,
        shard_ln1_bias,
        shard_b_qkv,
    ) = vector_shards
    return (
        block_output,
        input_grad,
        shard_ln1_gain,
        shard_ln1_bias,
        shard_w_qkv,
        shard_b_qkv,
        shard_w_out,
        shard_b_out,
        shard_ln2_gain,
        shard_ln2_bias,
        shard_w_fc,
        shard_b_fc,
        shard_w_proj,
        shard_b_proj,
    )


def solution(mesh):
    rows, vector, flags = (P(AXES, None), P(AXES), P("dp"))
    weights = (vector, vector, rows, vector, rows, vector, vector, vector, rows, vector, rows, vector)
    whole_slice = dict(
        mesh=mesh,
        in_specs=(rows, flags) + weights + (rows,),
        out_specs=(rows, rows) + weights,
        check_vma=False,
    )
    dp_size = mesh.shape["dp"]
    if mesh.shape["fsdp"] != 2 or dp_size < 8 or dp_size & (dp_size - 1):
        return jax.shard_map(on_device_generic, **whole_slice)

    def on_device(*args):
        return on_device_pair(dp_size, *args)

    return jax.shard_map(on_device, **whole_slice)
```
